32 devices in a mesh: batch: 8 (over z, core), seq: 4 (over y, x).
Axes of the slice: x: 2, y: 2, z: 4, core: 2. Of those that a mesh axis runs over, the one named last changes fastest.
Arguments:
- tokens: bfloat16 [16, 1024, 1024], P('batch', 'seq'), may hold values from -6 to 6
- memory: bfloat16 [16, 256, 1024], P('batch', 'seq'), may hold values from -6 to 6
- output_grad: bfloat16 [16, 1024, 1024], P('batch', 'seq'), may hold values from -6 to 6
- segments: int32 [16, 1024], P('batch', 'seq'), may hold values from 0 to 3, never falling along the last dimension, each value on 1 to 512 neighbouring positions
- memory_segments: int32 [16, 256], P('batch', 'seq'), may hold values from 0 to 3, never falling along the last dimension, each value on 1 to 128 neighbouring positions
- buckets: int32 [1024], replicated, may hold values from 0 to 31
- w_query: float32 [2, 1024, 1024], P(None, ('batch', 'seq')), may hold values from -0.03125 to 0.03125
- keyvalue_weight: float32 [2, 2, 1024, 512], P(None, None, ('batch', 'seq')), may hold values from -0.1875 to 0.1875
- w_output: float32 [2, 1024, 1024], P(None, ('batch', 'seq')), may hold values from -0.75 to 0.75
- w_expand: float32 [2, 1024, 2816], P(None, ('batch', 'seq')), may hold values from -0.1875 to 0.1875
- w_reduce: float32 [2816, 1024], P(('batch', 'seq')), may hold values from -0.109375 to 0.109375
- gains: float32 [3, 1024], P(None, ('batch', 'seq')), may hold values from 0.5 to 1.5
- position_bias: float32 [512], P(('batch', 'seq')), may hold values from -3 to 3
- momentum_query: float32 [2, 1024, 1024], P(None, ('batch', 'seq')), may hold values from -1536 to 1536
- keyvalue_momentum: float32 [2, 2, 1024, 512], P(None, None, ('batch', 'seq')), may hold values from -384 to 384
- momentum_output: float32 [2, 1024, 1024], P(None, ('batch', 'seq')), may hold values from -160 to 160
- momentum_expand: float32 [2, 1024, 2816], P(None, ('batch', 'seq')), may hold values from -320 to 320
- momentum_reduce: float32 [2816, 1024], P(('batch', 'seq')), may hold values from -448 to 448
- momentum_gains: float32 [3, 1024], P(None, ('batch', 'seq')), may hold values from -448 to 448
- momentum_position: float32 [512], P(('batch', 'seq')), may hold values from -224 to 224
- average_query: float32 [2, 1024, 1024], P(None, ('batch', 'seq')), may hold values from -0.03125 to 0.03125
- keyvalue_average: float32 [2, 2, 1024, 512], P(None, None, ('batch', 'seq')), may hold values from -0.1875 to 0.1875
- average_output: float32 [2, 1024, 1024], P(None, ('batch', 'seq')), may hold values from -0.75 to 0.75
- average_expand: float32 [2, 1024, 2816], P(None, ('batch', 'seq')), may hold values from -0.1875 to 0.1875
- average_reduce: float32 [2816, 1024], P(('batch', 'seq')), may hold values from -0.109375 to 0.109375
- average_gains: float32 [3, 1024], P(None, ('batch', 'seq')), may hold values from 0.5 to 1.5
- average_position: float32 [512], P(('batch', 'seq')), may hold values from -3 to 3
Outputs:
- output: bfloat16 [16, 1024, 1024], P('batch', 'seq')
- input_grad: float32 [16, 1024, 1024], P('batch', 'seq')
- memory_grad: float32 [16, 256, 1024], P('batch', 'seq')
- grad_query: float32 [2, 1024, 1024], P(None, ('batch', 'seq'))
- grad_keyval: float32 [2, 2, 1024, 512], P(None, None, ('batch', 'seq'))
- grad_output: float32 [2, 1024, 1024], P(None, ('batch', 'seq'))
- grad_expand: float32 [2, 1024, 2816], P(None, ('batch', 'seq'))
- grad_reduce: float32 [2816, 1024], P(('batch', 'seq'))
- grad_gains: float32 [3, 1024], P(None, ('batch', 'seq'))
- grad_position: float32 [512], P(('batch', 'seq'))
- renewed_query: float32 [2, 1024, 1024], P(None, ('batch', 'seq'))
- renewed_keyval: float32 [2, 2, 1024, 512], P(None, None, ('batch', 'seq'))
- renewed_output: float32 [2, 1024, 1024], P(None, ('batch', 'seq'))
- renewed_expand: float32 [2, 1024, 2816], P(None, ('batch', 'seq'))
- renewed_reduce: float32 [2816, 1024], P(('batch', 'seq'))
- renewed_gains: float32 [3, 1024], P(None, ('batch', 'seq'))
- renewed_position: float32 [512], P(('batch', 'seq'))
- state_query: float32 [2, 2, 1024, 1024], P(None, None, ('batch', 'seq'))
- state_keyval: float32 [2, 2, 2, 1024, 512], P(None, None, None, ('batch', 'seq'))
- state_output: float32 [2, 2, 1024, 1024], P(None, None, ('batch', 'seq'))
- state_expand: float32 [2, 2, 1024, 2816], P(None, None, ('batch', 'seq'))
- state_reduce: float32 [2, 2816, 1024], P(None, ('batch', 'seq'))
- state_gains: float32 [2, 3, 1024], P(None, None, ('batch', 'seq'))
- state_position: float32 [2, 512], P(None, ('batch', 'seq'))
The draws below stay inside these ranges and needn't reach their ends.
Inputs may be any that keep to these rules, and one draw needn't show every extreme that they name: `segments`: along each row the ids never fall, and each of the 4 ids occurs in every row. `memory_segments`: along each memory row the ids never fall, and each of the 4 ids occurs in every memory row.
All inputs are finite; a program needn't handle non-finite values.
Results may differ from the reference program's by a relative error of at most 0.02.
The reference program's roundings to bfloat16 on the way count: a program that leaves them out, or rounds other values in their place, can miss the bound.
Values may be sent and summed in bfloat16 or wider, within the bound.
No kernel may reach another device: no remote copies, remote signals or barrier semaphores. Data moves between devices by JAX's collectives and lax.ppermute only.
A program may use at most 256 MiB of HBM per device.

```python
import math
import jax
import jax.numpy as jnp
import numpy as np
from jax import lax

MODEL_WIDTH = 1024
FF = 2816
QUERY_HEADS = 16
HEAD_SIZE = 64
NB = 32
KEY_GROUPS = 8
NDOC = 4
BROWS = 16
PACKED_LENGTH = 1024
MEM = 256
DECODER_TOKENS = 16384


def plant(values, rng, least, high):
    longest = values.shape.index(max(values.shape))
    spots = []
    for shift in (0, 1):
        where = [jax.random.randint(jax.random.fold_in(rng, axis), (), 0, length) for axis, length in enumerate(values.shape)]
        where[longest] = (where[longest] + shift) % values.shape[longest]
        spots.append(tuple(where))
    return values.at[spots[0]].set(least).at[spots[1]].set(high)


def with_spikes(result, stream_key, source, target, shards_of, factor):
    owner, partner = [(jnp.arange(result.shape[axis_at]) // (result.shape[axis_at] // shards_of)).reshape([-1 if axis == axis_at else 1 for axis in range(result.ndim)]) for axis_at in (source, target)]
    chosen = jax.random.permutation(stream_key, shards_of)[partner]
    strong = (owner == chosen) | (owner == (partner + shards_of // 2) % shards_of)
    return jnp.where(strong, factor * result, result)


def block_levels(own_key, dims, pieces, smallest, high):
    level = 1.0
    for dim, shards_of in pieces:
        heights = jax.random.uniform(jax.random.fold_in(jax.random.fold_in(own_key, 6), dim), (shards_of,), jnp.float32, smallest / len(pieces), high / len(pieces))
        level = level * jnp.repeat(jnp.exp(heights), dims[dim] // shards_of).reshape((-1,) + (1,) * (len(dims) - 1 - dim))
    return level


def split_up(count, total, most, slope):
    weights = [(1 << 20) // math.isqrt(rank ** slope) + 1 for rank in range(2, count + 1)]
    surplus, holding = total - most - (count - 1), [1] * (count - 1)
    while surplus > 0:
        movable = [i for i in range(count - 1) if holding[i] < most]
        mass, left = sum([weights[i] for i in movable]), surplus
        for i in movable:
            addition = min(most - holding[i], max(1, left * weights[i] // mass), surplus)
            holding[i] = holding[i] + addition
            surplus = surplus - addition
    return np.array([most] + holding)


def ragged(stream_key, count, total, limit, slope):
    if count == 2:
        one = jax.random.randint(stream_key, (), max(1, total - limit), min(limit, total - 1) + 1)
        return jnp.stack([one, total - one])
    sizes = jnp.asarray(split_up(count, total, limit, slope), jnp.int32)
    couples = (count - 1) // 2
    donor, receiver = sizes[1:1 + 2 * couples:2], sizes[2:2 + 2 * couples:2]
    room = jnp.minimum(donor - 1, limit - receiver)
    moved = jax.random.randint(jax.random.fold_in(stream_key, 1), (couples,), 0, 1 << 20) % (room + 1)
    sizes = sizes.at[1:1 + 2 * couples:2].set(donor - moved).at[2:2 + 2 * couples:2].set(receiver + moved)
    return sizes[jax.random.permutation(jax.random.fold_in(stream_key, 2), count)]


def normal_values(own_key, dims, deviation, reach, shards=(), held_as=jnp.bfloat16):
    entries = jax.random.normal(own_key, dims, jnp.float32) * deviation
    if len(shards) > 0:
        entries = block_levels(own_key, dims, shards, -0.22, 0.18) * entries
    return jnp.clip(entries, min=-reach, max=reach).astype(held_as)


def noise_with(stream_key, dims, deviation, limit, pieces, heavy, kind=jnp.bfloat16):
    array = deviation * jax.random.normal(stream_key, dims, jnp.float32)
    if pieces:
        array = array * block_levels(stream_key, dims, pieces, -0.22, 0.18)
    return jnp.clip(with_spikes(array, jax.random.fold_in(stream_key, 3), *heavy), -limit, limit).astype(kind)


def setup_inputs(seed: int = 0) -> dict:
    splits = jax.random.split(jax.random.key(seed), 28)
    tokens = noise_with(splits[0], (BROWS, PACKED_LENGTH, MODEL_WIDTH), 1.0, 6.0, ((0, 8), (1, 4)), (0, 2, 8, 2.0))
    memory = normal_values(splits[1], (BROWS, MEM, MODEL_WIDTH), 1.0, 6.0, ((0, 8), (1, 4)))
    output_grad = normal_values(splits[2], (BROWS, PACKED_LENGTH, MODEL_WIDTH), 1.0, 6.0, ((0, 8), (1, 4)))
    segments = jax.vmap(lambda own: jnp.searchsorted(jnp.cumsum(ragged(own, NDOC, PACKED_LENGTH, PACKED_LENGTH // 2, 1)), jnp.arange(PACKED_LENGTH), side="right"))(jax.random.split(splits[3], BROWS)).reshape((BROWS, PACKED_LENGTH)).astype(jnp.int32)
    memory_segments = jax.vmap(lambda own: jnp.searchsorted(jnp.cumsum(ragged(own, NDOC, MEM, MEM // 2, 1)), jnp.arange(MEM), side="right"))(jax.random.split(splits[4], BROWS)).reshape((BROWS, MEM)).astype(jnp.int32)
    buckets = plant(jax.random.randint(splits[5], (PACKED_LENGTH,), 0, NB), jax.random.fold_in(splits[5], 1), 0, NB - 1).astype(jnp.int32)
    w_query = normal_values(splits[6], (2, MODEL_WIDTH, QUERY_HEADS * HEAD_SIZE), (32 * MODEL_WIDTH) ** -0.5, 0.03125, ((1, 32),), jnp.float32)
    keyvalue_weight = normal_values(splits[7], (2, 2, MODEL_WIDTH, KEY_GROUPS * HEAD_SIZE), MODEL_WIDTH ** -0.5, 0.1875, ((2, 32),), jnp.float32)
    w_output = normal_values(splits[8], (2, QUERY_HEADS * HEAD_SIZE, MODEL_WIDTH), (QUERY_HEADS * HEAD_SIZE // 16) ** -0.5, 0.75, ((1, 32),), jnp.float32)
    w_expand = normal_values(splits[9], (2, MODEL_WIDTH, FF), MODEL_WIDTH ** -0.5, 0.1875, ((1, 32),), jnp.float32)
    w_reduce = normal_values(splits[10], (FF, MODEL_WIDTH), FF ** -0.5, 0.109375, ((0, 32),), jnp.float32)
    gains = jnp.clip(1.0 + 0.1 * jax.random.normal(splits[11], (3, MODEL_WIDTH), jnp.float32), 0.5, 1.5)
    position_bias = normal_values(splits[12], (NB * QUERY_HEADS,), 0.5, 3.0, ((0, 32),), jnp.float32)
    momentum_query = normal_values(splits[13], (2, MODEL_WIDTH, QUERY_HEADS * HEAD_SIZE), (2.0 * DECODER_TOKENS ** 0.5), 1536.0, ((1, 32),), jnp.float32)
    keyvalue_momentum = normal_values(splits[14], (2, 2, MODEL_WIDTH, KEY_GROUPS * HEAD_SIZE), (0.5 * DECODER_TOKENS ** 0.5), 384.0, ((2, 32),), jnp.float32)
    momentum_output = normal_values(splits[15], (2, QUERY_HEADS * HEAD_SIZE, MODEL_WIDTH), (0.2 * DECODER_TOKENS ** 0.5), 160.0, ((1, 32),), jnp.float32)
    momentum_expand = normal_values(splits[16], (2, MODEL_WIDTH, FF), (0.4 * DECODER_TOKENS ** 0.5), 320.0, ((1, 32),), jnp.float32)
    momentum_reduce = normal_values(splits[17], (FF, MODEL_WIDTH), (0.6 * DECODER_TOKENS ** 0.5), 448.0, ((0, 32),), jnp.float32)
    momentum_gains = normal_values(splits[18], (3, MODEL_WIDTH), (0.6 * DECODER_TOKENS ** 0.5), 448.0, ((1, 32),), jnp.float32)
    momentum_position = normal_values(splits[19], (NB * QUERY_HEADS,), (0.3 * DECODER_TOKENS ** 0.5), 224.0, ((0, 32),), jnp.float32)
    average_query = normal_values(splits[20], (2, MODEL_WIDTH, QUERY_HEADS * HEAD_SIZE), (32 * MODEL_WIDTH) ** -0.5, 0.03125, ((1, 32),), jnp.float32)
    keyvalue_average = normal_values(splits[21], (2, 2, MODEL_WIDTH, KEY_GROUPS * HEAD_SIZE), MODEL_WIDTH ** -0.5, 0.1875, ((2, 32),), jnp.float32)
    average_output = normal_values(splits[22], (2, QUERY_HEADS * HEAD_SIZE, MODEL_WIDTH), (QUERY_HEADS * HEAD_SIZE // 16) ** -0.5, 0.75, ((1, 32),), jnp.float32)
    average_expand = normal_values(splits[23], (2, MODEL_WIDTH, FF), MODEL_WIDTH ** -0.5, 0.1875, ((1, 32),), jnp.float32)
    average_reduce = normal_values(splits[24], (FF, MODEL_WIDTH), FF ** -0.5, 0.109375, ((0, 32),), jnp.float32)
    average_gains = jnp.clip(1.0 + 0.1 * jax.random.normal(splits[25], (3, MODEL_WIDTH), jnp.float32), 0.5, 1.5)
    average_position = normal_values(splits[26], (NB * QUERY_HEADS,), 0.5, 3.0, ((0, 32),), jnp.float32)
    return {"tokens": tokens, "memory": memory, "output_grad": output_grad, "segments": segments, "memory_segments": memory_segments, "buckets": buckets, "w_query": w_query, "keyvalue_weight": keyvalue_weight, "w_output": w_output, "w_expand": w_expand, "w_reduce": w_reduce, "gains": gains, "position_bias": position_bias, "momentum_query": momentum_query, "keyvalue_momentum": keyvalue_momentum, "momentum_output": momentum_output, "momentum_expand": momentum_expand, "momentum_reduce": momentum_reduce, "momentum_gains": momentum_gains, "momentum_position": momentum_position, "average_query": average_query, "keyvalue_average": keyvalue_average, "average_output": average_output, "average_expand": average_expand, "average_reduce": average_reduce, "average_gains": average_gains, "average_position": average_position}


HIGHEST = lax.Precision.HIGHEST
EPSILON = 1e-06
NEGATIVE = -1e+30
MOMENTUM = 0.9
AVERAGE = 0.99
STEP_RATES = (0.0015, 0.03, 0.3, 0.04, 0.015, 0.1, 1.0)

@jax.custom_vjp
def low(v):
    return lax.optimization_barrier(v.astype(jnp.bfloat16)).astype(jnp.float32)

@jax.custom_vjp
def low_back(v):
    return v

def low_keep(v):
    return (low(v), None)

def low_pass(kept, grad):
    return (grad,)

def back_keep(v):
    return (v, None)

def back_low(kept, grad):
    return (low(grad),)
low.defvjp(low_keep, low_pass)
low_back.defvjp(back_keep, back_low)

def rounded_both(values):
    return low_back(low(values))

def normalize(values, gain):
    return values * lax.rsqrt(lax.optimization_barrier(jnp.mean(values * values, axis=-1, keepdims=True)) + EPSILON) * gain

def product(left, right):
    return jnp.dot(left, right, precision=HIGHEST)

def attend(query_rows, key_matrix_rows, value_matrix_rows, allowed, relative_bias_table):
    row_length = query_rows.shape[0]
    key_number = key_matrix_rows.shape[0]
    split_query_heads = query_rows.reshape(row_length, KEY_GROUPS, QUERY_HEADS // KEY_GROUPS, HEAD_SIZE)
    grouped_key_heads = key_matrix_rows.reshape(key_number, KEY_GROUPS, HEAD_SIZE)
    grouped_value_heads = value_matrix_rows.reshape(key_number, KEY_GROUPS, HEAD_SIZE)
    scores = jnp.einsum('qgcd,kgd->gcqk', split_query_heads, grouped_key_heads, precision=HIGHEST)
    if relative_bias_table is not None:
        scores = scores + relative_bias_table
    scores = jnp.where(allowed, low_back(scores), NEGATIVE)
    largest = lax.optimization_barrier(jnp.max(scores, axis=-1, keepdims=True))
    exponent = jnp.exp(scores - largest)
    weights = exponent / lax.optimization_barrier(jnp.sum(exponent, axis=-1, keepdims=True))
    context = jnp.einsum('gcqk,kgd->qgcd', low(weights), grouped_value_heads, precision=HIGHEST)
    return context.reshape(row_length, QUERY_HEADS * HEAD_SIZE)

def layer_row(weights, bucket_lookup, token_row, memory_row, segment_row, memory_segment_row):
    query_w, keyval_w, output_w, expand_w, reduce_w, gain_rows, position_bias_rows = weights
    positions = jnp.arange(PACKED_LENGTH, dtype=jnp.int32)
    self_mask = (segment_row[:, None] == segment_row[None, :]) & (positions[None, :] <= positions[:, None])
    cross_mask = segment_row[:, None] == memory_segment_row[None, :]
    relative_bias_table = jnp.transpose(position_bias_rows[bucket_lookup], (2, 0, 1)).reshape(KEY_GROUPS, QUERY_HEADS // KEY_GROUPS, PACKED_LENGTH, PACKED_LENGTH)
    normed = low(normalize(token_row, gain_rows[0]))
    query_rows = rounded_both(product(normed, query_w[0]))
    key_matrix_rows = rounded_both(product(normed, keyval_w[0, 0]))
    value_matrix_rows = rounded_both(product(normed, keyval_w[0, 1]))
    context = rounded_both(attend(query_rows, key_matrix_rows, value_matrix_rows, self_mask, relative_bias_table))
    hidden_one = token_row + low_back(product(context, output_w[0]))
    normed_one = low(normalize(hidden_one, gain_rows[1]))
    cross_queries = rounded_both(product(normed_one, query_w[1]))
    memory_keys = rounded_both(product(memory_row, keyval_w[1, 0]))
    memory_values = rounded_both(product(memory_row, keyval_w[1, 1]))
    cross_context = rounded_both(attend(cross_queries, memory_keys, memory_values, cross_mask, None))
    hidden_two = hidden_one + low_back(product(cross_context, output_w[1]))
    normed_two = low(normalize(hidden_two, gain_rows[2]))
    gate_values = low_back(product(normed_two, expand_w[0]))
    up_values = low_back(product(normed_two, expand_w[1]))
    activated = low(jax.nn.gelu(gate_values, approximate=True) * up_values)
    return hidden_two + low_back(product(activated, reduce_w))

def forward(parameters, token_values, memory_values, segments, memory_segments, bucket_lookup):
    rounded = [low(parameter) for parameter in parameters]
    weights = tuple(rounded[:6]) + (rounded[6].reshape(NB, QUERY_HEADS),)
    row_step = jax.checkpoint(layer_row)
    return lax.map(lambda inputs: row_step(weights, bucket_lookup, *inputs), (token_values, memory_values, segments, memory_segments))

def reference(tokens, memory, output_grad, segments, memory_segments, buckets, w_query, keyvalue_weight, w_output, w_expand, w_reduce, gains, position_bias, momentum_query, keyvalue_momentum, momentum_output, momentum_expand, momentum_reduce, momentum_gains, momentum_position, average_query, keyvalue_average, average_output, average_expand, average_reduce, average_gains, average_position):
    positions = jnp.arange(PACKED_LENGTH, dtype=jnp.int32)
    distance = jnp.clip(positions[:, None] - positions[None, :], 0, PACKED_LENGTH - 1)
    bucket_lookup = buckets[distance]
    params = (w_query, keyvalue_weight, w_output, w_expand, w_reduce, gains, position_bias)

    def wrapped(parameters, token_values, memory_values):
        return forward(parameters, token_values, memory_values, segments, memory_segments, bucket_lookup)
    output, pullback = jax.vjp(wrapped, params, tokens.astype(jnp.float32), memory.astype(jnp.float32))
    gradients, input_grad, memory_grad = pullback(output_grad.astype(jnp.float32))
    momenta = (momentum_query, keyvalue_momentum, momentum_output, momentum_expand, momentum_reduce, momentum_gains, momentum_position)
    averages = (average_query, keyvalue_average, average_output, average_expand, average_reduce, average_gains, average_position)
    token_scale = DECODER_TOKENS ** (-0.5)
    renewals = []
    states = []
    for gradient, master, momentum, average, step_rate in zip(gradients, params, momenta, averages, STEP_RATES):
        renewed = MOMENTUM * momentum + gradient
        weight = master - step_rate * token_scale * (gradient + MOMENTUM * renewed)
        renewals.append(renewed)
        states.append(jnp.stack([weight, AVERAGE * average + (1.0 - AVERAGE) * weight]))
    return (output.astype(jnp.bfloat16), input_grad, memory_grad, gradients[0], gradients[1], gradients[2], gradients[3], gradients[4], gradients[5], gradients[6], renewals[0], renewals[1], renewals[2], renewals[3], renewals[4], renewals[5], renewals[6], states[0], states[1], states[2], states[3], states[4], states[5], states[6])
```

```python
import functools

import jax
import jax.numpy as jnp
from jax import lax
from jax.experimental import pallas as pl
from jax.experimental.pallas import tpu as pltpu
from jax.sharding import PartitionSpec as P

HEAD_SIZE = 64
QUERY_HEADS = 16
NB = 32
EPSILON = 1e-06
NEGATIVE = -1e30
MOMENTUM = 0.9
AVERAGE = 0.99
STEP_RATES = (0.0015, 0.03, 0.3, 0.04, 0.015, 0.1, 1.0)
BF16 = jnp.bfloat16
F32 = jnp.float32
BQ = 128


def nt(a, b):
    return lax.dot_general(a, b, (((1,), (1,)), ((), ())), preferred_element_type=F32)


def nn(a, b):
    return lax.dot_general(a, b, (((1,), (0,)), ((), ())), preferred_element_type=F32)


def tn(a, b):
    return lax.dot_general(a, b, (((0,), (0,)), ((), ())), preferred_element_type=F32)


def stacked(block, group, per):
    first = group * per
    return jnp.concatenate(
        [block[:, (first + c) * HEAD_SIZE : (first + c + 1) * HEAD_SIZE] for c in range(per)], axis=0
    )


def lanes(block, index):
    return block[:, index * HEAD_SIZE : (index + 1) * HEAD_SIZE]


def skew(held, back):
    count, width = held.shape
    rows = lax.broadcasted_iota(jnp.int32, (count, width), 0)
    amount = 1
    while amount < count:
        turned = pltpu.roll(held, width - amount if back else amount, 1)
        held = jnp.where((rows & amount) != 0, turned, held)
        amount *= 2
    return held


def make_strips(base_ref, strip_ref):
    heads, rows, width = strip_ref.shape
    for h in range(heads):
        strip_ref[h] = skew(jnp.broadcast_to(base_ref[h : h + 1, :], (rows, width)), False)


def windows(length):
    reach = length // 2
    for step in range(length // BQ):
        here = slice(step * BQ, (step + 1) * BQ)
        start = max(step * BQ - reach, 0)
        lead = reach - (step * BQ - start)
        yield here, slice(start, (step + 1) * BQ), slice(lead, lead + (step + 1) * BQ - start)


def self_fwd_kernel(q_ref, k_ref, v_ref, seg_row_ref, seg_col_ref, base_ref, o_ref, lse_ref, strip_ref):
    heads = strip_ref.shape[0]
    groups = k_ref.shape[2] // HEAD_SIZE
    per = heads // groups

    @pl.when(pl.program_id(0) == 0)
    def _():
        make_strips(base_ref, strip_ref)

    for here, seen, strip in windows(k_ref.shape[1]):
        same = seg_col_ref[0, here, :] == seg_row_ref[0, :, seen]
        block, keys, values = q_ref[0, here, :], k_ref[0, seen, :], v_ref[0, seen, :]
        outs, sums = [], []
        for g in range(groups):
            scores = nt(stacked(block, g, per), lanes(keys, g))
            probs = []
            for c in range(per):
                bias = strip_ref[g * per + c, :, strip]
                s = jnp.where(same, scores[c * BQ : (c + 1) * BQ] + bias, NEGATIVE)
                top = jnp.max(s, axis=-1, keepdims=True)
                e = jnp.exp(s - top)
                total = jnp.sum(e, axis=-1, keepdims=True)
                probs.append((e * (1.0 / total)).astype(BF16))
                sums.append(top + jnp.log(total))
            ctx = nn(jnp.concatenate(probs, axis=0), lanes(values, g)).astype(BF16)
            outs += [ctx[c * BQ : (c + 1) * BQ] for c in range(per)]
        o_ref[0, here, :] = jnp.concatenate(outs, axis=1)
        lse_ref[0, here, :] = jnp.concatenate(sums, axis=1)


def self_bwd_kernel(
    q_ref, k_ref, v_ref, c_ref, lse_ref, seg_row_ref, seg_col_ref, base_ref,
    dq_ref, dk_ref, dv_ref, lag_ref, strip_ref, grad_ref, dk_acc, dv_acc,
):
    heads = strip_ref.shape[0]
    groups = k_ref.shape[2] // HEAD_SIZE
    per = heads // groups

    @pl.when(pl.program_id(0) == 0)
    def _():
        make_strips(base_ref, strip_ref)
        grad_ref[...] = jnp.zeros_like(grad_ref)

    dk_acc[...] = jnp.zeros_like(dk_acc)
    dv_acc[...] = jnp.zeros_like(dv_acc)
    for here, seen, strip in windows(k_ref.shape[1]):
        same = seg_col_ref[0, here, :] == seg_row_ref[0, :, seen]
        block, keys, values = q_ref[0, here, :], k_ref[0, seen, :], v_ref[0, seen, :]
        cots, lse = c_ref[0, here, :], lse_ref[0, here, :]
        outs = []
        for g in range(groups):
            q2, c2 = stacked(block, g, per), stacked(cots, g, per)
            scores = nt(q2, lanes(keys, g))
            dprobs = nt(c2, lanes(values, g))
            probs, dscores = [], []
            for c in range(per):
                h = g * per + c
                bias = strip_ref[h, :, strip]
                s = jnp.where(same, scores[c * BQ : (c + 1) * BQ] + bias, NEGATIVE)
                p = jnp.exp(s - lse[:, h : h + 1])
                dp = dprobs[c * BQ : (c + 1) * BQ]
                ds = (p * (dp - jnp.sum(p * dp, axis=-1, keepdims=True))).astype(BF16)
                grad_ref[h, :, strip] += ds.astype(F32)
                probs.append(p.astype(BF16))
                dscores.append(ds)
            p2, ds2 = jnp.concatenate(probs, axis=0), jnp.concatenate(dscores, axis=0)
            dq2 = nn(ds2, lanes(keys, g)).astype(BF16)
            outs += [dq2[c * BQ : (c + 1) * BQ] for c in range(per)]
            mine = slice(g * HEAD_SIZE, (g + 1) * HEAD_SIZE)
            dk_acc[mine, seen] += tn(q2, ds2)
            dv_acc[mine, seen] += tn(c2, p2)
        dq_ref[0, here, :] = jnp.concatenate(outs, axis=1)
    dk_ref[0] = dk_acc[...].T.astype(BF16)
    dv_ref[0] = dv_acc[...].T.astype(BF16)

    @pl.when(pl.program_id(0) == pl.num_programs(0) - 1)
    def _():
        for h in range(heads):
            lag_ref[h : h + 1, :] = jnp.sum(skew(grad_ref[h], True), axis=0, keepdims=True)


def self_specs(length, q_width, k_width, heads, strip_width):
    queries = pl.BlockSpec((1, length, q_width), lambda r: (r, 0, 0))
    keys = pl.BlockSpec((1, length, k_width), lambda r: (r, 0, 0))
    sums = pl.BlockSpec((1, length, heads), lambda r: (r, 0, 0))
    seg_row = pl.BlockSpec((1, 1, length), lambda r: (r, 0, 0))
    seg_col = pl.BlockSpec((1, length, 1), lambda r: (r, 0, 0))
    base = pl.BlockSpec((heads, strip_width), lambda r: (0, 0))
    return queries, keys, sums, seg_row, seg_col, base


def self_attention(q, k, v, segments, base):
    rows, length, q_width = q.shape
    heads, strip_width = base.shape
    queries, keys, sums, seg_row, seg_col, base_spec = self_specs(
        length, q_width, k.shape[2], heads, strip_width
    )
    work = rows * heads * length * length * 3 // 8
    return pl.pallas_call(
        self_fwd_kernel,
        grid=(rows,),
        in_specs=[queries, keys, keys, seg_row, seg_col, base_spec],
        out_specs=[queries, sums],
        out_shape=[
            jax.ShapeDtypeStruct(q.shape, BF16),
            jax.ShapeDtypeStruct((rows, length, heads), F32),
        ],
        scratch_shapes=[pltpu.VMEM((heads, BQ, strip_width), F32)],
        compiler_params=pltpu.CompilerParams(vmem_limit_bytes=48 << 20),
        cost_estimate=pl.CostEstimate(
            flops=work * 4 * HEAD_SIZE, transcendentals=work, bytes_accessed=q.size * 8
        ),
        name="self_attention",
    )(q, k, v, segments[:, None, :], segments[:, :, None], base)


def self_attention_back(q, k, v, cots, lse, segments, base):
    rows, length, q_width = q.shape
    heads, strip_width = base.shape
    k_width = k.shape[2]
    queries, keys, sums, seg_row, seg_col, base_spec = self_specs(
        length, q_width, k_width, heads, strip_width
    )
    work = rows * heads * length * length * 3 // 8
    return pl.pallas_call(
        self_bwd_kernel,
        grid=(rows,),
        in_specs=[queries, keys, keys, queries, sums, seg_row, seg_col, base_spec],
        out_specs=[queries, keys, keys, base_spec],
        out_shape=[
            jax.ShapeDtypeStruct(q.shape, BF16),
            jax.ShapeDtypeStruct(k.shape, BF16),
            jax.ShapeDtypeStruct(k.shape, BF16),
            jax.ShapeDtypeStruct((heads, strip_width), F32),
        ],
        scratch_shapes=[
            pltpu.VMEM((heads, BQ, strip_width), F32),
            pltpu.VMEM((heads, BQ, strip_width), F32),
            pltpu.VMEM((k_width, length), F32),
            pltpu.VMEM((k_width, length), F32),
        ],
        compiler_params=pltpu.CompilerParams(vmem_limit_bytes=48 << 20),
        cost_estimate=pl.CostEstimate(
            flops=work * 10 * HEAD_SIZE, transcendentals=work, bytes_accessed=q.size * 12
        ),
        name="self_attention_back",
    )(q, k, v, cots, lse, segments[:, None, :], segments[:, :, None], base)


def cross_fwd_kernel(q_ref, k_ref, v_ref, seg_row_ref, seg_col_ref, o_ref, *lse_refs):
    block, keys, values = q_ref[0], k_ref[0], v_ref[0]
    count = block.shape[0]
    groups = keys.shape[1] // HEAD_SIZE
    per = block.shape[1] // keys.shape[1]
    same = seg_col_ref[0] == seg_row_ref[0]
    outs = []
    for g in range(groups):
        scores = nt(stacked(block, g, per), lanes(keys, g))
        probs = []
        for c in range(per):
            s = jnp.where(same, scores[c * count : (c + 1) * count], NEGATIVE)
            top = jnp.max(s, axis=-1, keepdims=True)
            e = jnp.exp(s - top)
            total = jnp.sum(e, axis=-1, keepdims=True)
            probs.append((e * (1.0 / total)).astype(BF16))
        ctx = nn(jnp.concatenate(probs, axis=0), lanes(values, g)).astype(BF16)
        outs += [ctx[c * count : (c + 1) * count] for c in range(per)]
    o_ref[0] = jnp.concatenate(outs, axis=1)


def cross_bwd_kernel(q_ref, k_ref, v_ref, c_ref, seg_row_ref, seg_col_ref, dq_ref, dk_ref, dv_ref):
    block, keys, values, cots = q_ref[0], k_ref[0], v_ref[0], c_ref[0]
    count = block.shape[0]
    groups = keys.shape[1] // HEAD_SIZE
    per = block.shape[1] // keys.shape[1]
    same = seg_col_ref[0] == seg_row_ref[0]
    outs, dkeys, dvalues = [], [], []
    for g in range(groups):
        q2, c2 = stacked(block, g, per), stacked(cots, g, per)
        scores = nt(q2, lanes(keys, g))
        dprobs = nt(c2, lanes(values, g))
        probs, dscores = [], []
        for c in range(per):
            s = jnp.where(same, scores[c * count : (c + 1) * count], NEGATIVE)
            top = jnp.max(s, axis=-1, keepdims=True)
            e = jnp.exp(s - top)
            p = e * (1.0 / jnp.sum(e, axis=-1, keepdims=True))
            dp = dprobs[c * count : (c + 1) * count]
            dscores.append((p * (dp - jnp.sum(p * dp, axis=-1, keepdims=True))).astype(BF16))
            probs.append(p.astype(BF16))
        p2, ds2 = jnp.concatenate(probs, axis=0), jnp.concatenate(dscores, axis=0)
        dq2 = nn(ds2, lanes(keys, g)).astype(BF16)
        outs += [dq2[c * count : (c + 1) * count] for c in range(per)]
        dkeys.append(tn(q2, ds2))
        dvalues.append(tn(c2, p2))
    dq_ref[0] = jnp.concatenate(outs, axis=1)
    dk_ref[0] = jnp.concatenate(dkeys, axis=0).T.astype(dk_ref.dtype)
    dv_ref[0] = jnp.concatenate(dvalues, axis=0).T.astype(dv_ref.dtype)


def cross_specs(q, k):
    rows, count, q_width = q.shape
    memory, k_width = k.shape[1:]
    step = 2 * HEAD_SIZE
    q_step = step * (q_width // k_width)
    queries = pl.BlockSpec((1, count, q_step), lambda r, g: (r, 0, g))
    keys = pl.BlockSpec((1, memory, step), lambda r, g: (r, 0, g))
    seg_row = pl.BlockSpec((1, 1, memory), lambda r, g: (r, 0, 0))
    seg_col = pl.BlockSpec((1, count, 1), lambda r, g: (r, 0, 0))
    return (rows, k_width // step), queries, keys, seg_row, seg_col


def cross_attention(q, k, v, segments, memory_segments):
    grid, queries, keys, seg_row, seg_col = cross_specs(q, k)
    work = q.size // HEAD_SIZE * k.shape[1]
    return pl.pallas_call(
        cross_fwd_kernel,
        grid=grid,
        in_specs=[queries, keys, keys, seg_row, seg_col],
        out_specs=queries,
        out_shape=jax.ShapeDtypeStruct(q.shape, BF16),
        compiler_params=pltpu.CompilerParams(vmem_limit_bytes=48 << 20),
        cost_estimate=pl.CostEstimate(
            flops=work * 4 * HEAD_SIZE, transcendentals=work, bytes_accessed=q.size * 4 + k.size * 4
        ),
        name="cross_attention",
    )(q, k, v, memory_segments[:, None, :], segments[:, :, None])


def cross_attention_back(q, k, v, cots, segments, memory_segments):
    grid, queries, keys, seg_row, seg_col = cross_specs(q, k)
    work = q.size // HEAD_SIZE * k.shape[1]
    return pl.pallas_call(
        cross_bwd_kernel,
        grid=grid,
        in_specs=[queries, keys, keys, queries, seg_row, seg_col],
        out_specs=[queries, keys, keys],
        out_shape=[
            jax.ShapeDtypeStruct(q.shape, BF16),
            jax.ShapeDtypeStruct(k.shape, BF16),
            jax.ShapeDtypeStruct(k.shape, BF16),
        ],
        compiler_params=pltpu.CompilerParams(vmem_limit_bytes=48 << 20),
        cost_estimate=pl.CostEstimate(
            flops=work * 10 * HEAD_SIZE, transcendentals=work, bytes_accessed=q.size * 6 + k.size * 8
        ),
        name="cross_attention_back",
    )(q, k, v, cots, memory_segments[:, None, :], segments[:, :, None])


def bit_count(axis):
    return lax.axis_size(axis).bit_length() - 1


def flip(value, axis, bit):
    count = lax.axis_size(axis)
    return lax.ppermute(value, axis, [(i, i ^ (1 << bit)) for i in range(count)])


def scatter_order(first):
    seq_bits = list(range(bit_count("seq")))
    if first:
        seq_bits.reverse()
    return [("batch", 0)] + [("seq", b) for b in seq_bits] + [("batch", b) for b in range(1, bit_count("batch"))]


def scatter_sum(full, turned):
    batch_bits, seq_bits = bit_count("batch"), bit_count("seq")
    left = [("batch", b) for b in reversed(range(batch_bits))] + [("seq", b) for b in reversed(range(seq_bits))]
    own_rows = full.shape[0] >> len(left)
    parts = [full.reshape((2,) * len(left) + (own_rows,) + full.shape[1:])]
    for axis, bit in scatter_order(turned):
        where = left.index((axis, bit))
        mine = (lax.axis_index(axis) >> bit) & 1
        away = sum(lax.dynamic_index_in_dim(p, 1 - mine, where, False).astype(F32) for p in parts)
        came = flip(away.astype(BF16), axis, bit)
        parts = [lax.dynamic_index_in_dim(p, mine, where, False) for p in parts] + [came]
        left.pop(where)
    return sum(p.astype(F32) for p in parts)


def small_sum(values):
    got = lax.all_to_all(values, ("batch", "seq"), 0, 0, tiled=True)
    return jnp.sum(got, axis=0)


def inverse_rms(values):
    return lax.rsqrt(jnp.mean(values * values, axis=-1, keepdims=True) + EPSILON)


def norm_back(values, inverse, gain, upstream):
    weighted = gain * upstream
    dot = jnp.mean(weighted * values, axis=-1, keepdims=True)
    grad = inverse * weighted - values * (inverse * inverse * inverse) * dot
    return grad, jnp.sum(upstream * values * inverse, axis=0)


def gelu_parts(v):
    scale = 0.7978845608028654
    inner = scale * (v + 0.044715 * (v * v * v))
    t = jnp.tanh(inner)
    value = 0.5 * v * (1.0 + t)
    slope = 0.5 * (1.0 + t) + 0.5 * v * (1.0 - t * t) * (scale * (1.0 + 3 * 0.044715 * (v * v)))
    return value, slope


def shards(
    tokens, memory, output_grad, segments, memory_segments, buckets,
    w_query, keyvalue_weight, w_output, w_expand, w_reduce, gains, position_bias,
    momentum_query, keyvalue_momentum, momentum_output, momentum_expand, momentum_reduce,
    momentum_gains, momentum_position,
    average_query, keyvalue_average, average_output, average_expand, average_reduce,
    average_gains, average_position,
):
    every = ("batch", "seq")
    seq_count, seq_index = lax.axis_size("seq"), lax.axis_index("seq")
    devices = lax.axis_size("batch") * seq_count
    rows, part, width = tokens.shape
    length = part * seq_count
    memory_part = memory.shape[1]
    own = w_query.shape[1]
    kv_width = keyvalue_weight.shape[3]
    heads_local = QUERY_HEADS // seq_count
    q_local, kv_local = width // seq_count, kv_width // seq_count

    wq, wkv = w_query.astype(BF16), keyvalue_weight.astype(BF16)
    wo, we, wr = w_output.astype(BF16), w_expand.astype(BF16), w_reduce.astype(BF16)
    first = jnp.concatenate(
        [
            wq[0].reshape(own, seq_count, q_local),
            wkv[0, 0].reshape(own, seq_count, kv_local),
            wkv[0, 1].reshape(own, seq_count, kv_local),
        ],
        axis=2,
    ).reshape(own, -1)
    bias_own = position_bias.shape[0]
    small = jnp.concatenate([gains.astype(BF16).reshape(-1), position_bias.astype(BF16)])
    small = jnp.pad(small, (0, -small.shape[0] % 128))
    small_rows = lax.all_gather(small, every, axis=0)
    gain_values = (
        small_rows[:, : 3 * own].reshape(devices, 3, own).transpose(1, 0, 2).reshape(3, width).astype(F32)
    )
    table = small_rows[:, 3 * own : 3 * own + bias_own].reshape(NB, QUERY_HEADS).astype(F32)
    w_first = lax.all_gather(first, every, axis=0, tiled=True)
    middle = jnp.stack([jnp.concatenate([wkv[1, 0], wkv[1, 1]], axis=1), wo[0], wq[1], wo[1]])
    w_middle = lax.all_gather(middle, every, axis=1, tiled=True)
    w_kv1, w_o0, w_q1, w_o1 = w_middle[0], w_middle[1], w_middle[2], w_middle[3]
    w_exp = lax.all_gather(jnp.concatenate([we[0], we[1]], axis=1), every, axis=0, tiled=True)
    w_red = lax.all_gather(wr, every, axis=0, tiled=True)
    all_segments = lax.all_gather(segments, "seq", axis=1, tiled=True)
    all_memory_segments = lax.all_gather(memory_segments, "seq", axis=1, tiled=True)

    reach = length // 2
    strip_width = 2 * reach + BQ
    lag = reach - jnp.arange(strip_width, dtype=jnp.int32)
    lag_ok = lag >= 0
    lag_bucket = jnp.where(lag_ok, jnp.take(buckets, jnp.clip(lag, 0, length - 1)), -1)
    picks = (lag_bucket[None, :] == jnp.arange(NB, dtype=jnp.int32)[:, None]).astype(F32)
    table_local = lax.dynamic_slice_in_dim(table, seq_index * heads_local, heads_local, 1)
    base = jnp.dot(table_local.T, picks, precision=lax.Precision.HIGHEST)
    base = jnp.where(lag_ok[None, :], base, NEGATIVE)

    x = tokens.astype(F32).reshape(rows * part, width)
    inv_zero = inverse_rms(x)
    normed = (x * inv_zero * gain_values[0]).astype(BF16)
    qkv = nn(normed, w_first).astype(BF16).reshape(rows, part, -1)
    head_qkv = lax.all_to_all(qkv, "seq", split_axis=2, concat_axis=1, tiled=True)
    hq = head_qkv[:, :, :q_local]
    hk = head_qkv[:, :, q_local : q_local + kv_local]
    hv = head_qkv[:, :, q_local + kv_local :]
    head_context, lse = self_attention(hq, hk, hv, all_segments, base)
    context = lax.all_to_all(head_context, "seq", split_axis=1, concat_axis=2, tiled=True).reshape(-1, width)

    mem = memory.reshape(rows * memory_part, width)
    mkv = nn(mem, w_kv1).astype(BF16).reshape(rows, memory_part, -1)
    all_mkv = lax.all_gather(mkv, "seq", axis=1, tiled=True)
    mk, mv = all_mkv[:, :, :kv_width], all_mkv[:, :, kv_width:]
    hidden_one = x + nn(context, w_o0)
    inv_one = inverse_rms(hidden_one)
    normed_one = (hidden_one * inv_one * gain_values[1]).astype(BF16)
    cross_q = nn(normed_one, w_q1).astype(BF16).reshape(rows, part, width)
    cross_context = cross_attention(cross_q, mk, mv, segments, all_memory_segments)
    cross_flat = cross_context.reshape(-1, width)
    hidden_two = hidden_one + nn(cross_flat, w_o1)
    inv_two = inverse_rms(hidden_two)
    normed_two = (hidden_two * inv_two * gain_values[2]).astype(BF16)

    ff = we.shape[2]
    gate = nn(normed_two, w_exp[:, :ff])
    up = nn(normed_two, w_exp[:, ff:])
    gelu_value, gelu_slope = gelu_parts(gate)
    activated = (gelu_value * up).astype(BF16)
    og = output_grad.reshape(rows * part, width)
    result = (hidden_two + nn(activated, w_red)).astype(BF16).reshape(tokens.shape)
    grad_reduce = scatter_sum(tn(activated, og).astype(BF16), False)
    activated_grad = nt(og, w_red)
    gate_grad = (activated_grad * up * gelu_slope).astype(BF16)
    up_grad = (activated_grad * gelu_value).astype(BF16)
    grad_gate = scatter_sum(tn(normed_two, gate_grad).astype(BF16), False)
    grad_up = scatter_sum(tn(normed_two, up_grad).astype(BF16), True)
    normed_two_grad = nt(gate_grad, w_exp[:, :ff]) + nt(up_grad, w_exp[:, ff:])
    part_two, gain_two = norm_back(hidden_two, inv_two, gain_values[2], normed_two_grad)
    hidden_two_grad = og.astype(F32) + part_two

    cross_out_grad = hidden_two_grad.astype(BF16)
    grad_o1 = scatter_sum(tn(cross_flat, cross_out_grad).astype(BF16), True)
    cross_cots = nt(cross_out_grad, w_o1).astype(BF16).reshape(rows, part, width)
    cross_dq, mdk, mdv = cross_attention_back(cross_q, mk, mv, cross_cots, segments, all_memory_segments)
    mdkv = jnp.concatenate([mdk, mdv], axis=2).reshape(rows, seq_count, memory_part, -1)
    mdkv = lax.all_to_all(mdkv, "seq", split_axis=1, concat_axis=1, tiled=True)
    mdkv = jnp.sum(mdkv.astype(F32), axis=1).astype(BF16).reshape(rows * memory_part, -1)
    memory_grad = nt(mdkv, w_kv1).reshape(memory.shape)
    grad_kv1 = scatter_sum(tn(mem, mdkv).astype(BF16), False)
    cross_dq = cross_dq.reshape(-1, width)
    grad_q1 = scatter_sum(tn(normed_one, cross_dq).astype(BF16), True)
    part_one, gain_one = norm_back(hidden_one, inv_one, gain_values[1], nt(cross_dq, w_q1))
    hidden_one_grad = hidden_two_grad + part_one

    self_out_grad = hidden_one_grad.astype(BF16)
    grad_o0 = scatter_sum(tn(context, self_out_grad).astype(BF16), False)
    cots = nt(self_out_grad, w_o0).astype(BF16).reshape(rows, part, width)
    head_cots = lax.all_to_all(cots, "seq", split_axis=2, concat_axis=1, tiled=True)
    hdq, hdk, hdv, lag_sums = self_attention_back(hq, hk, hv, head_cots, lse, all_segments, base)
    head_grads = jnp.concatenate([hdq, hdk, hdv], axis=2)
    dqkv = lax.all_to_all(head_grads, "seq", split_axis=1, concat_axis=2, tiled=True).reshape(rows * part, -1)
    grad_first = scatter_sum(tn(normed, dqkv).astype(BF16), False)
    part_zero, gain_zero = norm_back(x, inv_zero, gain_values[0], nt(dqkv, w_first))
    input_grad = (hidden_one_grad + part_zero).reshape(tokens.shape)

    table_part = jnp.dot(picks, lag_sums.T, precision=lax.Precision.HIGHEST)
    table_grad = lax.dynamic_update_slice(
        jnp.zeros((NB, QUERY_HEADS), F32), table_part, (0, seq_index * heads_local)
    ).reshape(devices, -1)
    gains_grad = jnp.stack([gain_zero, gain_one, gain_two]).reshape(3, devices, own)
    gains_grad = gains_grad.transpose(1, 0, 2).reshape(devices, -1)
    small_grads = small_sum(jnp.concatenate([gains_grad, table_grad], axis=1))
    shard_gains = small_grads[: 3 * own].reshape(3, own)
    shard_table = small_grads[3 * own :]

    first_grads = grad_first.reshape(own, seq_count, -1)
    shard_query = jnp.stack([first_grads[:, :, :q_local].reshape(own, width), grad_q1])
    shard_keyval = jnp.stack(
        [
            jnp.stack(
                [
                    first_grads[:, :, q_local : q_local + kv_local].reshape(own, kv_width),
                    first_grads[:, :, q_local + kv_local :].reshape(own, kv_width),
                ]
            ),
            jnp.stack([grad_kv1[:, :kv_width], grad_kv1[:, kv_width:]]),
        ]
    )
    gradients = (
        shard_query,
        shard_keyval,
        jnp.stack([grad_o0, grad_o1]),
        jnp.stack([grad_gate, grad_up]),
        grad_reduce,
        shard_gains,
        shard_table,
    )
    token_scale = (rows * part * devices) ** (-0.5)
    masters = (w_query, keyvalue_weight, w_output, w_expand, w_reduce, gains, position_bias)
    momenta = (
        momentum_query, keyvalue_momentum, momentum_output, momentum_expand, momentum_reduce,
        momentum_gains, momentum_position,
    )
    averages = (
        average_query, keyvalue_average, average_output, average_expand, average_reduce,
        average_gains, average_position,
    )
    renewals, states = [], []
    for gradient, master, momentum, average, step_rate in zip(gradients, masters, momenta, averages, STEP_RATES):
        renewed = MOMENTUM * momentum + gradient
        weight = master - step_rate * token_scale * (gradient + MOMENTUM * renewed)
        renewals.append(renewed)
        states.append(jnp.stack([weight, AVERAGE * average + (1.0 - AVERAGE) * weight]))
    return (result, input_grad, memory_grad.astype(F32), *gradients, *renewals, *states)


def solution(mesh):
    every = ("batch", "seq")
    params = (
        P(None, every, None),
        P(None, None, every, None),
        P(None, every, None),
        P(None, every, None),
        P(every, None),
        P(None, every),
        P(every),
    )
    stacked_params = (
        P(None, None, every, None),
        P(None, None, None, every, None),
        P(None, None, every, None),
        P(None, None, every, None),
        P(None, every, None),
        P(None, None, every),
        P(None, every),
    )
    acts = P("batch", "seq", None)
    return jax.shard_map(
        shards,
        mesh=mesh,
        in_specs=(acts, acts, acts, P("batch", "seq"), P("batch", "seq"), P(), *params, *params, *params),
        out_specs=(acts, acts, acts, *params, *params, *stacked_params),
        check_vma=False,
    )
```

```python
import functools

import jax
import jax.numpy as jnp
from jax import lax
from jax.experimental import pallas as pl
from jax.experimental.pallas import tpu as pltpu
from jax.sharding import PartitionSpec as P

HEAD_SIZE = 64
QUERY_HEADS = 16
NB = 32
EPSILON = 1e-06
NEGATIVE = -1e30
MOMENTUM = 0.9
AVERAGE = 0.99
STEP_RATES = (0.0015, 0.03, 0.3, 0.04, 0.015, 0.1, 1.0)
BF16 = jnp.bfloat16
F32 = jnp.float32
BQ = 128


def nt(a, b):
    return lax.dot_general(a, b, (((1,), (1,)), ((), ())), preferred_element_type=F32)


def nn(a, b):
    return lax.dot_general(a, b, (((1,), (0,)), ((), ())), preferred_element_type=F32)


def tn(a, b):
    return lax.dot_general(a, b, (((0,), (0,)), ((), ())), preferred_element_type=F32)


def stacked(block, group, per):
    first = group * per
    return jnp.concatenate(
        [block[:, (first + c) * HEAD_SIZE : (first + c + 1) * HEAD_SIZE] for c in range(per)], axis=0
    )


def lanes(block, index):
    return block[:, index * HEAD_SIZE : (index + 1) * HEAD_SIZE]


def skew(held, back):
    count, width = held.shape
    rows = lax.broadcasted_iota(jnp.int32, (count, width), 0)
    amount = 1
    while amount < count:
        turned = pltpu.roll(held, width - amount if back else amount, 1)
        held = jnp.where((rows & amount) != 0, turned, held)
        amount *= 2
    return held


def make_strips(base_ref, strip_ref):
    heads, rows, width = strip_ref.shape
    for h in range(heads):
        strip_ref[h] = skew(jnp.broadcast_to(base_ref[h : h + 1, :], (rows, width)), False)


def windows(length):
    reach = length // 2
    for step in range(length // BQ):
        here = slice(step * BQ, (step + 1) * BQ)
        start = max(step * BQ - reach, 0)
        lead = reach - (step * BQ - start)
        yield here, slice(start, (step + 1) * BQ), slice(lead, lead + (step + 1) * BQ - start)


def head_layout(heads, width):
    q_width = heads * HEAD_SIZE
    k_width = (width - q_width) // 2
    return slice(0, q_width), slice(q_width, q_width + k_width), slice(q_width + k_width, width), k_width // HEAD_SIZE


def self_fwd_kernel(qkv_ref, seg_row_ref, seg_col_ref, base_ref, o_ref, lse_ref, strip_ref):
    heads = strip_ref.shape[0]
    in_q, in_k, in_v, groups = head_layout(heads, qkv_ref.shape[2])
    per = heads // groups

    @pl.when(pl.program_id(0) == 0)
    def _():
        make_strips(base_ref, strip_ref)

    for here, seen, strip in windows(qkv_ref.shape[1]):
        same = seg_col_ref[0, here, :] == seg_row_ref[0, :, seen]
        block, keys, values = qkv_ref[0, here, in_q], qkv_ref[0, seen, in_k], qkv_ref[0, seen, in_v]
        outs, sums = [], []
        for g in range(groups):
            scores = nt(stacked(block, g, per), lanes(keys, g))
            probs = []
            for c in range(per):
                bias = strip_ref[g * per + c, :, strip]
                s = jnp.where(same, scores[c * BQ : (c + 1) * BQ] + bias, NEGATIVE)
                top = jnp.max(s, axis=-1, keepdims=True)
                e = jnp.exp(s - top)
                total = jnp.sum(e, axis=-1, keepdims=True)
                probs.append((e * (1.0 / total)).astype(BF16))
                sums.append(top + jnp.log(total))
            ctx = nn(jnp.concatenate(probs, axis=0), lanes(values, g)).astype(BF16)
            outs += [ctx[c * BQ : (c + 1) * BQ] for c in range(per)]
        o_ref[0, here, :] = jnp.concatenate(outs, axis=1)
        lse_ref[0, here, :] = jnp.concatenate(sums, axis=1)


def self_bwd_kernel(
    qkv_ref, c_ref, lse_ref, seg_row_ref, seg_col_ref, base_ref,
    d_ref, lag_ref, strip_ref, grad_ref, dk_acc, dv_acc,
):
    heads = strip_ref.shape[0]
    in_q, in_k, in_v, groups = head_layout(heads, qkv_ref.shape[2])
    per = heads // groups

    @pl.when(pl.program_id(0) == 0)
    def _():
        make_strips(base_ref, strip_ref)
        grad_ref[...] = jnp.zeros_like(grad_ref)

    dk_acc[...] = jnp.zeros_like(dk_acc)
    dv_acc[...] = jnp.zeros_like(dv_acc)
    for here, seen, strip in windows(qkv_ref.shape[1]):
        same = seg_col_ref[0, here, :] == seg_row_ref[0, :, seen]
        block, keys, values = qkv_ref[0, here, in_q], qkv_ref[0, seen, in_k], qkv_ref[0, seen, in_v]
        cots, lse = c_ref[0, here, :], lse_ref[0, here, :]
        outs = []
        for g in range(groups):
            q2, c2 = stacked(block, g, per), stacked(cots, g, per)
            scores = nt(q2, lanes(keys, g))
            dprobs = nt(c2, lanes(values, g))
            probs, dscores = [], []
            for c in range(per):
                h = g * per + c
                bias = strip_ref[h, :, strip]
                s = jnp.where(same, scores[c * BQ : (c + 1) * BQ] + bias, NEGATIVE)
                p = jnp.exp(s - lse[:, h : h + 1])
                dp = dprobs[c * BQ : (c + 1) * BQ]
                ds = (p * (dp - jnp.sum(p * dp, axis=-1, keepdims=True))).astype(BF16)
                grad_ref[h, :, strip] += ds.astype(F32)
                probs.append(p.astype(BF16))
                dscores.append(ds)
            p2, ds2 = jnp.concatenate(probs, axis=0), jnp.concatenate(dscores, axis=0)
            dq2 = nn(ds2, lanes(keys, g)).astype(BF16)
            outs += [dq2[c * BQ : (c + 1) * BQ] for c in range(per)]
            mine = slice(g * HEAD_SIZE, (g + 1) * HEAD_SIZE)
            dk_acc[mine, seen] += tn(q2, ds2)
            dv_acc[mine, seen] += tn(c2, p2)
        d_ref[0, here, in_q] = jnp.concatenate(outs, axis=1)
    d_ref[0, :, in_k] = dk_acc[...].T.astype(BF16)
    d_ref[0, :, in_v] = dv_acc[...].T.astype(BF16)

    @pl.when(pl.program_id(0) == pl.num_programs(0) - 1)
    def _():
        for h in range(heads):
            lag_ref[h : h + 1, :] = jnp.sum(skew(grad_ref[h], True), axis=0, keepdims=True)


def self_specs(length, width, heads, strip_width):
    qkv = pl.BlockSpec((1, length, width), lambda r: (r, 0, 0))
    queries = pl.BlockSpec((1, length, heads * HEAD_SIZE), lambda r: (r, 0, 0))
    sums = pl.BlockSpec((1, length, heads), lambda r: (r, 0, 0))
    seg_row = pl.BlockSpec((1, 1, length), lambda r: (r, 0, 0))
    seg_col = pl.BlockSpec((1, length, 1), lambda r: (r, 0, 0))
    base = pl.BlockSpec((heads, strip_width), lambda r: (0, 0))
    return qkv, queries, sums, seg_row, seg_col, base


def self_attention(qkv, segments, base):
    rows, length, width = qkv.shape
    heads, strip_width = base.shape
    all_spec, queries, sums, seg_row, seg_col, base_spec = self_specs(length, width, heads, strip_width)
    work = rows * heads * length * length * 3 // 8
    return pl.pallas_call(
        self_fwd_kernel,
        grid=(rows,),
        in_specs=[all_spec, seg_row, seg_col, base_spec],
        out_specs=[queries, sums],
        out_shape=[
            jax.ShapeDtypeStruct((rows, length, heads * HEAD_SIZE), BF16),
            jax.ShapeDtypeStruct((rows, length, heads), F32),
        ],
        scratch_shapes=[pltpu.VMEM((heads, BQ, strip_width), F32)],
        compiler_params=pltpu.CompilerParams(vmem_limit_bytes=48 << 20),
        cost_estimate=pl.CostEstimate(
            flops=work * 4 * HEAD_SIZE, transcendentals=work, bytes_accessed=qkv.size * 4
        ),
        name="self_attention",
    )(qkv, segments[:, None, :], segments[:, :, None], base)


def self_attention_back(qkv, cots, lse, segments, base):
    rows, length, width = qkv.shape
    heads, strip_width = base.shape
    all_spec, queries, sums, seg_row, seg_col, base_spec = self_specs(length, width, heads, strip_width)
    k_width = (width - heads * HEAD_SIZE) // 2
    work = rows * heads * length * length * 3 // 8
    return pl.pallas_call(
        self_bwd_kernel,
        grid=(rows,),
        in_specs=[all_spec, queries, sums, seg_row, seg_col, base_spec],
        out_specs=[all_spec, base_spec],
        out_shape=[
            jax.ShapeDtypeStruct(qkv.shape, BF16),
            jax.ShapeDtypeStruct((heads, strip_width), F32),
        ],
        scratch_shapes=[
            pltpu.VMEM((heads, BQ, strip_width), F32),
            pltpu.VMEM((heads, BQ, strip_width), F32),
            pltpu.VMEM((k_width, length), F32),
            pltpu.VMEM((k_width, length), F32),
        ],
        compiler_params=pltpu.CompilerParams(vmem_limit_bytes=48 << 20),
        cost_estimate=pl.CostEstimate(
            flops=work * 10 * HEAD_SIZE, transcendentals=work, bytes_accessed=qkv.size * 6
        ),
        name="self_attention_back",
    )(qkv, cots, lse, segments[:, None, :], segments[:, :, None], base)


def cross_fwd_kernel(q_ref, k_ref, v_ref, seg_row_ref, seg_col_ref, o_ref, *lse_refs):
    block, keys, values = q_ref[0], k_ref[0], v_ref[0]
    count = block.shape[0]
    groups = keys.shape[1] // HEAD_SIZE
    per = block.shape[1] // keys.shape[1]
    same = seg_col_ref[0] == seg_row_ref[0]
    outs = []
    for g in range(groups):
        scores = nt(stacked(block, g, per), lanes(keys, g))
        probs = []
        for c in range(per):
            s = jnp.where(same, scores[c * count : (c + 1) * count], NEGATIVE)
            top = jnp.max(s, axis=-1, keepdims=True)
            e = jnp.exp(s - top)
            total = jnp.sum(e, axis=-1, keepdims=True)
            probs.append((e * (1.0 / total)).astype(BF16))
        ctx = nn(jnp.concatenate(probs, axis=0), lanes(values, g)).astype(BF16)
        outs += [ctx[c * count : (c + 1) * count] for c in range(per)]
    o_ref[0] = jnp.concatenate(outs, axis=1)


def cross_bwd_kernel(q_ref, k_ref, v_ref, c_ref, seg_row_ref, seg_col_ref, dq_ref, dk_ref, dv_ref):
    block, keys, values, cots = q_ref[0], k_ref[0], v_ref[0], c_ref[0]
    count = block.shape[0]
    groups = keys.shape[1] // HEAD_SIZE
    per = block.shape[1] // keys.shape[1]
    same = seg_col_ref[0] == seg_row_ref[0]
    outs, dkeys, dvalues = [], [], []
    for g in range(groups):
        q2, c2 = stacked(block, g, per), stacked(cots, g, per)
        scores = nt(q2, lanes(keys, g))
        dprobs = nt(c2, lanes(values, g))
        probs, dscores = [], []
        for c in range(per):
            s = jnp.where(same, scores[c * count : (c + 1) * count], NEGATIVE)
            top = jnp.max(s, axis=-1, keepdims=True)
            e = jnp.exp(s - top)
            p = e * (1.0 / jnp.sum(e, axis=-1, keepdims=True))
            dp = dprobs[c * count : (c + 1) * count]
            dscores.append((p * (dp - jnp.sum(p * dp, axis=-1, keepdims=True))).astype(BF16))
            probs.append(p.astype(BF16))
        p2, ds2 = jnp.concatenate(probs, axis=0), jnp.concatenate(dscores, axis=0)
        dq2 = nn(ds2, lanes(keys, g)).astype(BF16)
        outs += [dq2[c * count : (c + 1) * count] for c in range(per)]
        dkeys.append(tn(q2, ds2))
        dvalues.append(tn(c2, p2))
    dq_ref[0] = jnp.concatenate(outs, axis=1)
    dk_ref[0] = jnp.concatenate(dkeys, axis=0).T.astype(dk_ref.dtype)
    dv_ref[0] = jnp.concatenate(dvalues, axis=0).T.astype(dv_ref.dtype)


def cross_specs(q, k):
    rows, count, q_width = q.shape
    memory, k_width = k.shape[1:]
    step = 2 * HEAD_SIZE
    q_step = step * (q_width // k_width)
    queries = pl.BlockSpec((1, count, q_step), lambda r, g: (r, 0, g))
    keys = pl.BlockSpec((1, memory, step), lambda r, g: (r, 0, g))
    seg_row = pl.BlockSpec((1, 1, memory), lambda r, g: (r, 0, 0))
    seg_col = pl.BlockSpec((1, count, 1), lambda r, g: (r, 0, 0))
    return (rows, k_width // step), queries, keys, seg_row, seg_col


def cross_attention(q, k, v, segments, memory_segments):
    grid, queries, keys, seg_row, seg_col = cross_specs(q, k)
    work = q.size // HEAD_SIZE * k.shape[1]
    return pl.pallas_call(
        cross_fwd_kernel,
        grid=grid,
        in_specs=[queries, keys, keys, seg_row, seg_col],
        out_specs=queries,
        out_shape=jax.ShapeDtypeStruct(q.shape, BF16),
        compiler_params=pltpu.CompilerParams(vmem_limit_bytes=48 << 20),
        cost_estimate=pl.CostEstimate(
            flops=work * 4 * HEAD_SIZE, transcendentals=work, bytes_accessed=q.size * 4 + k.size * 4
        ),
        name="cross_attention",
    )(q, k, v, memory_segments[:, None, :], segments[:, :, None])


def cross_attention_back(q, k, v, cots, segments, memory_segments):
    grid, queries, keys, seg_row, seg_col = cross_specs(q, k)
    work = q.size // HEAD_SIZE * k.shape[1]
    return pl.pallas_call(
        cross_bwd_kernel,
        grid=grid,
        in_specs=[queries, keys, keys, queries, seg_row, seg_col],
        out_specs=[queries, keys, keys],
        out_shape=[
            jax.ShapeDtypeStruct(q.shape, BF16),
            jax.ShapeDtypeStruct(k.shape, BF16),
            jax.ShapeDtypeStruct(k.shape, BF16),
        ],
        compiler_params=pltpu.CompilerParams(vmem_limit_bytes=48 << 20),
        cost_estimate=pl.CostEstimate(
            flops=work * 10 * HEAD_SIZE, transcendentals=work, bytes_accessed=q.size * 6 + k.size * 8
        ),
        name="cross_attention_back",
    )(q, k, v, cots, memory_segments[:, None, :], segments[:, :, None])


def bit_count(axis):
    return lax.axis_size(axis).bit_length() - 1


def my_bit(axis, bit):
    return (lax.axis_index(axis) >> bit) & 1


def flip(value, axis, mask):
    return lax.ppermute(value, axis, [(i, i ^ mask) for i in range(lax.axis_size(axis))])


def gather_pieces(value, axis, order):
    pieces = {0: value}
    for bit in order:
        for j in list(pieces):
            pieces[j | (1 << bit)] = flip(pieces[j], axis, 1 << bit)
    return [pieces[j] for j in range(len(pieces))]


def gather_direct(value, axis):
    return [value] + [flip(value, axis, j) for j in range(1, lax.axis_size(axis))]


def absolute(values, axis):
    place = lax.axis_index(axis)
    values = jnp.stack(values) if isinstance(values, list) else values
    return [lax.dynamic_index_in_dim(values, j ^ place, 0, False) for j in range(values.shape[0])]


def settle(*groups):
    flat, tree = jax.tree.flatten(groups)
    return jax.tree.unflatten(tree, lax.optimization_barrier(flat))


class Chain:
    def __init__(self, full, bits, order):
        shape = (2,) * len(bits) + (full.shape[0] >> len(bits),) + full.shape[1:]
        self.parts, self.left, self.order, self.flying = [full.reshape(shape)], list(bits), list(order), None

    def half(self, choice):
        where = self.left.index(self.order[0])
        return [lax.dynamic_index_in_dim(p, choice, where, False) for p in self.parts]

    def outgoing(self):
        return sum(p.astype(F32) for p in self.half(1 - my_bit(*self.order[0]))).astype(BF16)

    def launch(self, away):
        self.parts = self.half(my_bit(*self.order[0]))
        axis, bit = self.order.pop(0)
        self.left.remove((axis, bit))
        self.flying = flip(away, axis, 1 << bit)

    def land(self):
        self.parts = self.parts + [self.flying]
        self.flying = None

    def result(self):
        return sum(p.astype(F32) for p in self.parts)


def joined(chains, order):
    chain = Chain.__new__(Chain)
    chain.left, chain.order, chain.flying = list(chains[0].left), list(order), None
    chain.parts = [jnp.concatenate(parts, axis=-1) for parts in zip(*[c.parts for c in chains])]
    return chain


class Gather:
    def __init__(self, value, order, lead=0):
        self.held, self.order, self.lead, self.done, self.flying, self.last = value, list(order), lead, [], None, None

    def outgoing(self):
        return self.held

    def launch(self, value):
        self.held = value
        self.last = self.order.pop(0)
        self.flying = flip(value, self.last[0], 1 << self.last[1])

    def land(self):
        self.done = [bit for bit in place_bits() if bit in self.done or bit == self.last]
        where = self.lead + self.done.index(self.last)
        pair = jnp.arange(2).reshape((2,) + (1,) * (self.held.ndim - where))
        own, came = jnp.expand_dims(self.held, where), jnp.expand_dims(self.flying, where)
        self.held = jnp.where(pair == my_bit(*self.last), own, came)
        self.flying = None


def land(main, *chains):
    arrive = [c for c in chains if c.flying is not None]
    main, flown = settle(main, [c.flying for c in arrive])
    for chain, value in zip(arrive, flown):
        chain.flying = value
        chain.land()
    return main


def tick(main, *chains):
    main = land(main, *chains)
    depart = [c for c in chains if c.order]
    main, sends = settle(main, [c.outgoing() for c in depart])
    for chain, value in zip(depart, sends):
        chain.launch(value)
    return main


def place_bits():
    return [("batch", b) for b in reversed(range(bit_count("batch")))] + [
        ("seq", b) for b in reversed(range(bit_count("seq")))
    ]


def hops(seq_first, turned):
    seq = [("seq", b) for b in range(bit_count("seq"))]
    far = [("batch", b) for b in range(1, bit_count("batch"))]
    if turned:
        seq.reverse()
    return [("batch", 0)] + (seq + far if seq_first else far + seq)


def chain_of(full, seq_first=True, turned=False):
    return Chain(full, place_bits(), hops(seq_first, turned))


def small_sum(values):
    got = lax.all_to_all(values, ("batch", "seq"), 0, 0, tiled=True)
    return jnp.sum(got, axis=0)


def inverse_rms(values):
    return lax.rsqrt(jnp.mean(values * values, axis=-1, keepdims=True) + EPSILON)


def norm_back(values, inverse, gain, upstream):
    weighted = gain * upstream
    dot = jnp.mean(weighted * values, axis=-1, keepdims=True)
    grad = inverse * weighted - values * (inverse * inverse * inverse) * dot
    return grad, jnp.sum(upstream * values * inverse, axis=0)


def gelu_parts(v):
    scale = 0.7978845608028654
    inner = scale * (v + 0.044715 * (v * v * v))
    t = jnp.tanh(inner)
    value = 0.5 * v * (1.0 + t)
    slope = 0.5 * (1.0 + t) + 0.5 * v * (1.0 - t * t) * (scale * (1.0 + 3 * 0.044715 * (v * v)))
    return value, slope


def shards(
    tokens, memory, output_grad, segments, memory_segments, buckets,
    w_query, keyvalue_weight, w_output, w_expand, w_reduce, gains, position_bias,
    momentum_query, keyvalue_momentum, momentum_output, momentum_expand, momentum_reduce,
    momentum_gains, momentum_position,
    average_query, keyvalue_average, average_output, average_expand, average_reduce,
    average_gains, average_position,
):
    every = ("batch", "seq")
    seq_count, seq_index = lax.axis_size("seq"), lax.axis_index("seq")
    devices = lax.axis_size("batch") * seq_count
    rows, part, width = tokens.shape
    length = part * seq_count
    memory_part = memory.shape[1]
    own = w_query.shape[1]
    kv_width = keyvalue_weight.shape[3]
    heads_local = QUERY_HEADS // seq_count
    q_local, kv_local = width // seq_count, kv_width // seq_count

    wq, wkv = w_query.astype(BF16), keyvalue_weight.astype(BF16)
    wo, we, wr = w_output.astype(BF16), w_expand.astype(BF16), w_reduce.astype(BF16)
    first = jnp.concatenate(
        [
            wq[0].reshape(own, seq_count, q_local),
            wkv[0, 0].reshape(own, seq_count, kv_local),
            wkv[0, 1].reshape(own, seq_count, kv_local),
        ],
        axis=2,
    )
    cols = first.shape[2]
    bias_own = position_bias.shape[0]
    small = jnp.concatenate([gains.astype(BF16).reshape(-1), position_bias.astype(BF16)])
    small = jnp.pad(small, (0, 8 * cols - small.shape[0])).reshape(1, 8, cols)
    packet = jnp.concatenate([first.transpose(1, 0, 2), jnp.broadcast_to(small, (seq_count, 8, cols))], axis=1)
    packet = lax.all_to_all(packet, "seq", 0, 0, tiled=True)
    batch_far = [("batch", b) for b in reversed(range(1, bit_count("batch")))]
    seq_up = [("seq", b) for b in range(bit_count("seq"))]
    core = [("batch", 0)]
    gather_p = Gather(packet, batch_far + core)
    for _ in batch_far + core:
        gather_p.launch(gather_p.held)
        gather_p.land()
    orders = [[b for _, b in (seq_up if r % 2 == 0 else seq_up[::-1])] for r in range(rows)]
    first_hop = [flip(tokens[r], "seq", 1 << orders[r][0]) for r in range(rows)]
    token_pieces = []
    for r in range(rows):
        pieces = {0: tokens[r], 1 << orders[r][0]: first_hop[r]}
        for bit in orders[r][1:]:
            for j in list(pieces):
                pieces[j | (1 << bit)] = flip(pieces[j], "seq", 1 << bit)
        token_pieces.append([pieces[j] for j in range(seq_count)])
    ids = jnp.concatenate([segments, memory_segments], axis=1)
    all_ids = jnp.stack(absolute(gather_direct(ids, "seq"), "seq"), axis=1)
    all_segments = all_ids[:, :, :part].reshape(rows, length)
    all_memory_segments = all_ids[:, :, part:].reshape(rows, -1)
    packets = gather_p.held.reshape(-1, seq_count, own + 8, cols)
    w_heads = packets[:, :, :own].reshape(width, cols)
    small_rows = packets[:, :, own:].reshape(devices, -1)
    gain_values = (
        small_rows[:, : 3 * own].reshape(devices, 3, own).transpose(1, 0, 2).reshape(3, width).astype(F32)
    )
    table = small_rows[:, 3 * own : 3 * own + bias_own].reshape(NB, QUERY_HEADS).astype(F32)

    mid_a = jnp.stack([jnp.concatenate([wkv[1, 0], wkv[1, 1]], axis=1), wo[0]])
    mid_b = jnp.stack([wq[1], wo[1]])
    _, _, mid_a, mid_b = settle(packet, first_hop, mid_a, mid_b)
    gather_a = Gather(mid_a, batch_far + seq_up + core, 1)
    gather_b = Gather(mid_b, batch_far + seq_up[::-1] + core, 1)
    gather_r = Gather(wr, seq_up + batch_far + core)
    for _ in batch_far:
        for gather in (gather_a, gather_b):
            if gather.flying is not None:
                gather.land()
            gather.launch(gather.held)
    w_exp = lax.all_gather(jnp.concatenate([we[0], we[1]], axis=1), every, axis=0, tiled=True)

    reach = length // 2
    strip_width = 2 * reach + BQ
    lag = reach - jnp.arange(strip_width, dtype=jnp.int32)
    lag_ok = lag >= 0
    lag_bucket = jnp.where(lag_ok, jnp.take(buckets, jnp.clip(lag, 0, length - 1)), -1)
    picks = (lag_bucket[None, :] == jnp.arange(NB, dtype=jnp.int32)[:, None]).astype(F32)
    table_local = lax.dynamic_slice_in_dim(table, seq_index * heads_local, heads_local, 1)
    base = jnp.dot(table_local.T, picks, precision=lax.Precision.HIGHEST)
    base = jnp.where(lag_ok[None, :], base, NEGATIVE)

    token_pieces = tick(token_pieces, gather_a, gather_b, gather_r)
    all_tokens = jnp.stack([jnp.stack(p) for p in token_pieces], axis=1).astype(F32)
    all_normed = (all_tokens * inverse_rms(all_tokens) * gain_values[0]).astype(BF16).reshape(-1, width)
    head_qkv = nn(all_normed, w_heads).astype(BF16).reshape(seq_count, rows, part, cols)
    head_qkv = jnp.stack(absolute(head_qkv, "seq"), axis=1).reshape(rows, length, cols)
    head_qkv = tick(head_qkv, gather_a, gather_b)
    head_context, lse = self_attention(head_qkv, all_segments, base)
    while gather_r.order[0][0] == "seq":
        head_context = tick(head_context, gather_r)
    head_context = tick(head_context, gather_r)
    context = lax.all_to_all(head_context, "seq", split_axis=1, concat_axis=2, tiled=True).reshape(-1, width)
    while gather_a.order:
        context = tick(context, gather_a, gather_b)
    context = land(context, gather_a, gather_b)
    w_mid_a, w_mid_b = gather_a.held.reshape(2, width, width), gather_b.held.reshape(2, width, width)
    w_kv1, w_o0, w_q1, w_o1 = w_mid_a[0], w_mid_a[1], w_mid_b[0], w_mid_b[1]

    mem = memory.reshape(rows * memory_part, width)
    mkv = nn(mem, w_kv1).astype(BF16).reshape(rows, memory_part, -1)
    all_mkv = jnp.stack(absolute(gather_direct(mkv, "seq"), "seq"), axis=1).reshape(rows, -1, 2 * kv_width)
    mk, mv = all_mkv[:, :, :kv_width], all_mkv[:, :, kv_width:]
    x = tokens.astype(F32).reshape(rows * part, width)
    inv_zero = inverse_rms(x)
    hidden_one = x + nn(context, w_o0)
    inv_one = inverse_rms(hidden_one)
    normed_one = (hidden_one * inv_one * gain_values[1]).astype(BF16)
    cross_q = nn(normed_one, w_q1).astype(BF16).reshape(rows, part, width)
    while len(gather_r.order) > 1:
        cross_q = tick(cross_q, gather_r)
    cross_context = cross_attention(cross_q, mk, mv, segments, all_memory_segments)
    cross_context, first = settle(cross_context, first)
    w_first = lax.all_gather(first.reshape(own, -1), every, axis=0, tiled=True)
    cross_flat = cross_context.reshape(-1, width)
    hidden_two = hidden_one + nn(cross_flat, w_o1)
    inv_two = inverse_rms(hidden_two)
    normed_two = (hidden_two * inv_two * gain_values[2]).astype(BF16)

    ff = we.shape[2]
    normed_two = tick(normed_two, gather_r)
    gate = nn(normed_two, w_exp[:, :ff])
    up = nn(normed_two, w_exp[:, ff:])
    gelu_value, gelu_slope = gelu_parts(gate)
    activated = (gelu_value * up).astype(BF16)
    og = output_grad.reshape(rows * part, width)
    activated = land(activated, gather_r)
    w_red = gather_r.held.reshape(-1, width)
    wide_og = jnp.pad(og, ((0, 0), (0, -width % 384)))
    reduce_part = tn(activated, wide_og).astype(BF16)
    activated, reduce_part = settle(activated, reduce_part)
    (grad_reduce,) = settle(lax.psum_scatter(reduce_part, every, scatter_dimension=0, tiled=True))
    grad_reduce = grad_reduce[:, :width].astype(F32)
    result = (hidden_two + nn(activated, w_red)).astype(BF16).reshape(tokens.shape)
    activated_grad = nt(og, w_red)
    gate_grad = (activated_grad * up * gelu_slope).astype(BF16)
    up_grad = (activated_grad * gelu_value).astype(BF16)
    gate_grad, up_grad, result = settle(gate_grad, up_grad, result)
    chain_g = chain_of(tn(normed_two, gate_grad).astype(BF16))
    chain_u = chain_of(tn(normed_two, up_grad).astype(BF16), turned=True)
    gate_grad, up_grad = tick((gate_grad, up_grad), chain_g, chain_u)
    normed_two_grad = nt(gate_grad, w_exp[:, :ff]) + nt(up_grad, w_exp[:, ff:])
    part_two, gain_two = norm_back(hidden_two, inv_two, gain_values[2], normed_two_grad)
    hidden_two_grad = og.astype(F32) + part_two
    hidden_two_grad = tick(hidden_two_grad, chain_g, chain_u)

    cross_out_grad = hidden_two_grad.astype(BF16)
    cross_cots = nt(cross_out_grad, w_o1).astype(BF16).reshape(rows, part, width)
    cross_dq, mdk, mdv = cross_attention_back(cross_q, mk, mv, cross_cots, segments, all_memory_segments)
    mdkv = jnp.concatenate([mdk, mdv], axis=2).reshape(rows, seq_count, memory_part, -1)
    mdkv = lax.all_to_all(mdkv, "seq", split_axis=1, concat_axis=1, tiled=True)
    cross_dq = cross_dq.reshape(-1, width)
    part_one, gain_one = norm_back(hidden_one, inv_one, gain_values[1], nt(cross_dq, w_q1))
    hidden_one_grad = hidden_two_grad + part_one

    self_out_grad = hidden_one_grad.astype(BF16)
    cots = nt(self_out_grad, w_o0).astype(BF16).reshape(rows, part, width)
    chain_o1 = chain_of(tn(cross_flat, cross_out_grad).astype(BF16))
    chain_q1 = chain_of(tn(normed_one, cross_dq).astype(BF16))
    chain_a = joined([chain_o1, chain_q1], chain_o1.order)
    chain_o0 = chain_of(tn(context, self_out_grad).astype(BF16), turned=True)
    cots = tick(cots, chain_g, chain_u, chain_a, chain_o0)
    head_cots = lax.all_to_all(cots, "seq", split_axis=2, concat_axis=1, tiled=True)
    head_cots, mdkv = settle(head_cots, mdkv)
    mdkv = jnp.sum(mdkv.astype(F32), axis=1).astype(BF16).reshape(rows * memory_part, -1)
    memory_grad = nt(mdkv, w_kv1).reshape(memory.shape)
    chain_k1 = chain_of(tn(mem, mdkv).astype(BF16), turned=True)
    head_cots, memory_grad = tick((head_cots, memory_grad), chain_a, chain_o0, chain_k1)
    head_grads, lag_sums = self_attention_back(head_qkv, head_cots, lse, all_segments, base)
    relative = jnp.stack(absolute(head_grads.reshape(rows, seq_count, part, cols).swapaxes(0, 1), "seq"))
    batch_bits = [("batch", b) for b in reversed(range(bit_count("batch")))]
    chain_f = Chain(tn(all_normed, relative.reshape(-1, cols)).astype(BF16), batch_bits, hops(False, False)[: len(batch_bits)])
    head_grads = land(head_grads, chain_g, chain_u)
    while chain_g.order[0][0] == "seq":
        head_grads = land(tick(head_grads, chain_g, chain_u), chain_g, chain_u)
    chain_gu = joined([chain_g, chain_u], chain_g.order)
    chains = (chain_f, chain_gu, chain_a, chain_o0, chain_k1)
    head_grads, lag_sums = tick((head_grads, lag_sums), *chains)
    dqkv = lax.all_to_all(head_grads, "seq", split_axis=1, concat_axis=2, tiled=True).reshape(rows * part, -1)
    dqkv = tick(dqkv, chain_f)
    part_zero, gain_zero = norm_back(x, inv_zero, gain_values[0], nt(dqkv, w_first))
    input_grad = (hidden_one_grad + part_zero).reshape(tokens.shape)
    while any(c.order or c.flying is not None for c in chains):
        input_grad = tick(input_grad, *chains)
    grad_gu, grad_a = chain_gu.result(), chain_a.result()
    grad_o0, grad_k1 = chain_o0.result(), chain_k1.result()
    grad_gate, grad_up = grad_gu[:, :ff], grad_gu[:, ff:]
    grad_o1, grad_q1 = grad_a[:, :width], grad_a[:, width:]
    first_grads = lax.all_to_all(chain_f.result().reshape(seq_count, own, cols), "seq", 0, 0, tiled=True)
    first_grads = first_grads.transpose(1, 0, 2)

    table_part = jnp.dot(picks, lag_sums.T, precision=lax.Precision.HIGHEST)
    table_grad = lax.dynamic_update_slice(
        jnp.zeros((NB, QUERY_HEADS), F32), table_part, (0, seq_index * heads_local)
    ).reshape(devices, -1)
    gains_grad = jnp.stack([gain_zero, gain_one, gain_two]).reshape(3, devices, own)
    gains_grad = gains_grad.transpose(1, 0, 2).reshape(devices, -1)
    small_grads = small_sum(jnp.concatenate([gains_grad, table_grad], axis=1))
    shard_gains = small_grads[: 3 * own].reshape(3, own)
    shard_table = small_grads[3 * own :]

    shard_query = jnp.stack([first_grads[:, :, :q_local].reshape(own, width), grad_q1])
    shard_keyval = jnp.stack(
        [
            jnp.stack(
                [
                    first_grads[:, :, q_local : q_local + kv_local].reshape(own, kv_width),
                    first_grads[:, :, q_local + kv_local :].reshape(own, kv_width),
                ]
            ),
            jnp.stack([grad_k1[:, :kv_width], grad_k1[:, kv_width:]]),
        ]
    )
    gradients = (
        shard_query,
        shard_keyval,
        jnp.stack([grad_o0, grad_o1]),
        jnp.stack([grad_gate, grad_up]),
        grad_reduce,
        shard_gains,
        shard_table,
    )
    token_scale = (rows * part * devices) ** (-0.5)
    masters = (w_query, keyvalue_weight, w_output, w_expand, w_reduce, gains, position_bias)
    momenta = (
        momentum_query, keyvalue_momentum, momentum_output, momentum_expand, momentum_reduce,
        momentum_gains, momentum_position,
    )
    averages = (
        average_query, keyvalue_average, average_output, average_expand, average_reduce,
        average_gains, average_position,
    )
    renewals, states = [], []
    for gradient, master, momentum, average, step_rate in zip(gradients, masters, momenta, averages, STEP_RATES):
        renewed = MOMENTUM * momentum + gradient
        weight = master - step_rate * token_scale * (gradient + MOMENTUM * renewed)
        renewals.append(renewed)
        states.append(jnp.stack([weight, AVERAGE * average + (1.0 - AVERAGE) * weight]))
    return (result, input_grad, memory_grad.astype(F32), *gradients, *renewals, *states)


def solution(mesh):
    every = ("batch", "seq")
    params = (
        P(None, every, None),
        P(None, None, every, None),
        P(None, every, None),
        P(None, every, None),
        P(every, None),
        P(None, every),
        P(every),
    )
    stacked_params = (
        P(None, None, every, None),
        P(None, None, None, every, None),
        P(None, None, every, None),
        P(None, None, every, None),
        P(None, every, None),
        P(None, None, every),
        P(None, every),
    )
    acts = P("batch", "seq", None)
    return jax.shard_map(
        shards,
        mesh=mesh,
        in_specs=(acts, acts, acts, P("batch", "seq"), P("batch", "seq"), P(), *params, *params, *params),
        out_specs=(acts, acts, acts, *params, *params, *stacked_params),
        check_vma=False,
    )
```

```python
import functools

import jax
import jax.numpy as jnp
from jax import lax
from jax.experimental import pallas as pl
from jax.experimental.pallas import tpu as pltpu
from jax.sharding import PartitionSpec as P

HEAD_SIZE = 64
QUERY_HEADS = 16
NB = 32
EPSILON = 1e-06
NEGATIVE = -1e30
MOMENTUM = 0.9
AVERAGE = 0.99
STEP_RATES = (0.0015, 0.03, 0.3, 0.04, 0.015, 0.1, 1.0)
BF16 = jnp.bfloat16
F32 = jnp.float32
BQ = 128
FF_BLOCK = 256


def nt(a, b):
    return lax.dot_general(a, b, (((1,), (1,)), ((), ())), preferred_element_type=F32)


def nn(a, b):
    return lax.dot_general(a, b, (((1,), (0,)), ((), ())), preferred_element_type=F32)


def tn(a, b):
    return lax.dot_general(a, b, (((0,), (0,)), ((), ())), preferred_element_type=F32)


def stacked(block, group, per):
    first = group * per
    return jnp.concatenate(
        [block[:, (first + c) * HEAD_SIZE : (first + c + 1) * HEAD_SIZE] for c in range(per)], axis=0
    )


def lanes(block, index):
    return block[:, index * HEAD_SIZE : (index + 1) * HEAD_SIZE]


def skew(held, back):
    count, width = held.shape
    rows = lax.broadcasted_iota(jnp.int32, (count, width), 0)
    amount = 1
    while amount < count:
        turned = pltpu.roll(held, width - amount if back else amount, 1)
        held = jnp.where((rows & amount) != 0, turned, held)
        amount *= 2
    return held


def make_strips(base_ref, strip_ref):
    heads, rows, width = strip_ref.shape
    for h in range(heads):
        strip_ref[h] = skew(jnp.broadcast_to(base_ref[h : h + 1, :], (rows, width)), False)


def windows(length):
    reach = length // 2
    for step in range(length // BQ):
        here = slice(step * BQ, (step + 1) * BQ)
        start = max(step * BQ - reach, 0)
        lead = reach - (step * BQ - start)
        yield here, slice(start, (step + 1) * BQ), slice(lead, lead + (step + 1) * BQ - start)


def head_layout(heads, width):
    q_width = heads * HEAD_SIZE
    k_width = (width - q_width) // 2
    return slice(0, q_width), slice(q_width, q_width + k_width), slice(q_width + k_width, width), k_width // HEAD_SIZE


def self_fwd_kernel(qkv_ref, seg_row_ref, seg_col_ref, base_ref, o_ref, lse_ref, strip_ref):
    heads = strip_ref.shape[0]
    in_q, in_k, in_v, groups = head_layout(heads, qkv_ref.shape[2])
    per = heads // groups

    @pl.when(pl.program_id(0) == 0)
    def _():
        make_strips(base_ref, strip_ref)

    for here, seen, strip in windows(qkv_ref.shape[1]):
        same = seg_col_ref[0, here, :] == seg_row_ref[0, :, seen]
        block, keys, values = qkv_ref[0, here, in_q], qkv_ref[0, seen, in_k], qkv_ref[0, seen, in_v]
        outs, sums = [], []
        for g in range(groups):
            scores = nt(stacked(block, g, per), lanes(keys, g))
            probs = []
            for c in range(per):
                bias = strip_ref[g * per + c, :, strip]
                s = jnp.where(same, scores[c * BQ : (c + 1) * BQ] + bias, NEGATIVE)
                top = jnp.max(s, axis=-1, keepdims=True)
                e = jnp.exp(s - top)
                total = jnp.sum(e, axis=-1, keepdims=True)
                probs.append((e * (1.0 / total)).astype(BF16))
                sums.append(top + jnp.log(total))
            ctx = nn(jnp.concatenate(probs, axis=0), lanes(values, g)).astype(BF16)
            outs += [ctx[c * BQ : (c + 1) * BQ] for c in range(per)]
        o_ref[0, here, :] = jnp.concatenate(outs, axis=1)
        lse_ref[0, here, :] = jnp.concatenate(sums, axis=1)


def self_bwd_kernel(
    qkv_ref, c_ref, lse_ref, seg_row_ref, seg_col_ref, base_ref,
    d_ref, lag_ref, strip_ref, grad_ref, dk_acc, dv_acc,
):
    heads = strip_ref.shape[0]
    in_q, in_k, in_v, groups = head_layout(heads, qkv_ref.shape[2])
    per = heads // groups

    @pl.when(pl.program_id(0) == 0)
    def _():
        make_strips(base_ref, strip_ref)
        grad_ref[...] = jnp.zeros_like(grad_ref)

    dk_acc[...] = jnp.zeros_like(dk_acc)
    dv_acc[...] = jnp.zeros_like(dv_acc)
    for here, seen, strip in windows(qkv_ref.shape[1]):
        same = seg_col_ref[0, here, :] == seg_row_ref[0, :, seen]
        block, keys, values = qkv_ref[0, here, in_q], qkv_ref[0, seen, in_k], qkv_ref[0, seen, in_v]
        cots, lse = c_ref[0, here, :], lse_ref[0, here, :]
        outs = []
        for g in range(groups):
            q2, c2 = stacked(block, g, per), stacked(cots, g, per)
            scores = nt(q2, lanes(keys, g))
            dprobs = nt(c2, lanes(values, g))
            probs, dscores = [], []
            for c in range(per):
                h = g * per + c
                bias = strip_ref[h, :, strip]
                s = jnp.where(same, scores[c * BQ : (c + 1) * BQ] + bias, NEGATIVE)
                p = jnp.exp(s - lse[:, h : h + 1])
                dp = dprobs[c * BQ : (c + 1) * BQ]
                ds = (p * (dp - jnp.sum(p * dp, axis=-1, keepdims=True))).astype(BF16)
                grad_ref[h, :, strip] += ds.astype(F32)
                probs.append(p.astype(BF16))
                dscores.append(ds)
            p2, ds2 = jnp.concatenate(probs, axis=0), jnp.concatenate(dscores, axis=0)
            dq2 = nn(ds2, lanes(keys, g)).astype(BF16)
            outs += [dq2[c * BQ : (c + 1) * BQ] for c in range(per)]
            mine = slice(g * HEAD_SIZE, (g + 1) * HEAD_SIZE)
            dk_acc[mine, seen] += tn(q2, ds2)
            dv_acc[mine, seen] += tn(c2, p2)
        d_ref[0, here, in_q] = jnp.concatenate(outs, axis=1)
    d_ref[0, :, in_k] = dk_acc[...].T.astype(BF16)
    d_ref[0, :, in_v] = dv_acc[...].T.astype(BF16)

    @pl.when(pl.program_id(0) == pl.num_programs(0) - 1)
    def _():
        for h in range(heads):
            lag_ref[h : h + 1, :] = jnp.sum(skew(grad_ref[h], True), axis=0, keepdims=True)


def self_specs(length, width, heads, strip_width):
    qkv = pl.BlockSpec((1, length, width), lambda r: (r, 0, 0))
    queries = pl.BlockSpec((1, length, heads * HEAD_SIZE), lambda r: (r, 0, 0))
    sums = pl.BlockSpec((1, length, heads), lambda r: (r, 0, 0))
    seg_row = pl.BlockSpec((1, 1, length), lambda r: (r, 0, 0))
    seg_col = pl.BlockSpec((1, length, 1), lambda r: (r, 0, 0))
    base = pl.BlockSpec((heads, strip_width), lambda r: (0, 0))
    return qkv, queries, sums, seg_row, seg_col, base


def self_attention(qkv, segments, base):
    rows, length, width = qkv.shape
    heads, strip_width = base.shape
    all_spec, queries, sums, seg_row, seg_col, base_spec = self_specs(length, width, heads, strip_width)
    work = rows * heads * length * length * 3 // 8
    return pl.pallas_call(
        self_fwd_kernel,
        grid=(rows,),
        in_specs=[all_spec, seg_row, seg_col, base_spec],
        out_specs=[queries, sums],
        out_shape=[
            jax.ShapeDtypeStruct((rows, length, heads * HEAD_SIZE), BF16),
            jax.ShapeDtypeStruct((rows, length, heads), F32),
        ],
        scratch_shapes=[pltpu.VMEM((heads, BQ, strip_width), F32)],
        compiler_params=pltpu.CompilerParams(vmem_limit_bytes=48 << 20),
        cost_estimate=pl.CostEstimate(
            flops=work * 4 * HEAD_SIZE, transcendentals=work, bytes_accessed=qkv.size * 4
        ),
        name="self_attention",
    )(qkv, segments[:, None, :], segments[:, :, None], base)


def self_attention_back(qkv, cots, lse, segments, base):
    rows, length, width = qkv.shape
    heads, strip_width = base.shape
    all_spec, queries, sums, seg_row, seg_col, base_spec = self_specs(length, width, heads, strip_width)
    k_width = (width - heads * HEAD_SIZE) // 2
    work = rows * heads * length * length * 3 // 8
    return pl.pallas_call(
        self_bwd_kernel,
        grid=(rows,),
        in_specs=[all_spec, queries, sums, seg_row, seg_col, base_spec],
        out_specs=[all_spec, base_spec],
        out_shape=[
            jax.ShapeDtypeStruct(qkv.shape, BF16),
            jax.ShapeDtypeStruct((heads, strip_width), F32),
        ],
        scratch_shapes=[
            pltpu.VMEM((heads, BQ, strip_width), F32),
            pltpu.VMEM((heads, BQ, strip_width), F32),
            pltpu.VMEM((k_width, length), F32),
            pltpu.VMEM((k_width, length), F32),
        ],
        compiler_params=pltpu.CompilerParams(vmem_limit_bytes=48 << 20),
        cost_estimate=pl.CostEstimate(
            flops=work * 10 * HEAD_SIZE, transcendentals=work, bytes_accessed=qkv.size * 6
        ),
        name="self_attention_back",
    )(qkv, cots, lse, segments[:, None, :], segments[:, :, None], base)


def cross_fwd_kernel(q_ref, k_ref, v_ref, seg_row_ref, seg_col_ref, o_ref, *lse_refs):
    block, keys, values = q_ref[0], k_ref[0], v_ref[0]
    count = block.shape[0]
    groups = keys.shape[1] // HEAD_SIZE
    per = block.shape[1] // keys.shape[1]
    same = seg_col_ref[0] == seg_row_ref[0]
    outs = []
    for g in range(groups):
        scores = nt(stacked(block, g, per), lanes(keys, g))
        probs = []
        for c in range(per):
            s = jnp.where(same, scores[c * count : (c + 1) * count], NEGATIVE)
            top = jnp.max(s, axis=-1, keepdims=True)
            e = jnp.exp(s - top)
            total = jnp.sum(e, axis=-1, keepdims=True)
            probs.append((e * (1.0 / total)).astype(BF16))
        ctx = nn(jnp.concatenate(probs, axis=0), lanes(values, g)).astype(BF16)
        outs += [ctx[c * count : (c + 1) * count] for c in range(per)]
    o_ref[0] = jnp.concatenate(outs, axis=1)


def cross_bwd_kernel(q_ref, k_ref, v_ref, c_ref, seg_row_ref, seg_col_ref, dq_ref, dk_ref, dv_ref):
    block, keys, values, cots = q_ref[0], k_ref[0], v_ref[0], c_ref[0]
    count = block.shape[0]
    groups = keys.shape[1] // HEAD_SIZE
    per = block.shape[1] // keys.shape[1]
    same = seg_col_ref[0] == seg_row_ref[0]
    outs, dkeys, dvalues = [], [], []
    for g in range(groups):
        q2, c2 = stacked(block, g, per), stacked(cots, g, per)
        scores = nt(q2, lanes(keys, g))
        dprobs = nt(c2, lanes(values, g))
        probs, dscores = [], []
        for c in range(per):
            s = jnp.where(same, scores[c * count : (c + 1) * count], NEGATIVE)
            top = jnp.max(s, axis=-1, keepdims=True)
            e = jnp.exp(s - top)
            p = e * (1.0 / jnp.sum(e, axis=-1, keepdims=True))
            dp = dprobs[c * count : (c + 1) * count]
            dscores.append((p * (dp - jnp.sum(p * dp, axis=-1, keepdims=True))).astype(BF16))
            probs.append(p.astype(BF16))
        p2, ds2 = jnp.concatenate(probs, axis=0), jnp.concatenate(dscores, axis=0)
        dq2 = nn(ds2, lanes(keys, g)).astype(BF16)
        outs += [dq2[c * count : (c + 1) * count] for c in range(per)]
        dkeys.append(tn(q2, ds2))
        dvalues.append(tn(c2, p2))
    dq_ref[0] = jnp.concatenate(outs, axis=1)
    dk_ref[0] = jnp.concatenate(dkeys, axis=0).T.astype(dk_ref.dtype)
    dv_ref[0] = jnp.concatenate(dvalues, axis=0).T.astype(dv_ref.dtype)


def cross_specs(q, k):
    rows, count, q_width = q.shape
    memory, k_width = k.shape[1:]
    step = 2 * HEAD_SIZE
    q_step = step * (q_width // k_width)
    queries = pl.BlockSpec((1, count, q_step), lambda r, g: (r, 0, g))
    keys = pl.BlockSpec((1, memory, step), lambda r, g: (r, 0, g))
    seg_row = pl.BlockSpec((1, 1, memory), lambda r, g: (r, 0, 0))
    seg_col = pl.BlockSpec((1, count, 1), lambda r, g: (r, 0, 0))
    return (rows, k_width // step), queries, keys, seg_row, seg_col


def cross_attention(q, k, v, segments, memory_segments):
    grid, queries, keys, seg_row, seg_col = cross_specs(q, k)
    work = q.size // HEAD_SIZE * k.shape[1]
    return pl.pallas_call(
        cross_fwd_kernel,
        grid=grid,
        in_specs=[queries, keys, keys, seg_row, seg_col],
        out_specs=queries,
        out_shape=jax.ShapeDtypeStruct(q.shape, BF16),
        compiler_params=pltpu.CompilerParams(vmem_limit_bytes=48 << 20),
        cost_estimate=pl.CostEstimate(
            flops=work * 4 * HEAD_SIZE, transcendentals=work, bytes_accessed=q.size * 4 + k.size * 4
        ),
        name="cross_attention",
    )(q, k, v, memory_segments[:, None, :], segments[:, :, None])


def cross_attention_back(q, k, v, cots, segments, memory_segments):
    grid, queries, keys, seg_row, seg_col = cross_specs(q, k)
    work = q.size // HEAD_SIZE * k.shape[1]
    return pl.pallas_call(
        cross_bwd_kernel,
        grid=grid,
        in_specs=[queries, keys, keys, queries, seg_row, seg_col],
        out_specs=[queries, keys, keys],
        out_shape=[
            jax.ShapeDtypeStruct(q.shape, BF16),
            jax.ShapeDtypeStruct(k.shape, BF16),
            jax.ShapeDtypeStruct(k.shape, BF16),
        ],
        compiler_params=pltpu.CompilerParams(vmem_limit_bytes=48 << 20),
        cost_estimate=pl.CostEstimate(
            flops=work * 10 * HEAD_SIZE, transcendentals=work, bytes_accessed=q.size * 6 + k.size * 8
        ),
        name="cross_attention_back",
    )(q, k, v, cots, memory_segments[:, None, :], segments[:, :, None])


def bit_count(axis):
    return lax.axis_size(axis).bit_length() - 1


def my_bit(axis, bit):
    return (lax.axis_index(axis) >> bit) & 1


def flip(value, axis, mask):
    return lax.ppermute(value, axis, [(i, i ^ mask) for i in range(lax.axis_size(axis))])


def gather_pieces(value, axis, order):
    pieces = {0: value}
    for bit in order:
        for j in list(pieces):
            pieces[j | (1 << bit)] = flip(pieces[j], axis, 1 << bit)
    return [pieces[j] for j in range(len(pieces))]


def gather_direct(value, axis):
    return [value] + [flip(value, axis, j) for j in range(1, lax.axis_size(axis))]


def absolute(values, axis):
    place = lax.axis_index(axis)
    values = jnp.stack(values) if isinstance(values, list) else values
    return [lax.dynamic_index_in_dim(values, j ^ place, 0, False) for j in range(values.shape[0])]


def settle(*groups):
    flat, tree = jax.tree.flatten(groups)
    return jax.tree.unflatten(tree, lax.optimization_barrier(flat))


class Chain:
    def __init__(self, full, bits, order):
        shape = (2,) * len(bits) + (full.shape[0] >> len(bits),) + full.shape[1:]
        self.parts, self.left, self.order, self.flying = [full.reshape(shape)], list(bits), list(order), None

    def half(self, choice):
        where = self.left.index(self.order[0])
        return [lax.dynamic_index_in_dim(p, choice, where, False) for p in self.parts]

    def outgoing(self):
        return sum(p.astype(F32) for p in self.half(1 - my_bit(*self.order[0]))).astype(BF16)

    def launch(self, away):
        self.parts = self.half(my_bit(*self.order[0]))
        axis, bit = self.order.pop(0)
        self.left.remove((axis, bit))
        self.flying = flip(away, axis, 1 << bit)

    def land(self):
        self.parts = self.parts + [self.flying]
        self.flying = None

    def finish(self):
        if self.flying is not None:
            self.land()
        while self.order:
            self.launch(self.outgoing())
            self.land()

    def result(self):
        return sum(p.astype(F32) for p in self.parts)


def joined(chains, order):
    chain = Chain.__new__(Chain)
    chain.left, chain.order, chain.flying = list(chains[0].left), list(order), None
    chain.parts = [jnp.concatenate(parts, axis=-1) for parts in zip(*[c.parts for c in chains])]
    return chain


class Gather:
    def __init__(self, value, order, lead=0):
        self.held, self.order, self.lead, self.done, self.flying, self.last = value, list(order), lead, [], None, None

    def outgoing(self):
        return self.held

    def launch(self, value):
        self.held = value
        self.last = self.order.pop(0)
        self.flying = flip(value, self.last[0], 1 << self.last[1])

    def land(self):
        self.done = [bit for bit in place_bits() if bit in self.done or bit == self.last]
        where = self.lead + self.done.index(self.last)
        pair = jnp.arange(2).reshape((2,) + (1,) * (self.held.ndim - where))
        own, came = jnp.expand_dims(self.held, where), jnp.expand_dims(self.flying, where)
        self.held = jnp.where(pair == my_bit(*self.last), own, came)
        self.flying = None


def land(main, *chains):
    arrive = [c for c in chains if c.flying is not None]
    main, flown = settle(main, [c.flying for c in arrive])
    for chain, value in zip(arrive, flown):
        chain.flying = value
        chain.land()
    return main


def tick(main, *chains):
    main = land(main, *chains)
    depart = [c for c in chains if c.order]
    main, sends = settle(main, [c.outgoing() for c in depart])
    for chain, value in zip(depart, sends):
        chain.launch(value)
    return main


def place_bits():
    return [("batch", b) for b in reversed(range(bit_count("batch")))] + [
        ("seq", b) for b in reversed(range(bit_count("seq")))
    ]


def hops(seq_first, turned):
    seq = [("seq", b) for b in range(bit_count("seq"))]
    far = [("batch", b) for b in range(1, bit_count("batch"))]
    if turned:
        seq.reverse()
    return [("batch", 0)] + (seq + far if seq_first else far + seq)


def chain_of(full, seq_first=True, turned=False):
    return Chain(full, place_bits(), hops(seq_first, turned))


def chain_of_halves(away, kept, seq_first=True, turned=False):
    chain = Chain(kept, [b for b in place_bits() if b != ("batch", 0)], hops(seq_first, turned)[1:])
    chain.flying = flip(away, "batch", 1).reshape(chain.parts[0].shape)
    return chain


def small_sum(values):
    got = lax.all_to_all(values, ("batch", "seq"), 0, 0, tiled=True)
    return jnp.sum(got, axis=0)


def inverse_rms(values):
    return lax.rsqrt(jnp.mean(values * values, axis=-1, keepdims=True) + EPSILON)


def norm_back(values, inverse, gain, upstream):
    weighted = gain * upstream
    dot = jnp.mean(weighted * values, axis=-1, keepdims=True)
    grad = inverse * weighted - values * (inverse * inverse * inverse) * dot
    return grad, jnp.sum(upstream * values * inverse, axis=0)


def gelu_parts(v):
    scale = 0.7978845608028654
    inner = scale * (v + 0.044715 * (v * v * v))
    t = jnp.tanh(inner)
    value = 0.5 * v * (1.0 + t)
    slope = 0.5 * (1.0 + t) + 0.5 * v * (1.0 - t * t) * (scale * (1.0 + 3 * 0.044715 * (v * v)))
    return value, slope


def hidden_rows(x, core_rows):
    turned = x.T
    blocks = [turned[i : i + core_rows] for i in range(0, turned.shape[0], core_rows)]
    return jnp.concatenate(blocks[0::2], axis=0), jnp.concatenate(blocks[1::2], axis=0)


def ffn_kernel(
    core_ref, h_ref, gain_ref, og_ref, wg_ref, wu_ref, wr_ref,
    out_ref, hgrad_ref, gain_grad_ref, dg_away_ref, dg_ref, du_away_ref, du_ref, dr_ref,
    x_ref, xt_ref, res_ref, back_ref, *, core_rows,
):
    half = dg_ref.shape[0]
    step = pl.program_id(0)

    @pl.when(step == 0)
    def _():
        hidden = h_ref[...]
        x = (hidden * inverse_rms(hidden) * gain_ref[...]).astype(BF16)
        x_ref[...] = x
        flipped = hidden_rows(x, core_rows)
        first_core = core_ref[0] == 0
        xt_ref[:half] = jnp.where(first_core, flipped[1], flipped[0])
        xt_ref[half:] = jnp.where(first_core, flipped[0], flipped[1])
        res_ref[...] = jnp.zeros_like(res_ref)
        back_ref[...] = jnp.zeros_like(back_ref)

    x, og = x_ref[...], og_ref[...]
    wg, wu, wr = wg_ref[...], wu_ref[...], wr_ref[...]
    gelu_value, gelu_slope = gelu_parts(nn(x, wg))
    up = nn(x, wu)
    activated = (gelu_value * up).astype(BF16)
    upstream = nt(og, wr)
    gate_grad = (upstream * up * gelu_slope).astype(BF16)
    up_grad = (upstream * gelu_value).astype(BF16)
    res_ref[...] += nn(activated, wr)
    back_ref[...] += nt(gate_grad, wg) + nt(up_grad, wu)
    dr_ref[...] = tn(activated, og).astype(BF16)
    xt = xt_ref[...]
    gate_product, up_product = nn(xt, gate_grad).astype(BF16), nn(xt, up_grad).astype(BF16)
    dg_away_ref[...], dg_ref[...] = gate_product[:half], gate_product[half:]
    du_away_ref[...], du_ref[...] = up_product[:half], up_product[half:]

    @pl.when(step == pl.num_programs(0) - 1)
    def _():
        hidden = h_ref[...]
        out_ref[...] = (hidden + res_ref[...]).astype(BF16)
        inverse = inverse_rms(hidden)
        upward = back_ref[...]
        weighted = gain_ref[...] * upward
        dot = jnp.mean(weighted * hidden, axis=-1, keepdims=True)
        part = inverse * weighted - hidden * (inverse * inverse * inverse) * dot
        hgrad_ref[...] = og_ref[...].astype(F32) + part
        gain_grad_ref[...] = jnp.sum(upward * hidden * inverse, axis=0, keepdims=True)


def feed_forward(hidden, gain, og, w_rest, w_red, ff_first):
    count, width = hidden.shape
    ff = w_red.shape[0]
    steps, gate_first = ff // FF_BLOCK, ff_first // FF_BLOCK
    whole = pl.BlockSpec((count, width), lambda j: (0, 0))
    row = pl.BlockSpec((1, width), lambda j: (0, 0))
    down = pl.BlockSpec((FF_BLOCK, width), lambda j: (j, 0))
    cols = pl.BlockSpec((width // 2, FF_BLOCK), lambda j: (0, j))
    core_rows = width // lax.axis_size("batch")
    return pl.pallas_call(
        functools.partial(ffn_kernel, core_rows=core_rows),
        grid=(steps,),
        in_specs=[
            pl.BlockSpec(memory_space=pltpu.SMEM),
            whole, row, whole,
            pl.BlockSpec((width, FF_BLOCK), lambda j: (0, j + gate_first)),
            pl.BlockSpec((width, FF_BLOCK), lambda j: (0, j + gate_first + steps)),
            down,
        ],
        out_specs=[whole, whole, row, cols, cols, cols, cols, down],
        out_shape=[
            jax.ShapeDtypeStruct((count, width), BF16),
            jax.ShapeDtypeStruct((count, width), F32),
            jax.ShapeDtypeStruct((1, width), F32),
            *[jax.ShapeDtypeStruct((width // 2, ff), BF16)] * 4,
            jax.ShapeDtypeStruct((ff, width), BF16),
        ],
        scratch_shapes=[
            pltpu.VMEM((count, width), BF16),
            pltpu.VMEM((width, count), BF16),
            pltpu.VMEM((count, width), F32),
            pltpu.VMEM((count, width), F32),
        ],
        compiler_params=pltpu.CompilerParams(vmem_limit_bytes=56 << 20),
        cost_estimate=pl.CostEstimate(
            flops=18 * count * width * ff, transcendentals=count * ff, bytes_accessed=12 * width * ff
        ),
        name="feed_forward",
    )(my_bit("batch", 0).reshape(1).astype(jnp.int32), hidden, gain, og, w_rest, w_rest, w_red)


def shards(
    tokens, memory, output_grad, segments, memory_segments, buckets,
    w_query, keyvalue_weight, w_output, w_expand, w_reduce, gains, position_bias,
    momentum_query, keyvalue_momentum, momentum_output, momentum_expand, momentum_reduce,
    momentum_gains, momentum_position,
    average_query, keyvalue_average, average_output, average_expand, average_reduce,
    average_gains, average_position,
):
    every = ("batch", "seq")
    seq_count, seq_index = lax.axis_size("seq"), lax.axis_index("seq")
    devices = lax.axis_size("batch") * seq_count
    rows, part, width = tokens.shape
    length = part * seq_count
    memory_part = memory.shape[1]
    own = w_query.shape[1]
    kv_width = keyvalue_weight.shape[3]
    heads_local = QUERY_HEADS // seq_count
    q_local, kv_local = width // seq_count, kv_width // seq_count

    wq, wkv = w_query.astype(BF16), keyvalue_weight.astype(BF16)
    wo, we, wr = w_output.astype(BF16), w_expand.astype(BF16), w_reduce.astype(BF16)
    first = jnp.concatenate(
        [
            wq[0].reshape(own, seq_count, q_local),
            wkv[0, 0].reshape(own, seq_count, kv_local),
            wkv[0, 1].reshape(own, seq_count, kv_local),
        ],
        axis=2,
    )
    cols = first.shape[2]
    bias_own = position_bias.shape[0]
    small = jnp.concatenate([gains.astype(BF16).reshape(-1), position_bias.astype(BF16)])
    small = jnp.pad(small, (0, 8 * cols - small.shape[0])).reshape(1, 8, cols)
    packet = jnp.concatenate([first.transpose(1, 0, 2), jnp.broadcast_to(small, (seq_count, 8, cols))], axis=1)
    packet = lax.all_to_all(packet, "seq", 0, 0, tiled=True)
    batch_far = [("batch", b) for b in reversed(range(1, bit_count("batch")))]
    seq_up = [("seq", b) for b in range(bit_count("seq"))]
    core = [("batch", 0)]
    gather_p = Gather(packet, batch_far + core)
    for _ in batch_far + core:
        gather_p.launch(gather_p.held)
        gather_p.land()
    orders = [[b for _, b in (seq_up if r % 2 == 0 else seq_up[::-1])] for r in range(rows)]
    first_hop = [flip(tokens[r], "seq", 1 << orders[r][0]) for r in range(rows)]
    token_pieces = []
    for r in range(rows):
        pieces = {0: tokens[r], 1 << orders[r][0]: first_hop[r]}
        for bit in orders[r][1:]:
            for j in list(pieces):
                pieces[j | (1 << bit)] = flip(pieces[j], "seq", 1 << bit)
        token_pieces.append([pieces[j] for j in range(seq_count)])
    ids = jnp.concatenate([segments, memory_segments], axis=1)
    all_ids = jnp.stack(absolute(gather_direct(ids, "seq"), "seq"), axis=1)
    all_segments = all_ids[:, :, :part].reshape(rows, length)
    all_memory_segments = all_ids[:, :, part:].reshape(rows, -1)
    packets = gather_p.held.reshape(-1, seq_count, own + 8, cols)
    w_heads = packets[:, :, :own].reshape(width, cols)
    small_rows = packets[:, :, own:].reshape(devices, -1)
    gain_values = (
        small_rows[:, : 3 * own].reshape(devices, 3, own).transpose(1, 0, 2).reshape(3, width).astype(F32)
    )
    table = small_rows[:, 3 * own : 3 * own + bias_own].reshape(NB, QUERY_HEADS).astype(F32)

    ff, ff_own = we.shape[2], wr.shape[0]
    folds = -(-ff_own // own)
    wr_rows = jnp.pad(wr, ((0, folds * own - ff_own), (0, 0))).reshape(folds, own, width)
    pieces = [wkv[1, 0], wkv[1, 1], wo[0], wq[1], wo[1], we[0], we[1], *[wr_rows[i] for i in range(folds)]]
    w_rest = lax.all_gather(jnp.concatenate(pieces, axis=1), every, axis=0, tiled=True)
    w_kv1, w_o0, w_q1, w_o1 = (w_rest[:, i * width : (i + 1) * width] for i in range(4))
    ff_first = 4 * width
    down_first = ff_first + 2 * ff
    w_red = jnp.concatenate(
        [
            w_rest[:, down_first + i * width : down_first + (i + 1) * width].reshape(devices, own, width)
            for i in range(folds)
        ],
        axis=1,
    )[:, :ff_own].reshape(ff, width)

    reach = length // 2
    strip_width = 2 * reach + BQ
    lag = reach - jnp.arange(strip_width, dtype=jnp.int32)
    lag_ok = lag >= 0
    lag_bucket = jnp.where(lag_ok, jnp.take(buckets, jnp.clip(lag, 0, length - 1)), -1)
    picks = (lag_bucket[None, :] == jnp.arange(NB, dtype=jnp.int32)[:, None]).astype(F32)
    table_local = lax.dynamic_slice_in_dim(table, seq_index * heads_local, heads_local, 1)
    base = jnp.dot(table_local.T, picks, precision=lax.Precision.HIGHEST)
    base = jnp.where(lag_ok[None, :], base, NEGATIVE)

    all_tokens = jnp.stack([jnp.stack(p) for p in token_pieces], axis=1).astype(F32)
    all_normed = (all_tokens * inverse_rms(all_tokens) * gain_values[0]).astype(BF16).reshape(-1, width)
    head_qkv = nn(all_normed, w_heads).astype(BF16).reshape(seq_count, rows, part, cols)
    head_qkv = jnp.stack(absolute(head_qkv, "seq"), axis=1).reshape(rows, length, cols)
    head_context, lse = self_attention(head_qkv, all_segments, base)
    context = lax.all_to_all(head_context, "seq", split_axis=1, concat_axis=2, tiled=True).reshape(-1, width)

    mem = memory.reshape(rows * memory_part, width)
    mkv = nn(mem, w_kv1).astype(BF16).reshape(rows, memory_part, -1)
    all_mkv = jnp.stack(absolute(gather_direct(mkv, "seq"), "seq"), axis=1).reshape(rows, -1, 2 * kv_width)
    mk, mv = all_mkv[:, :, :kv_width], all_mkv[:, :, kv_width:]
    x = tokens.astype(F32).reshape(rows * part, width)
    inv_zero = inverse_rms(x)
    hidden_one = x + nn(context, w_o0)
    inv_one = inverse_rms(hidden_one)
    normed_one = (hidden_one * inv_one * gain_values[1]).astype(BF16)
    cross_q = nn(normed_one, w_q1).astype(BF16).reshape(rows, part, width)
    cross_context = cross_attention(cross_q, mk, mv, segments, all_memory_segments)
    cross_flat = cross_context.reshape(-1, width)
    hidden_two = hidden_one + nn(cross_flat, w_o1)
    hidden_two, w_red, w_heads = settle(hidden_two, w_red, w_heads)
    w_first = jnp.concatenate(gather_direct(w_heads, "seq"), axis=1)
    og = output_grad.reshape(rows * part, width)
    result, hidden_two_grad, gain_two, *part_gu, part_reduce = feed_forward(
        hidden_two, gain_values[2:3], og, w_rest, w_red, ff_first
    )
    result, gain_two = result.reshape(tokens.shape), gain_two[0]
    chain_g = chain_of_halves(part_gu[0], part_gu[1])
    chain_u = chain_of_halves(part_gu[2], part_gu[3], turned=True)
    chain_r = chain_of(part_reduce, seq_first=False)
    hidden_two_grad, w_first = tick((hidden_two_grad, w_first), chain_r)

    cross_out_grad = hidden_two_grad.astype(BF16)
    cross_cots = nt(cross_out_grad, w_o1).astype(BF16).reshape(rows, part, width)
    cross_cots = tick(cross_cots, chain_r, chain_g, chain_u)
    cross_dq, mdk, mdv = cross_attention_back(cross_q, mk, mv, cross_cots, segments, all_memory_segments)
    mdkv = jnp.concatenate([mdk, mdv], axis=2).reshape(rows, seq_count, memory_part, -1)
    mdkv = absolute(mdkv.swapaxes(0, 1), "seq")
    mdkv = [mdkv[0]] + [flip(mdkv[j], "seq", j) for j in range(1, seq_count)]
    cross_dq = cross_dq.reshape(-1, width)
    part_one, gain_one = norm_back(hidden_one, inv_one, gain_values[1], nt(cross_dq, w_q1))
    hidden_one_grad = hidden_two_grad + part_one

    self_out_grad = hidden_one_grad.astype(BF16)
    cots = nt(self_out_grad, w_o0).astype(BF16).reshape(rows, part, width)
    chain_o1 = chain_of(tn(cross_flat, cross_out_grad).astype(BF16))
    chain_q1 = chain_of(tn(normed_one, cross_dq).astype(BF16))
    chain_a = joined([chain_o1, chain_q1], chain_o1.order)
    chain_o0 = chain_of(tn(context, self_out_grad).astype(BF16), turned=True)
    cots = tick(cots, chain_r, chain_g, chain_u, chain_a, chain_o0)
    head_cots = lax.all_to_all(cots, "seq", split_axis=2, concat_axis=1, tiled=True)
    head_cots, mdkv = settle(head_cots, mdkv)
    mdkv = sum(m.astype(F32) for m in mdkv).astype(BF16).reshape(rows * memory_part, -1)
    memory_grad = nt(mdkv, w_kv1).reshape(memory.shape)
    chain_k1 = chain_of(tn(mem, mdkv).astype(BF16), turned=True)
    head_cots, memory_grad = tick((head_cots, memory_grad), chain_a, chain_o0, chain_k1)
    head_grads, lag_sums = self_attention_back(head_qkv, head_cots, lse, all_segments, base)
    relative = absolute(head_grads.reshape(rows, seq_count, part, cols).swapaxes(0, 1), "seq")
    lag_sums, *relative = settle(lag_sums, *relative)
    came = [relative[0]] + [flip(relative[j], "seq", j) for j in range(1, seq_count)]
    batch_bits = [("batch", b) for b in reversed(range(bit_count("batch")))]
    all_grads = jnp.stack(relative).reshape(-1, cols)
    chain_f = Chain(tn(all_normed, all_grads).astype(BF16), batch_bits, hops(False, False)[: len(batch_bits)])
    lag_sums = land(lag_sums, chain_g, chain_u)
    while chain_g.order[0][0] == "seq":
        lag_sums = land(tick(lag_sums, chain_g, chain_u), chain_g, chain_u)
    chain_gu = joined([chain_g, chain_u], chain_g.order)
    chains = (chain_f, chain_gu, chain_r, chain_a, chain_o0, chain_k1)
    lag_sums = tick(lag_sums, *chains)
    dqkv = jnp.concatenate(came, axis=-1).reshape(rows * part, -1)
    dqkv = tick(dqkv, chain_f)
    part_zero, gain_zero = norm_back(x, inv_zero, gain_values[0], nt(dqkv, w_first))
    input_grad = (hidden_one_grad + part_zero).reshape(tokens.shape)
    input_grad = tick(input_grad, *chains)
    for chain in chains:
        chain.finish()
    grad_gu, grad_reduce = chain_gu.result(), chain_r.result()
    grad_gate, grad_up = grad_gu[:, :ff], grad_gu[:, ff:]
    grad_a = chain_a.result()
    grad_o0, grad_k1 = chain_o0.result(), chain_k1.result()
    grad_o1, grad_q1 = grad_a[:, :width], grad_a[:, width:]
    first_grads = lax.all_to_all(chain_f.result().reshape(seq_count, own, cols), "seq", 0, 0, tiled=True)
    first_grads = first_grads.transpose(1, 0, 2)

    table_part = jnp.dot(picks, lag_sums.T, precision=lax.Precision.HIGHEST)
    table_grad = lax.dynamic_update_slice(
        jnp.zeros((NB, QUERY_HEADS), F32), table_part, (0, seq_index * heads_local)
    ).reshape(devices, -1)
    gains_grad = jnp.stack([gain_zero, gain_one, gain_two]).reshape(3, devices, own)
    gains_grad = gains_grad.transpose(1, 0, 2).reshape(devices, -1)
    small_grads = small_sum(jnp.concatenate([gains_grad, table_grad], axis=1))
    shard_gains = small_grads[: 3 * own].reshape(3, own)
    shard_table = small_grads[3 * own :]

    shard_query = jnp.stack([first_grads[:, :, :q_local].reshape(own, width), grad_q1])
    shard_keyval = jnp.stack(
        [
            jnp.stack(
                [
                    first_grads[:, :, q_local : q_local + kv_local].reshape(own, kv_width),
                    first_grads[:, :, q_local + kv_local :].reshape(own, kv_width),
                ]
            ),
            jnp.stack([grad_k1[:, :kv_width], grad_k1[:, kv_width:]]),
        ]
    )
    gradients = (
        shard_query,
        shard_keyval,
        jnp.stack([grad_o0, grad_o1]),
        jnp.stack([grad_gate, grad_up]),
        grad_reduce,
        shard_gains,
        shard_table,
    )
    token_scale = (rows * part * devices) ** (-0.5)
    masters = (w_query, keyvalue_weight, w_output, w_expand, w_reduce, gains, position_bias)
    momenta = (
        momentum_query, keyvalue_momentum, momentum_output, momentum_expand, momentum_reduce,
        momentum_gains, momentum_position,
    )
    averages = (
        average_query, keyvalue_average, average_output, average_expand, average_reduce,
        average_gains, average_position,
    )
    renewals, states = [], []
    for gradient, master, momentum, average, step_rate in zip(gradients, masters, momenta, averages, STEP_RATES):
        renewed = MOMENTUM * momentum + gradient
        weight = master - step_rate * token_scale * (gradient + MOMENTUM * renewed)
        renewals.append(renewed)
        states.append(jnp.stack([weight, AVERAGE * average + (1.0 - AVERAGE) * weight]))
    return (result, input_grad, memory_grad.astype(F32), *gradients, *renewals, *states)


def solution(mesh):
    every = ("batch", "seq")
    params = (
        P(None, every, None),
        P(None, None, every, None),
        P(None, every, None),
        P(None, every, None),
        P(every, None),
        P(None, every),
        P(every),
    )
    stacked_params = (
        P(None, None, every, None),
        P(None, None, None, every, None),
        P(None, None, every, None),
        P(None, None, every, None),
        P(None, every, None),
        P(None, None, every),
        P(None, every),
    )
    acts = P("batch", "seq", None)
    return jax.shard_map(
        shards,
        mesh=mesh,
        in_specs=(acts, acts, acts, P("batch", "seq"), P("batch", "seq"), P(), *params, *params, *params),
        out_specs=(acts, acts, acts, *params, *params, *stacked_params),
        check_vma=False,
    )
```

```python
import functools

import jax
import jax.numpy as jnp
from jax import lax
from jax.experimental import pallas as pl
from jax.experimental.pallas import tpu as pltpu
from jax.sharding import PartitionSpec as P

HEAD_SIZE = 64
QUERY_HEADS = 16
NB = 32
EPSILON = 1e-06
NEGATIVE = -1e30
MOMENTUM = 0.9
AVERAGE = 0.99
STEP_RATES = (0.0015, 0.03, 0.3, 0.04, 0.015, 0.1, 1.0)
BF16 = jnp.bfloat16
F32 = jnp.float32
BQ = 128
FF_BLOCK = 256


def nt(a, b):
    return lax.dot_general(a, b, (((1,), (1,)), ((), ())), preferred_element_type=F32)


def nn(a, b):
    return lax.dot_general(a, b, (((1,), (0,)), ((), ())), preferred_element_type=F32)


def tn(a, b):
    return lax.dot_general(a, b, (((0,), (0,)), ((), ())), preferred_element_type=F32)


def stacked(block, group, per):
    first = group * per
    return jnp.concatenate(
        [block[:, (first + c) * HEAD_SIZE : (first + c + 1) * HEAD_SIZE] for c in range(per)], axis=0
    )


def lanes(block, index):
    return block[:, index * HEAD_SIZE : (index + 1) * HEAD_SIZE]


def skew(held, back):
    count, width = held.shape
    rows = lax.broadcasted_iota(jnp.int32, (count, width), 0)
    amount = 1
    while amount < count:
        turned = pltpu.roll(held, width - amount if back else amount, 1)
        held = jnp.where((rows & amount) != 0, turned, held)
        amount *= 2
    return held


def make_strips(base_ref, strip_ref):
    heads, rows, width = strip_ref.shape
    for h in range(heads):
        strip_ref[h] = skew(jnp.broadcast_to(base_ref[h : h + 1, :], (rows, width)), False)


def windows(length):
    reach = length // 2
    for step in range(length // BQ):
        here = slice(step * BQ, (step + 1) * BQ)
        start = max(step * BQ - reach, 0)
        lead = reach - (step * BQ - start)
        yield here, slice(start, (step + 1) * BQ), slice(lead, lead + (step + 1) * BQ - start)


def head_layout(heads, width):
    q_width = heads * HEAD_SIZE
    k_width = (width - q_width) // 2
    return slice(0, q_width), slice(q_width, q_width + k_width), slice(q_width + k_width, width), k_width // HEAD_SIZE


def self_fwd_kernel(qkv_ref, seg_row_ref, seg_col_ref, base_ref, o_ref, lse_ref, strip_ref):
    heads = strip_ref.shape[0]
    in_q, in_k, in_v, groups = head_layout(heads, qkv_ref.shape[2])
    per = heads // groups

    @pl.when(pl.program_id(0) == 0)
    def _():
        make_strips(base_ref, strip_ref)

    for here, seen, strip in windows(qkv_ref.shape[1]):
        same = seg_col_ref[0, here, :] == seg_row_ref[0, :, seen]
        block, keys, values = qkv_ref[0, here, in_q], qkv_ref[0, seen, in_k], qkv_ref[0, seen, in_v]
        outs, sums = [], []
        for g in range(groups):
            scores = nt(stacked(block, g, per), lanes(keys, g))
            probs = []
            for c in range(per):
                bias = strip_ref[g * per + c, :, strip]
                s = jnp.where(same, scores[c * BQ : (c + 1) * BQ] + bias, NEGATIVE)
                top = jnp.max(s, axis=-1, keepdims=True)
                e = jnp.exp(s - top)
                total = jnp.sum(e, axis=-1, keepdims=True)
                probs.append((e * (1.0 / total)).astype(BF16))
                sums.append(top + jnp.log(total))
            ctx = nn(jnp.concatenate(probs, axis=0), lanes(values, g)).astype(BF16)
            outs += [ctx[c * BQ : (c + 1) * BQ] for c in range(per)]
        o_ref[0, here, :] = jnp.concatenate(outs, axis=1)
        lse_ref[0, here, :] = jnp.concatenate(sums, axis=1)


def self_bwd_kernel(
    qkv_ref, c_ref, lse_ref, seg_row_ref, seg_col_ref, base_ref,
    d_ref, lag_ref, strip_ref, grad_ref, dk_acc, dv_acc,
):
    heads = strip_ref.shape[0]
    in_q, in_k, in_v, groups = head_layout(heads, qkv_ref.shape[2])
    per = heads // groups

    @pl.when(pl.program_id(0) == 0)
    def _():
        make_strips(base_ref, strip_ref)
        grad_ref[...] = jnp.zeros_like(grad_ref)

    dk_acc[...] = jnp.zeros_like(dk_acc)
    dv_acc[...] = jnp.zeros_like(dv_acc)
    for here, seen, strip in windows(qkv_ref.shape[1]):
        same = seg_col_ref[0, here, :] == seg_row_ref[0, :, seen]
        block, keys, values = qkv_ref[0, here, in_q], qkv_ref[0, seen, in_k], qkv_ref[0, seen, in_v]
        cots, lse = c_ref[0, here, :], lse_ref[0, here, :]
        outs = []
        for g in range(groups):
            q2, c2 = stacked(block, g, per), stacked(cots, g, per)
            scores = nt(q2, lanes(keys, g))
            dprobs = nt(c2, lanes(values, g))
            probs, dscores = [], []
            for c in range(per):
                h = g * per + c
                bias = strip_ref[h, :, strip]
                s = jnp.where(same, scores[c * BQ : (c + 1) * BQ] + bias, NEGATIVE)
                p = jnp.exp(s - lse[:, h : h + 1])
                dp = dprobs[c * BQ : (c + 1) * BQ]
                ds = (p * (dp - jnp.sum(p * dp, axis=-1, keepdims=True))).astype(BF16)
                grad_ref[h, :, strip] += ds.astype(F32)
                probs.append(p.astype(BF16))
                dscores.append(ds)
            p2, ds2 = jnp.concatenate(probs, axis=0), jnp.concatenate(dscores, axis=0)
            dq2 = nn(ds2, lanes(keys, g)).astype(BF16)
            outs += [dq2[c * BQ : (c + 1) * BQ] for c in range(per)]
            mine = slice(g * HEAD_SIZE, (g + 1) * HEAD_SIZE)
            dk_acc[mine, seen] += tn(q2, ds2)
            dv_acc[mine, seen] += tn(c2, p2)
        d_ref[0, here, in_q] = jnp.concatenate(outs, axis=1)
    d_ref[0, :, in_k] = dk_acc[...].T.astype(BF16)
    d_ref[0, :, in_v] = dv_acc[...].T.astype(BF16)

    @pl.when(pl.program_id(0) == pl.num_programs(0) - 1)
    def _():
        for h in range(heads):
            lag_ref[h : h + 1, :] = jnp.sum(skew(grad_ref[h], True), axis=0, keepdims=True)


def self_specs(length, width, heads, strip_width):
    qkv = pl.BlockSpec((1, length, width), lambda r: (r, 0, 0))
    queries = pl.BlockSpec((1, length, heads * HEAD_SIZE), lambda r: (r, 0, 0))
    sums = pl.BlockSpec((1, length, heads), lambda r: (r, 0, 0))
    seg_row = pl.BlockSpec((1, 1, length), lambda r: (r, 0, 0))
    seg_col = pl.BlockSpec((1, length, 1), lambda r: (r, 0, 0))
    base = pl.BlockSpec((heads, strip_width), lambda r: (0, 0))
    return qkv, queries, sums, seg_row, seg_col, base


def self_attention(qkv, segments, base):
    rows, length, width = qkv.shape
    heads, strip_width = base.shape
    all_spec, queries, sums, seg_row, seg_col, base_spec = self_specs(length, width, heads, strip_width)
    work = rows * heads * length * length * 3 // 8
    return pl.pallas_call(
        self_fwd_kernel,
        grid=(rows,),
        in_specs=[all_spec, seg_row, seg_col, base_spec],
        out_specs=[queries, sums],
        out_shape=[
            jax.ShapeDtypeStruct((rows, length, heads * HEAD_SIZE), BF16),
            jax.ShapeDtypeStruct((rows, length, heads), F32),
        ],
        scratch_shapes=[pltpu.VMEM((heads, BQ, strip_width), F32)],
        compiler_params=pltpu.CompilerParams(vmem_limit_bytes=48 << 20),
        cost_estimate=pl.CostEstimate(
            flops=work * 4 * HEAD_SIZE, transcendentals=work, bytes_accessed=qkv.size * 4
        ),
        name="self_attention",
    )(qkv, segments[:, None, :], segments[:, :, None], base)


def self_attention_back(qkv, cots, lse, segments, base):
    rows, length, width = qkv.shape
    heads, strip_width = base.shape
    all_spec, queries, sums, seg_row, seg_col, base_spec = self_specs(length, width, heads, strip_width)
    k_width = (width - heads * HEAD_SIZE) // 2
    work = rows * heads * length * length * 3 // 8
    return pl.pallas_call(
        self_bwd_kernel,
        grid=(rows,),
        in_specs=[all_spec, queries, sums, seg_row, seg_col, base_spec],
        out_specs=[all_spec, base_spec],
        out_shape=[
            jax.ShapeDtypeStruct(qkv.shape, BF16),
            jax.ShapeDtypeStruct((heads, strip_width), F32),
        ],
        scratch_shapes=[
            pltpu.VMEM((heads, BQ, strip_width), F32),
            pltpu.VMEM((heads, BQ, strip_width), F32),
            pltpu.VMEM((k_width, length), F32),
            pltpu.VMEM((k_width, length), F32),
        ],
        compiler_params=pltpu.CompilerParams(vmem_limit_bytes=48 << 20),
        cost_estimate=pl.CostEstimate(
            flops=work * 10 * HEAD_SIZE, transcendentals=work, bytes_accessed=qkv.size * 6
        ),
        name="self_attention_back",
    )(qkv, cots, lse, segments[:, None, :], segments[:, :, None], base)


def cross_fwd_kernel(q_ref, k_ref, v_ref, seg_row_ref, seg_col_ref, o_ref, *lse_refs):
    block, keys, values = q_ref[0], k_ref[0], v_ref[0]
    count = block.shape[0]
    groups = keys.shape[1] // HEAD_SIZE
    per = block.shape[1] // keys.shape[1]
    same = seg_col_ref[0] == seg_row_ref[0]
    outs = []
    for g in range(groups):
        scores = nt(stacked(block, g, per), lanes(keys, g))
        probs = []
        for c in range(per):
            s = jnp.where(same, scores[c * count : (c + 1) * count], NEGATIVE)
            top = jnp.max(s, axis=-1, keepdims=True)
            e = jnp.exp(s - top)
            total = jnp.sum(e, axis=-1, keepdims=True)
            probs.append((e * (1.0 / total)).astype(BF16))
        ctx = nn(jnp.concatenate(probs, axis=0), lanes(values, g)).astype(BF16)
        outs += [ctx[c * count : (c + 1) * count] for c in range(per)]
    o_ref[0] = jnp.concatenate(outs, axis=1)


def cross_bwd_kernel(q_ref, k_ref, v_ref, c_ref, seg_row_ref, seg_col_ref, dq_ref, dk_ref, dv_ref):
    block, keys, values, cots = q_ref[0], k_ref[0], v_ref[0], c_ref[0]
    count = block.shape[0]
    groups = keys.shape[1] // HEAD_SIZE
    per = block.shape[1] // keys.shape[1]
    same = seg_col_ref[0] == seg_row_ref[0]
    outs, dkeys, dvalues = [], [], []
    for g in range(groups):
        q2, c2 = stacked(block, g, per), stacked(cots, g, per)
        scores = nt(q2, lanes(keys, g))
        dprobs = nt(c2, lanes(values, g))
        probs, dscores = [], []
        for c in range(per):
            s = jnp.where(same, scores[c * count : (c + 1) * count], NEGATIVE)
            top = jnp.max(s, axis=-1, keepdims=True)
            e = jnp.exp(s - top)
            p = e * (1.0 / jnp.sum(e, axis=-1, keepdims=True))
            dp = dprobs[c * count : (c + 1) * count]
            dscores.append((p * (dp - jnp.sum(p * dp, axis=-1, keepdims=True))).astype(BF16))
            probs.append(p.astype(BF16))
        p2, ds2 = jnp.concatenate(probs, axis=0), jnp.concatenate(dscores, axis=0)
        dq2 = nn(ds2, lanes(keys, g)).astype(BF16)
        outs += [dq2[c * count : (c + 1) * count] for c in range(per)]
        dkeys.append(tn(q2, ds2))
        dvalues.append(tn(c2, p2))
    dq_ref[0] = jnp.concatenate(outs, axis=1)
    dk_ref[0] = jnp.concatenate(dkeys, axis=0).T.astype(dk_ref.dtype)
    dv_ref[0] = jnp.concatenate(dvalues, axis=0).T.astype(dv_ref.dtype)


def cross_specs(q, k):
    rows, count, q_width = q.shape
    memory, k_width = k.shape[1:]
    step = 2 * HEAD_SIZE
    q_step = step * (q_width // k_width)
    queries = pl.BlockSpec((1, count, q_step), lambda r, g: (r, 0, g))
    keys = pl.BlockSpec((1, memory, step), lambda r, g: (r, 0, g))
    seg_row = pl.BlockSpec((1, 1, memory), lambda r, g: (r, 0, 0))
    seg_col = pl.BlockSpec((1, count, 1), lambda r, g: (r, 0, 0))
    return (rows, k_width // step), queries, keys, seg_row, seg_col


def cross_attention(q, k, v, segments, memory_segments):
    grid, queries, keys, seg_row, seg_col = cross_specs(q, k)
    work = q.size // HEAD_SIZE * k.shape[1]
    return pl.pallas_call(
        cross_fwd_kernel,
        grid=grid,
        in_specs=[queries, keys, keys, seg_row, seg_col],
        out_specs=queries,
        out_shape=jax.ShapeDtypeStruct(q.shape, BF16),
        compiler_params=pltpu.CompilerParams(vmem_limit_bytes=48 << 20),
        cost_estimate=pl.CostEstimate(
            flops=work * 4 * HEAD_SIZE, transcendentals=work, bytes_accessed=q.size * 4 + k.size * 4
        ),
        name="cross_attention",
    )(q, k, v, memory_segments[:, None, :], segments[:, :, None])


def cross_attention_back(q, k, v, cots, segments, memory_segments):
    grid, queries, keys, seg_row, seg_col = cross_specs(q, k)
    work = q.size // HEAD_SIZE * k.shape[1]
    return pl.pallas_call(
        cross_bwd_kernel,
        grid=grid,
        in_specs=[queries, keys, keys, queries, seg_row, seg_col],
        out_specs=[queries, keys, keys],
        out_shape=[
            jax.ShapeDtypeStruct(q.shape, BF16),
            jax.ShapeDtypeStruct(k.shape, BF16),
            jax.ShapeDtypeStruct(k.shape, BF16),
        ],
        compiler_params=pltpu.CompilerParams(vmem_limit_bytes=48 << 20),
        cost_estimate=pl.CostEstimate(
            flops=work * 10 * HEAD_SIZE, transcendentals=work, bytes_accessed=q.size * 6 + k.size * 8
        ),
        name="cross_attention_back",
    )(q, k, v, cots, memory_segments[:, None, :], segments[:, :, None])


def bit_count(axis):
    return lax.axis_size(axis).bit_length() - 1


def my_bit(axis, bit):
    return (lax.axis_index(axis) >> bit) & 1


def flip(value, axis, mask):
    return lax.ppermute(value, axis, [(i, i ^ mask) for i in range(lax.axis_size(axis))])


def gather_pieces(value, axis, order):
    pieces = {0: value}
    for bit in order:
        for j in list(pieces):
            pieces[j | (1 << bit)] = flip(pieces[j], axis, 1 << bit)
    return [pieces[j] for j in range(len(pieces))]


def gather_direct(value, axis):
    return [value] + [flip(value, axis, j) for j in range(1, lax.axis_size(axis))]


def absolute(values, axis):
    place = lax.axis_index(axis)
    values = jnp.stack(values) if isinstance(values, list) else values
    return [lax.dynamic_index_in_dim(values, j ^ place, 0, False) for j in range(values.shape[0])]


def settle(*groups):
    flat, tree = jax.tree.flatten(groups)
    return jax.tree.unflatten(tree, lax.optimization_barrier(flat))


class Chain:
    def __init__(self, full, bits, order):
        shape = (2,) * len(bits) + (full.shape[0] >> len(bits),) + full.shape[1:]
        self.parts, self.left, self.order, self.flying = [full.reshape(shape)], list(bits), list(order), None

    def half(self, choice):
        where = self.left.index(self.order[0])
        return [lax.dynamic_index_in_dim(p, choice, where, False) for p in self.parts]

    def outgoing(self):
        return sum(p.astype(F32) for p in self.half(1 - my_bit(*self.order[0]))).astype(BF16)

    def launch(self, away):
        self.parts = self.half(my_bit(*self.order[0]))
        axis, bit = self.order.pop(0)
        self.left.remove((axis, bit))
        self.flying = flip(away, axis, 1 << bit)

    def land(self):
        self.parts = self.parts + [self.flying]
        self.flying = None

    def finish(self):
        if self.flying is not None:
            self.land()
        while self.order:
            self.launch(self.outgoing())
            self.land()

    def result(self):
        return sum(p.astype(F32) for p in self.parts)


def joined(chains, order):
    chain = Chain.__new__(Chain)
    chain.left, chain.order, chain.flying = list(chains[0].left), list(order), None
    chain.parts = [jnp.concatenate(parts, axis=-1) for parts in zip(*[c.parts for c in chains])]
    return chain


class Gather:
    def __init__(self, value, order, lead=0):
        self.held, self.order, self.lead, self.done, self.flying, self.last = value, list(order), lead, [], None, None

    def outgoing(self):
        return self.held

    def launch(self, value):
        self.held = value
        self.last = self.order.pop(0)
        self.flying = flip(value, self.last[0], 1 << self.last[1])

    def land(self):
        self.done = [bit for bit in place_bits() if bit in self.done or bit == self.last]
        where = self.lead + self.done.index(self.last)
        pair = jnp.arange(2).reshape((2,) + (1,) * (self.held.ndim - where))
        own, came = jnp.expand_dims(self.held, where), jnp.expand_dims(self.flying, where)
        self.held = jnp.where(pair == my_bit(*self.last), own, came)
        self.flying = None


def land(main, *chains):
    arrive = [c for c in chains if c.flying is not None]
    main, flown = settle(main, [c.flying for c in arrive])
    for chain, value in zip(arrive, flown):
        chain.flying = value
        chain.land()
    return main


def tick(main, *chains):
    main = land(main, *chains)
    depart = [c for c in chains if c.order]
    main, sends = settle(main, [c.outgoing() for c in depart])
    for chain, value in zip(depart, sends):
        chain.launch(value)
    return main


def place_bits():
    return [("batch", b) for b in reversed(range(bit_count("batch")))] + [
        ("seq", b) for b in reversed(range(bit_count("seq")))
    ]


def hops(seq_first, turned):
    seq = [("seq", b) for b in range(bit_count("seq"))]
    far = [("batch", b) for b in range(1, bit_count("batch"))]
    if turned:
        seq.reverse()
    return [("batch", 0)] + (seq + far if seq_first else far + seq)


def chain_of(full, seq_first=True, turned=False):
    return Chain(full, place_bits(), hops(seq_first, turned))


def chain_of_halves(away, kept, seq_first=True, turned=False):
    chain = Chain(kept, [b for b in place_bits() if b != ("batch", 0)], hops(seq_first, turned)[1:])
    chain.flying = flip(away, "batch", 1).reshape(chain.parts[0].shape)
    return chain


def small_sum(values):
    got = lax.all_to_all(values, ("batch", "seq"), 0, 0, tiled=True)
    return jnp.sum(got, axis=0)


def inverse_rms(values):
    return lax.rsqrt(jnp.mean(values * values, axis=-1, keepdims=True) + EPSILON)


def norm_back(values, inverse, gain, upstream):
    weighted = gain * upstream
    dot = jnp.mean(weighted * values, axis=-1, keepdims=True)
    grad = inverse * weighted - values * (inverse * inverse * inverse) * dot
    return grad, jnp.sum(upstream * values * inverse, axis=0)


def gelu_parts(v):
    scale = 0.7978845608028654
    inner = scale * (v + 0.044715 * (v * v * v))
    t = jnp.tanh(inner)
    value = 0.5 * v * (1.0 + t)
    slope = 0.5 * (1.0 + t) + 0.5 * v * (1.0 - t * t) * (scale * (1.0 + 3 * 0.044715 * (v * v)))
    return value, slope


def hidden_rows(x, core_rows):
    turned = x.T
    blocks = [turned[i : i + core_rows] for i in range(0, turned.shape[0], core_rows)]
    return jnp.concatenate(blocks[0::2], axis=0), jnp.concatenate(blocks[1::2], axis=0)


def ffn_kernel(
    core_ref, h_ref, gain_ref, og_ref, wg_ref, wu_ref, wr_ref,
    out_ref, hgrad_ref, gain_grad_ref, dg_away_ref, dg_ref, du_away_ref, du_ref, dr_ref,
    x_ref, xt_ref, res_ref, back_ref, *, core_rows,
):
    half = dg_ref.shape[0]
    step = pl.program_id(0)

    @pl.when(step == 0)
    def _():
        hidden = h_ref[...]
        x = (hidden * inverse_rms(hidden) * gain_ref[...]).astype(BF16)
        x_ref[...] = x
        flipped = hidden_rows(x, core_rows)
        first_core = core_ref[0] == 0
        xt_ref[:half] = jnp.where(first_core, flipped[1], flipped[0])
        xt_ref[half:] = jnp.where(first_core, flipped[0], flipped[1])
        res_ref[...] = jnp.zeros_like(res_ref)
        back_ref[...] = jnp.zeros_like(back_ref)

    x, og = x_ref[...], og_ref[...]
    wg, wu, wr = wg_ref[...], wu_ref[...], wr_ref[...]
    gelu_value, gelu_slope = gelu_parts(nn(x, wg))
    up = nn(x, wu)
    activated = (gelu_value * up).astype(BF16)
    upstream = nt(og, wr)
    gate_grad = (upstream * up * gelu_slope).astype(BF16)
    up_grad = (upstream * gelu_value).astype(BF16)
    res_ref[...] += nn(activated, wr)
    back_ref[...] += nt(gate_grad, wg) + nt(up_grad, wu)
    dr_ref[...] = tn(activated, og).astype(BF16)
    xt = xt_ref[...]
    gate_product, up_product = nn(xt, gate_grad).astype(BF16), nn(xt, up_grad).astype(BF16)
    dg_away_ref[...], dg_ref[...] = gate_product[:half], gate_product[half:]
    du_away_ref[...], du_ref[...] = up_product[:half], up_product[half:]

    @pl.when(step == pl.num_programs(0) - 1)
    def _():
        hidden = h_ref[...]
        out_ref[...] = (hidden + res_ref[...]).astype(BF16)
        inverse = inverse_rms(hidden)
        upward = back_ref[...]
        weighted = gain_ref[...] * upward
        dot = jnp.mean(weighted * hidden, axis=-1, keepdims=True)
        part = inverse * weighted - hidden * (inverse * inverse * inverse) * dot
        hgrad_ref[...] = og_ref[...].astype(F32) + part
        gain_grad_ref[...] = jnp.sum(upward * hidden * inverse, axis=0, keepdims=True)


def feed_forward(hidden, gain, og, w_rest, w_red, ff_first):
    count, width = hidden.shape
    ff = w_red.shape[0]
    steps, gate_first = ff // FF_BLOCK, ff_first // FF_BLOCK
    whole = pl.BlockSpec((count, width), lambda j: (0, 0))
    row = pl.BlockSpec((1, width), lambda j: (0, 0))
    down = pl.BlockSpec((FF_BLOCK, width), lambda j: (j, 0))
    cols = pl.BlockSpec((width // 2, FF_BLOCK), lambda j: (0, j))
    core_rows = width // lax.axis_size("batch")
    return pl.pallas_call(
        functools.partial(ffn_kernel, core_rows=core_rows),
        grid=(steps,),
        in_specs=[
            pl.BlockSpec(memory_space=pltpu.SMEM),
            whole, row, whole,
            pl.BlockSpec((width, FF_BLOCK), lambda j: (0, j + gate_first)),
            pl.BlockSpec((width, FF_BLOCK), lambda j: (0, j + gate_first + steps)),
            down,
        ],
        out_specs=[whole, whole, row, cols, cols, cols, cols, down],
        out_shape=[
            jax.ShapeDtypeStruct((count, width), BF16),
            jax.ShapeDtypeStruct((count, width), F32),
            jax.ShapeDtypeStruct((1, width), F32),
            *[jax.ShapeDtypeStruct((width // 2, ff), BF16)] * 4,
            jax.ShapeDtypeStruct((ff, width), BF16),
        ],
        scratch_shapes=[
            pltpu.VMEM((count, width), BF16),
            pltpu.VMEM((width, count), BF16),
            pltpu.VMEM((count, width), F32),
            pltpu.VMEM((count, width), F32),
        ],
        compiler_params=pltpu.CompilerParams(vmem_limit_bytes=56 << 20),
        cost_estimate=pl.CostEstimate(
            flops=18 * count * width * ff, transcendentals=count * ff, bytes_accessed=12 * width * ff
        ),
        name="feed_forward",
    )(my_bit("batch", 0).reshape(1).astype(jnp.int32), hidden, gain, og, w_rest, w_rest, w_red)


def shards(
    tokens, memory, output_grad, segments, memory_segments, buckets,
    w_query, keyvalue_weight, w_output, w_expand, w_reduce, gains, position_bias,
    momentum_query, keyvalue_momentum, momentum_output, momentum_expand, momentum_reduce,
    momentum_gains, momentum_position,
    average_query, keyvalue_average, average_output, average_expand, average_reduce,
    average_gains, average_position,
):
    every = ("batch", "seq")
    seq_count, seq_index = lax.axis_size("seq"), lax.axis_index("seq")
    devices = lax.axis_size("batch") * seq_count
    rows, part, width = tokens.shape
    length = part * seq_count
    memory_part = memory.shape[1]
    own = w_query.shape[1]
    kv_width = keyvalue_weight.shape[3]
    heads_local = QUERY_HEADS // seq_count
    q_local, kv_local = width // seq_count, kv_width // seq_count

    wq, wkv = w_query.astype(BF16), keyvalue_weight.astype(BF16)
    wo, we, wr = w_output.astype(BF16), w_expand.astype(BF16), w_reduce.astype(BF16)
    first = jnp.concatenate(
        [
            wq[0].reshape(own, seq_count, q_local),
            wkv[0, 0].reshape(own, seq_count, kv_local),
            wkv[0, 1].reshape(own, seq_count, kv_local),
        ],
        axis=2,
    )
    cols = first.shape[2]
    bias_own = position_bias.shape[0]
    small = jnp.concatenate([gains.astype(BF16).reshape(-1), position_bias.astype(BF16)])
    small = jnp.pad(small, (0, 8 * cols - small.shape[0])).reshape(1, 8, cols)
    packet = jnp.concatenate([first.transpose(1, 0, 2), jnp.broadcast_to(small, (seq_count, 8, cols))], axis=1)
    packet = lax.all_to_all(packet, "seq", 0, 0, tiled=True)
    batch_far = [("batch", b) for b in reversed(range(1, bit_count("batch")))]
    seq_up = [("seq", b) for b in range(bit_count("seq"))]
    core = [("batch", 0)]
    gather_p = Gather(packet, batch_far + core)
    for _ in batch_far + core:
        gather_p.launch(gather_p.held)
        gather_p.land()
    orders = [[b for _, b in (seq_up if r % 2 == 0 else seq_up[::-1])] for r in range(rows)]
    first_hop = [flip(tokens[r], "seq", 1 << orders[r][0]) for r in range(rows)]
    token_pieces = []
    for r in range(rows):
        pieces = {0: tokens[r], 1 << orders[r][0]: first_hop[r]}
        for bit in orders[r][1:]:
            for j in list(pieces):
                pieces[j | (1 << bit)] = flip(pieces[j], "seq", 1 << bit)
        token_pieces.append([pieces[j] for j in range(seq_count)])
    ids = jnp.concatenate([segments, memory_segments], axis=1)
    all_ids = jnp.stack(absolute(gather_direct(ids, "seq"), "seq"), axis=1)
    all_segments = all_ids[:, :, :part].reshape(rows, length)
    all_memory_segments = all_ids[:, :, part:].reshape(rows, -1)
    packets = gather_p.held.reshape(-1, seq_count, own + 8, cols)
    w_heads = packets[:, :, :own].reshape(width, cols)
    small_rows = packets[:, :, own:].reshape(devices, -1)
    gain_values = (
        small_rows[:, : 3 * own].reshape(devices, 3, own).transpose(1, 0, 2).reshape(3, width).astype(F32)
    )
    table = small_rows[:, 3 * own : 3 * own + bias_own].reshape(NB, QUERY_HEADS).astype(F32)

    ff, ff_own = we.shape[2], wr.shape[0]
    folds = -(-ff_own // own)
    wr_rows = jnp.pad(wr, ((0, folds * own - ff_own), (0, 0))).reshape(folds, own, width)
    pieces = [wkv[1, 0], wkv[1, 1], wo[0], wq[1], wo[1], we[0], we[1], *[wr_rows[i] for i in range(folds)]]
    w_rest = lax.all_gather(jnp.concatenate(pieces, axis=1), every, axis=0, tiled=True)
    w_kv1, w_o0, w_q1, w_o1 = (w_rest[:, i * width : (i + 1) * width] for i in range(4))
    ff_first = 4 * width
    down_first = ff_first + 2 * ff
    w_red = jnp.concatenate(
        [
            w_rest[:, down_first + i * width : down_first + (i + 1) * width].reshape(devices, own, width)
            for i in range(folds)
        ],
        axis=1,
    )[:, :ff_own].reshape(ff, width)

    reach = length // 2
    strip_width = 2 * reach + BQ
    lag = reach - jnp.arange(strip_width, dtype=jnp.int32)
    lag_ok = lag >= 0
    lag_bucket = jnp.where(lag_ok, jnp.take(buckets, jnp.clip(lag, 0, length - 1)), -1)
    picks = (lag_bucket[None, :] == jnp.arange(NB, dtype=jnp.int32)[:, None]).astype(F32)
    table_local = lax.dynamic_slice_in_dim(table, seq_index * heads_local, heads_local, 1)
    base = jnp.dot(table_local.T, picks, precision=lax.Precision.HIGHEST)
    base = jnp.where(lag_ok[None, :], base, NEGATIVE)

    all_tokens = jnp.stack([jnp.stack(p) for p in token_pieces], axis=1).astype(F32)
    all_normed = (all_tokens * inverse_rms(all_tokens) * gain_values[0]).astype(BF16).reshape(-1, width)
    head_qkv = nn(all_normed, w_heads).astype(BF16).reshape(seq_count, rows, part, cols)
    head_qkv = jnp.stack(absolute(head_qkv, "seq"), axis=1).reshape(rows, length, cols)
    head_context, lse = self_attention(head_qkv, all_segments, base)
    context = lax.all_to_all(head_context, "seq", split_axis=1, concat_axis=2, tiled=True).reshape(-1, width)

    mem = memory.reshape(rows * memory_part, width)
    mkv = nn(mem, w_kv1).astype(BF16).reshape(rows, memory_part, -1)
    all_mkv = jnp.stack(absolute(gather_direct(mkv, "seq"), "seq"), axis=1).reshape(rows, -1, 2 * kv_width)
    mk, mv = all_mkv[:, :, :kv_width], all_mkv[:, :, kv_width:]
    x = tokens.astype(F32).reshape(rows * part, width)
    inv_zero = inverse_rms(x)
    hidden_one = x + nn(context, w_o0)
    inv_one = inverse_rms(hidden_one)
    normed_one = (hidden_one * inv_one * gain_values[1]).astype(BF16)
    cross_q = nn(normed_one, w_q1).astype(BF16).reshape(rows, part, width)
    cross_context = cross_attention(cross_q, mk, mv, segments, all_memory_segments)
    cross_flat = cross_context.reshape(-1, width)
    hidden_two = hidden_one + nn(cross_flat, w_o1)
    hidden_two, w_red, w_heads = settle(hidden_two, w_red, w_heads)
    w_first = jnp.concatenate(gather_direct(w_heads, "seq"), axis=1)
    og = output_grad.reshape(rows * part, width)
    result, hidden_two_grad, gain_two, *part_gu, part_reduce = feed_forward(
        hidden_two, gain_values[2:3], og, w_rest, w_red, ff_first
    )
    result, gain_two = result.reshape(tokens.shape), gain_two[0]
    chain_g = chain_of_halves(part_gu[0], part_gu[1])
    chain_u = chain_of_halves(part_gu[2], part_gu[3], turned=True)
    chain_r = chain_of(part_reduce, seq_first=False)
    hidden_two_grad, w_first = tick((hidden_two_grad, w_first), chain_r)

    cross_out_grad = hidden_two_grad.astype(BF16)
    cross_cots = nt(cross_out_grad, w_o1).astype(BF16).reshape(rows, part, width)
    cross_cots = tick(cross_cots, chain_r, chain_g, chain_u)
    cross_dq, mdk, mdv = cross_attention_back(cross_q, mk, mv, cross_cots, segments, all_memory_segments)
    mdkv = jnp.concatenate([mdk, mdv], axis=2).reshape(rows, seq_count, memory_part, -1)
    mdkv = lax.all_to_all(mdkv, "seq", split_axis=1, concat_axis=1, tiled=True)
    cross_dq = cross_dq.reshape(-1, width)
    part_one, gain_one = norm_back(hidden_one, inv_one, gain_values[1], nt(cross_dq, w_q1))
    hidden_one_grad = hidden_two_grad + part_one

    self_out_grad = hidden_one_grad.astype(BF16)
    cots = nt(self_out_grad, w_o0).astype(BF16).reshape(rows, part, width)
    chain_o1 = chain_of(tn(cross_flat, cross_out_grad).astype(BF16))
    chain_q1 = chain_of(tn(normed_one, cross_dq).astype(BF16))
    chain_a = joined([chain_o1, chain_q1], chain_o1.order)
    mdkv = jnp.sum(mdkv.astype(F32), axis=1).astype(BF16).reshape(rows * memory_part, -1)
    memory_grad = nt(mdkv, w_kv1).reshape(memory.shape)
    chain_o0 = chain_of(tn(context, self_out_grad).astype(BF16), turned=True)
    chain_k1 = chain_of(tn(mem, mdkv).astype(BF16), turned=True)
    chain_b = joined([chain_o0, chain_k1], chain_o0.order)
    cots = tick(cots, chain_a, chain_b)
    head_cots = lax.all_to_all(cots, "seq", split_axis=2, concat_axis=1, tiled=True)
    head_cots, memory_grad = tick((head_cots, memory_grad), chain_r, chain_g, chain_u, chain_a, chain_b)
    head_grads, lag_sums = self_attention_back(head_qkv, head_cots, lse, all_segments, base)
    by_place = head_grads.reshape(rows, seq_count, part, cols)
    relative = absolute(by_place.swapaxes(0, 1), "seq")
    batch_bits = [("batch", b) for b in reversed(range(bit_count("batch")))]
    all_grads = jnp.stack(relative).reshape(-1, cols)
    chain_f = Chain(tn(all_normed, all_grads).astype(BF16), batch_bits, hops(False, False)[: len(batch_bits)])
    by_place, lag_sums = land((by_place, lag_sums), chain_g, chain_u)
    while chain_g.order[0][0] == "seq":
        by_place, lag_sums = land(tick((by_place, lag_sums), chain_g, chain_u), chain_g, chain_u)
    chain_gu = joined([chain_g, chain_u], chain_g.order)
    chains = (chain_f, chain_gu, chain_r, chain_a, chain_b)
    by_place, lag_sums = tick((by_place, lag_sums), *chains)
    dqkv = lax.all_to_all(by_place, "seq", split_axis=1, concat_axis=1, tiled=True)
    dqkv = jnp.concatenate(absolute(dqkv.swapaxes(0, 1), "seq"), axis=-1).reshape(rows * part, -1)
    dqkv = tick(dqkv, chain_f)
    part_zero, gain_zero = norm_back(x, inv_zero, gain_values[0], nt(dqkv, w_first))
    input_grad = (hidden_one_grad + part_zero).reshape(tokens.shape)
    input_grad = land(input_grad, chain_a, chain_b)
    while chain_a.order[0][0] == "seq":
        input_grad = land(tick(input_grad, chain_a, chain_b), chain_a, chain_b)
    chain_ab = joined([chain_a, chain_b], chain_a.order)
    chains = (chain_f, chain_gu, chain_r, chain_ab)
    input_grad = tick(input_grad, *chains)
    for chain in chains:
        chain.finish()
    grad_gu, grad_reduce = chain_gu.result(), chain_r.result()
    grad_gate, grad_up = grad_gu[:, :ff], grad_gu[:, ff:]
    grad_ab = chain_ab.result()
    grad_o1, grad_q1, grad_o0, grad_k1 = (grad_ab[:, i * width : (i + 1) * width] for i in range(4))
    first_grads = lax.all_to_all(chain_f.result().reshape(seq_count, own, cols), "seq", 0, 0, tiled=True)
    first_grads = first_grads.transpose(1, 0, 2)

    table_part = jnp.dot(picks, lag_sums.T, precision=lax.Precision.HIGHEST)
    table_grad = lax.dynamic_update_slice(
        jnp.zeros((NB, QUERY_HEADS), F32), table_part, (0, seq_index * heads_local)
    ).reshape(devices, -1)
    gains_grad = jnp.stack([gain_zero, gain_one, gain_two]).reshape(3, devices, own)
    gains_grad = gains_grad.transpose(1, 0, 2).reshape(devices, -1)
    small_grads = small_sum(jnp.concatenate([gains_grad, table_grad], axis=1))
    shard_gains = small_grads[: 3 * own].reshape(3, own)
    shard_table = small_grads[3 * own :]

    shard_query = jnp.stack([first_grads[:, :, :q_local].reshape(own, width), grad_q1])
    shard_keyval = jnp.stack(
        [
            jnp.stack(
                [
                    first_grads[:, :, q_local : q_local + kv_local].reshape(own, kv_width),
                    first_grads[:, :, q_local + kv_local :].reshape(own, kv_width),
                ]
            ),
            jnp.stack([grad_k1[:, :kv_width], grad_k1[:, kv_width:]]),
        ]
    )
    gradients = (
        shard_query,
        shard_keyval,
        jnp.stack([grad_o0, grad_o1]),
        jnp.stack([grad_gate, grad_up]),
        grad_reduce,
        shard_gains,
        shard_table,
    )
    token_scale = (rows * part * devices) ** (-0.5)
    masters = (w_query, keyvalue_weight, w_output, w_expand, w_reduce, gains, position_bias)
    momenta = (
        momentum_query, keyvalue_momentum, momentum_output, momentum_expand, momentum_reduce,
        momentum_gains, momentum_position,
    )
    averages = (
        average_query, keyvalue_average, average_output, average_expand, average_reduce,
        average_gains, average_position,
    )
    renewals, states = [], []
    for gradient, master, momentum, average, step_rate in zip(gradients, masters, momenta, averages, STEP_RATES):
        renewed = MOMENTUM * momentum + gradient
        weight = master - step_rate * token_scale * (gradient + MOMENTUM * renewed)
        renewals.append(renewed)
        states.append(jnp.stack([weight, AVERAGE * average + (1.0 - AVERAGE) * weight]))
    return (result, input_grad, memory_grad.astype(F32), *gradients, *renewals, *states)


def solution(mesh):
    every = ("batch", "seq")
    params = (
        P(None, every, None),
        P(None, None, every, None),
        P(None, every, None),
        P(None, every, None),
        P(every, None),
        P(None, every),
        P(every),
    )
    stacked_params = (
        P(None, None, every, None),
        P(None, None, None, every, None),
        P(None, None, every, None),
        P(None, None, every, None),
        P(None, every, None),
        P(None, None, every),
        P(None, every),
    )
    acts = P("batch", "seq", None)
    return jax.shard_map(
        shards,
        mesh=mesh,
        in_specs=(acts, acts, acts, P("batch", "seq"), P("batch", "seq"), P(), *params, *params, *params),
        out_specs=(acts, acts, acts, *params, *params, *stacked_params),
        check_vma=False,
    )
```

```python
import functools

import jax
import jax.numpy as jnp
from jax import lax
from jax.experimental import pallas as pl
from jax.experimental.pallas import tpu as pltpu
from jax.sharding import PartitionSpec as P

HEAD_SIZE = 64
QUERY_HEADS = 16
NB = 32
EPSILON = 1e-06
NEGATIVE = -1e30
MOMENTUM = 0.9
AVERAGE = 0.99
STEP_RATES = (0.0015, 0.03, 0.3, 0.04, 0.015, 0.1, 1.0)
BF16 = jnp.bfloat16
F32 = jnp.float32
BQ = 128
FF_BLOCK = 256


def nt(a, b):
    return lax.dot_general(a, b, (((1,), (1,)), ((), ())), preferred_element_type=F32)


def nn(a, b):
    return lax.dot_general(a, b, (((1,), (0,)), ((), ())), preferred_element_type=F32)


def tn(a, b):
    return lax.dot_general(a, b, (((0,), (0,)), ((), ())), preferred_element_type=F32)


def stacked(block, group, per):
    first = group * per
    return jnp.concatenate(
        [block[:, (first + c) * HEAD_SIZE : (first + c + 1) * HEAD_SIZE] for c in range(per)], axis=0
    )


def lanes(block, index):
    return block[:, index * HEAD_SIZE : (index + 1) * HEAD_SIZE]


def skew(held, back):
    count, width = held.shape
    rows = lax.broadcasted_iota(jnp.int32, (count, width), 0)
    amount = 1
    while amount < count:
        turned = pltpu.roll(held, width - amount if back else amount, 1)
        held = jnp.where((rows & amount) != 0, turned, held)
        amount *= 2
    return held


def make_strips(base_ref, strip_ref):
    heads, rows, width = strip_ref.shape
    for h in range(heads):
        strip_ref[h] = skew(jnp.broadcast_to(base_ref[h : h + 1, :], (rows, width)), False)


def windows(length):
    reach = length // 2
    for step in range(length // BQ):
        here = slice(step * BQ, (step + 1) * BQ)
        start = max(step * BQ - reach, 0)
        lead = reach - (step * BQ - start)
        yield here, slice(start, (step + 1) * BQ), slice(lead, lead + (step + 1) * BQ - start)


def head_layout(heads, width):
    q_width = heads * HEAD_SIZE
    k_width = (width - q_width) // 2
    return slice(0, q_width), slice(q_width, q_width + k_width), slice(q_width + k_width, width), k_width // HEAD_SIZE


def self_fwd_kernel(qkv_ref, seg_row_ref, seg_col_ref, base_ref, o_ref, lse_ref, strip_ref):
    heads = strip_ref.shape[0]
    in_q, in_k, in_v, groups = head_layout(heads, qkv_ref.shape[2])
    per = heads // groups

    @pl.when(pl.program_id(0) == 0)
    def _():
        make_strips(base_ref, strip_ref)

    for here, seen, strip in windows(qkv_ref.shape[1]):
        same = seg_col_ref[0, here, :] == seg_row_ref[0, :, seen]
        block, keys, values = qkv_ref[0, here, in_q], qkv_ref[0, seen, in_k], qkv_ref[0, seen, in_v]
        outs, sums = [], []
        for g in range(groups):
            scores = nt(stacked(block, g, per), lanes(keys, g))
            probs = []
            for c in range(per):
                bias = strip_ref[g * per + c, :, strip]
                s = jnp.where(same, scores[c * BQ : (c + 1) * BQ] + bias, NEGATIVE)
                top = jnp.max(s, axis=-1, keepdims=True)
                e = jnp.exp(s - top)
                total = jnp.sum(e, axis=-1, keepdims=True)
                probs.append((e * (1.0 / total)).astype(BF16))
                sums.append(top + jnp.log(total))
            ctx = nn(jnp.concatenate(probs, axis=0), lanes(values, g)).astype(BF16)
            outs += [ctx[c * BQ : (c + 1) * BQ] for c in range(per)]
        o_ref[0, here, :] = jnp.concatenate(outs, axis=1)
        lse_ref[0, here, :] = jnp.concatenate(sums, axis=1)


def self_bwd_kernel(
    qkv_ref, c_ref, lse_ref, seg_row_ref, seg_col_ref, base_ref,
    d_ref, lag_ref, strip_ref, grad_ref, dk_acc, dv_acc,
):
    heads = strip_ref.shape[0]
    in_q, in_k, in_v, groups = head_layout(heads, qkv_ref.shape[2])
    per = heads // groups

    @pl.when(pl.program_id(0) == 0)
    def _():
        make_strips(base_ref, strip_ref)
        grad_ref[...] = jnp.zeros_like(grad_ref)

    dk_acc[...] = jnp.zeros_like(dk_acc)
    dv_acc[...] = jnp.zeros_like(dv_acc)
    for here, seen, strip in windows(qkv_ref.shape[1]):
        same = seg_col_ref[0, here, :] == seg_row_ref[0, :, seen]
        block, keys, values = qkv_ref[0, here, in_q], qkv_ref[0, seen, in_k], qkv_ref[0, seen, in_v]
        cots, lse = c_ref[0, here, :], lse_ref[0, here, :]
        outs = []
        for g in range(groups):
            q2, c2 = stacked(block, g, per), stacked(cots, g, per)
            scores = nt(q2, lanes(keys, g))
            dprobs = nt(c2, lanes(values, g))
            probs, dscores = [], []
            for c in range(per):
                h = g * per + c
                bias = strip_ref[h, :, strip]
                s = jnp.where(same, scores[c * BQ : (c + 1) * BQ] + bias, NEGATIVE)
                p = jnp.exp(s - lse[:, h : h + 1])
                dp = dprobs[c * BQ : (c + 1) * BQ]
                ds = (p * (dp - jnp.sum(p * dp, axis=-1, keepdims=True))).astype(BF16)
                grad_ref[h, :, strip] += ds.astype(F32)
                probs.append(p.astype(BF16))
                dscores.append(ds)
            p2, ds2 = jnp.concatenate(probs, axis=0), jnp.concatenate(dscores, axis=0)
            dq2 = nn(ds2, lanes(keys, g)).astype(BF16)
            outs += [dq2[c * BQ : (c + 1) * BQ] for c in range(per)]
            mine = slice(g * HEAD_SIZE, (g + 1) * HEAD_SIZE)
            dk_acc[mine, seen] += tn(q2, ds2)
            dv_acc[mine, seen] += tn(c2, p2)
        d_ref[0, here, in_q] = jnp.concatenate(outs, axis=1)
    d_ref[0, :, in_k] = dk_acc[...].T.astype(BF16)
    d_ref[0, :, in_v] = dv_acc[...].T.astype(BF16)

    @pl.when(pl.program_id(0) == pl.num_programs(0) - 1)
    def _():
        for h in range(heads):
            lag_ref[h : h + 1, :] = jnp.sum(skew(grad_ref[h], True), axis=0, keepdims=True)


def self_specs(length, width, heads, strip_width):
    qkv = pl.BlockSpec((1, length, width), lambda r: (r, 0, 0))
    queries = pl.BlockSpec((1, length, heads * HEAD_SIZE), lambda r: (r, 0, 0))
    sums = pl.BlockSpec((1, length, heads), lambda r: (r, 0, 0))
    seg_row = pl.BlockSpec((1, 1, length), lambda r: (r, 0, 0))
    seg_col = pl.BlockSpec((1, length, 1), lambda r: (r, 0, 0))
    base = pl.BlockSpec((heads, strip_width), lambda r: (0, 0))
    return qkv, queries, sums, seg_row, seg_col, base


def self_attention(qkv, segments, base):
    rows, length, width = qkv.shape
    heads, strip_width = base.shape
    all_spec, queries, sums, seg_row, seg_col, base_spec = self_specs(length, width, heads, strip_width)
    work = rows * heads * length * length * 3 // 8
    return pl.pallas_call(
        self_fwd_kernel,
        grid=(rows,),
        in_specs=[all_spec, seg_row, seg_col, base_spec],
        out_specs=[queries, sums],
        out_shape=[
            jax.ShapeDtypeStruct((rows, length, heads * HEAD_SIZE), BF16),
            jax.ShapeDtypeStruct((rows, length, heads), F32),
        ],
        scratch_shapes=[pltpu.VMEM((heads, BQ, strip_width), F32)],
        compiler_params=pltpu.CompilerParams(vmem_limit_bytes=48 << 20),
        cost_estimate=pl.CostEstimate(
            flops=work * 4 * HEAD_SIZE, transcendentals=work, bytes_accessed=qkv.size * 4
        ),
        name="self_attention",
    )(qkv, segments[:, None, :], segments[:, :, None], base)


def self_attention_back(qkv, cots, lse, segments, base):
    rows, length, width = qkv.shape
    heads, strip_width = base.shape
    all_spec, queries, sums, seg_row, seg_col, base_spec = self_specs(length, width, heads, strip_width)
    k_width = (width - heads * HEAD_SIZE) // 2
    work = rows * heads * length * length * 3 // 8
    return pl.pallas_call(
        self_bwd_kernel,
        grid=(rows,),
        in_specs=[all_spec, queries, sums, seg_row, seg_col, base_spec],
        out_specs=[all_spec, base_spec],
        out_shape=[
            jax.ShapeDtypeStruct(qkv.shape, BF16),
            jax.ShapeDtypeStruct((heads, strip_width), F32),
        ],
        scratch_shapes=[
            pltpu.VMEM((heads, BQ, strip_width), F32),
            pltpu.VMEM((heads, BQ, strip_width), F32),
            pltpu.VMEM((k_width, length), F32),
            pltpu.VMEM((k_width, length), F32),
        ],
        compiler_params=pltpu.CompilerParams(vmem_limit_bytes=48 << 20),
        cost_estimate=pl.CostEstimate(
            flops=work * 10 * HEAD_SIZE, transcendentals=work, bytes_accessed=qkv.size * 6
        ),
        name="self_attention_back",
    )(qkv, cots, lse, segments[:, None, :], segments[:, :, None], base)


def cross_fwd_kernel(q_ref, k_ref, v_ref, seg_row_ref, seg_col_ref, o_ref, *lse_refs):
    block, keys, values = q_ref[0], k_ref[0], v_ref[0]
    count = block.shape[0]
    groups = keys.shape[1] // HEAD_SIZE
    per = block.shape[1] // keys.shape[1]
    same = seg_col_ref[0] == seg_row_ref[0]
    outs = []
    for g in range(groups):
        scores = nt(stacked(block, g, per), lanes(keys, g))
        probs = []
        for c in range(per):
            s = jnp.where(same, scores[c * count : (c + 1) * count], NEGATIVE)
            top = jnp.max(s, axis=-1, keepdims=True)
            e = jnp.exp(s - top)
            total = jnp.sum(e, axis=-1, keepdims=True)
            probs.append((e * (1.0 / total)).astype(BF16))
        ctx = nn(jnp.concatenate(probs, axis=0), lanes(values, g)).astype(BF16)
        outs += [ctx[c * count : (c + 1) * count] for c in range(per)]
    o_ref[0] = jnp.concatenate(outs, axis=1)


def cross_bwd_kernel(q_ref, k_ref, v_ref, c_ref, seg_row_ref, seg_col_ref, dq_ref, dk_ref, dv_ref):
    block, keys, values, cots = q_ref[0], k_ref[0], v_ref[0], c_ref[0]
    count = block.shape[0]
    groups = keys.shape[1] // HEAD_SIZE
    per = block.shape[1] // keys.shape[1]
    same = seg_col_ref[0] == seg_row_ref[0]
    outs, dkeys, dvalues = [], [], []
    for g in range(groups):
        q2, c2 = stacked(block, g, per), stacked(cots, g, per)
        scores = nt(q2, lanes(keys, g))
        dprobs = nt(c2, lanes(values, g))
        probs, dscores = [], []
        for c in range(per):
            s = jnp.where(same, scores[c * count : (c + 1) * count], NEGATIVE)
            top = jnp.max(s, axis=-1, keepdims=True)
            e = jnp.exp(s - top)
            p = e * (1.0 / jnp.sum(e, axis=-1, keepdims=True))
            dp = dprobs[c * count : (c + 1) * count]
            dscores.append((p * (dp - jnp.sum(p * dp, axis=-1, keepdims=True))).astype(BF16))
            probs.append(p.astype(BF16))
        p2, ds2 = jnp.concatenate(probs, axis=0), jnp.concatenate(dscores, axis=0)
        dq2 = nn(ds2, lanes(keys, g)).astype(BF16)
        outs += [dq2[c * count : (c + 1) * count] for c in range(per)]
        dkeys.append(tn(q2, ds2))
        dvalues.append(tn(c2, p2))
    dq_ref[0] = jnp.concatenate(outs, axis=1)
    dk_ref[0] = jnp.concatenate(dkeys, axis=0).T.astype(dk_ref.dtype)
    dv_ref[0] = jnp.concatenate(dvalues, axis=0).T.astype(dv_ref.dtype)


def cross_specs(q, k):
    rows, count, q_width = q.shape
    memory, k_width = k.shape[1:]
    step = 2 * HEAD_SIZE
    q_step = step * (q_width // k_width)
    queries = pl.BlockSpec((1, count, q_step), lambda r, g: (r, 0, g))
    keys = pl.BlockSpec((1, memory, step), lambda r, g: (r, 0, g))
    seg_row = pl.BlockSpec((1, 1, memory), lambda r, g: (r, 0, 0))
    seg_col = pl.BlockSpec((1, count, 1), lambda r, g: (r, 0, 0))
    return (rows, k_width // step), queries, keys, seg_row, seg_col


def cross_attention(q, k, v, segments, memory_segments):
    grid, queries, keys, seg_row, seg_col = cross_specs(q, k)
    work = q.size // HEAD_SIZE * k.shape[1]
    return pl.pallas_call(
        cross_fwd_kernel,
        grid=grid,
        in_specs=[queries, keys, keys, seg_row, seg_col],
        out_specs=queries,
        out_shape=jax.ShapeDtypeStruct(q.shape, BF16),
        compiler_params=pltpu.CompilerParams(vmem_limit_bytes=48 << 20),
        cost_estimate=pl.CostEstimate(
            flops=work * 4 * HEAD_SIZE, transcendentals=work, bytes_accessed=q.size * 4 + k.size * 4
        ),
        name="cross_attention",
    )(q, k, v, memory_segments[:, None, :], segments[:, :, None])


def cross_attention_back(q, k, v, cots, segments, memory_segments):
    grid, queries, keys, seg_row, seg_col = cross_specs(q, k)
    work = q.size // HEAD_SIZE * k.shape[1]
    return pl.pallas_call(
        cross_bwd_kernel,
        grid=grid,
        in_specs=[queries, keys, keys, queries, seg_row, seg_col],
        out_specs=[queries, keys, keys],
        out_shape=[
            jax.ShapeDtypeStruct(q.shape, BF16),
            jax.ShapeDtypeStruct(k.shape, BF16),
            jax.ShapeDtypeStruct(k.shape, BF16),
        ],
        compiler_params=pltpu.CompilerParams(vmem_limit_bytes=48 << 20),
        cost_estimate=pl.CostEstimate(
            flops=work * 10 * HEAD_SIZE, transcendentals=work, bytes_accessed=q.size * 6 + k.size * 8
        ),
        name="cross_attention_back",
    )(q, k, v, cots, memory_segments[:, None, :], segments[:, :, None])


def bit_count(axis):
    return lax.axis_size(axis).bit_length() - 1


def my_bit(axis, bit):
    return (lax.axis_index(axis) >> bit) & 1


def flip(value, axis, mask):
    return lax.ppermute(value, axis, [(i, i ^ mask) for i in range(lax.axis_size(axis))])


def gather_pieces(value, axis, order):
    pieces = {0: value}
    for bit in order:
        for j in list(pieces):
            pieces[j | (1 << bit)] = flip(pieces[j], axis, 1 << bit)
    return [pieces[j] for j in range(len(pieces))]


def gather_direct(value, axis):
    return [value] + [flip(value, axis, j) for j in range(1, lax.axis_size(axis))]


def absolute(values, axis):
    place = lax.axis_index(axis)
    values = jnp.stack(values) if isinstance(values, list) else values
    return [lax.dynamic_index_in_dim(values, j ^ place, 0, False) for j in range(values.shape[0])]


def settle(*groups):
    flat, tree = jax.tree.flatten(groups)
    return jax.tree.unflatten(tree, lax.optimization_barrier(flat))


class Chain:
    def __init__(self, full, bits, order):
        shape = (2,) * len(bits) + (full.shape[0] >> len(bits),) + full.shape[1:]
        self.parts, self.left, self.order, self.flying = [full.reshape(shape)], list(bits), list(order), None

    def half(self, choice):
        where = self.left.index(self.order[0])
        return [lax.dynamic_index_in_dim(p, choice, where, False) for p in self.parts]

    def outgoing(self):
        return sum(p.astype(F32) for p in self.half(1 - my_bit(*self.order[0]))).astype(BF16)

    def launch(self, away):
        self.parts = self.half(my_bit(*self.order[0]))
        axis, bit = self.order.pop(0)
        self.left.remove((axis, bit))
        self.flying = flip(away, axis, 1 << bit)

    def land(self):
        self.parts = self.parts + [self.flying]
        self.flying = None

    def finish(self):
        if self.flying is not None:
            self.land()
        while self.order:
            self.launch(self.outgoing())
            self.land()

    def result(self):
        return sum(p.astype(F32) for p in self.parts)


def joined(chains, order):
    chain = Chain.__new__(Chain)
    chain.left, chain.order, chain.flying = list(chains[0].left), list(order), None
    chain.parts = [jnp.concatenate(parts, axis=-1) for parts in zip(*[c.parts for c in chains])]
    return chain


class Gather:
    def __init__(self, value, order, lead=0):
        self.held, self.order, self.lead, self.done, self.flying, self.last = value, list(order), lead, [], None, None

    def outgoing(self):
        return self.held

    def launch(self, value):
        self.held = value
        self.last = self.order.pop(0)
        self.flying = flip(value, self.last[0], 1 << self.last[1])

    def land(self):
        self.done = [bit for bit in place_bits() if bit in self.done or bit == self.last]
        where = self.lead + self.done.index(self.last)
        pair = jnp.arange(2).reshape((2,) + (1,) * (self.held.ndim - where))
        own, came = jnp.expand_dims(self.held, where), jnp.expand_dims(self.flying, where)
        self.held = jnp.where(pair == my_bit(*self.last), own, came)
        self.flying = None


def land(main, *chains):
    arrive = [c for c in chains if c.flying is not None]
    main, flown = settle(main, [c.flying for c in arrive])
    for chain, value in zip(arrive, flown):
        chain.flying = value
        chain.land()
    return main


def tick(main, *chains):
    main = land(main, *chains)
    depart = [c for c in chains if c.order]
    main, sends = settle(main, [c.outgoing() for c in depart])
    for chain, value in zip(depart, sends):
        chain.launch(value)
    return main


def place_bits():
    return [("batch", b) for b in reversed(range(bit_count("batch")))] + [
        ("seq", b) for b in reversed(range(bit_count("seq")))
    ]


def hops(seq_first, turned):
    seq = [("seq", b) for b in range(bit_count("seq"))]
    far = [("batch", b) for b in range(1, bit_count("batch"))]
    if turned:
        seq.reverse()
    return [("batch", 0)] + (seq + far if seq_first else far + seq)


def chain_of(full, seq_first=True, turned=False):
    return Chain(full, place_bits(), hops(seq_first, turned))


def chain_of_halves(away, kept, seq_first=True, turned=False):
    chain = Chain(kept, [b for b in place_bits() if b != ("batch", 0)], hops(seq_first, turned)[1:])
    chain.flying = flip(away, "batch", 1).reshape(chain.parts[0].shape)
    return chain


def small_sum(values):
    got = lax.all_to_all(values, ("batch", "seq"), 0, 0, tiled=True)
    return jnp.sum(got, axis=0)


def inverse_rms(values):
    return lax.rsqrt(jnp.mean(values * values, axis=-1, keepdims=True) + EPSILON)


def norm_back(values, inverse, gain, upstream):
    weighted = gain * upstream
    dot = jnp.mean(weighted * values, axis=-1, keepdims=True)
    grad = inverse * weighted - values * (inverse * inverse * inverse) * dot
    return grad, jnp.sum(upstream * values * inverse, axis=0)


def gelu_parts(v):
    scale = 0.7978845608028654
    inner = scale * (v + 0.044715 * (v * v * v))
    t = jnp.tanh(inner)
    value = 0.5 * v * (1.0 + t)
    slope = 0.5 * (1.0 + t) + 0.5 * v * (1.0 - t * t) * (scale * (1.0 + 3 * 0.044715 * (v * v)))
    return value, slope


def hidden_rows(x, core_rows):
    turned = x.T
    blocks = [turned[i : i + core_rows] for i in range(0, turned.shape[0], core_rows)]
    return jnp.concatenate(blocks[0::2], axis=0), jnp.concatenate(blocks[1::2], axis=0)


def ffn_kernel(
    core_ref, h_ref, gain_ref, og_ref, wg_ref, wu_ref, wr_ref,
    out_ref, hgrad_ref, gain_grad_ref, dg_away_ref, dg_ref, du_away_ref, du_ref, dr_ref,
    x_ref, xt_ref, res_ref, back_ref, *, core_rows,
):
    half = dg_ref.shape[0]
    step = pl.program_id(0)

    @pl.when(step == 0)
    def _():
        hidden = h_ref[...]
        x = (hidden * inverse_rms(hidden) * gain_ref[...]).astype(BF16)
        x_ref[...] = x
        flipped = hidden_rows(x, core_rows)
        first_core = core_ref[0] == 0
        xt_ref[:half] = jnp.where(first_core, flipped[1], flipped[0])
        xt_ref[half:] = jnp.where(first_core, flipped[0], flipped[1])
        res_ref[...] = jnp.zeros_like(res_ref)
        back_ref[...] = jnp.zeros_like(back_ref)

    x, og = x_ref[...], og_ref[...]
    wg, wu, wr = wg_ref[...], wu_ref[...], wr_ref[...]
    gelu_value, gelu_slope = gelu_parts(nn(x, wg))
    up = nn(x, wu)
    activated = (gelu_value * up).astype(BF16)
    upstream = nt(og, wr)
    gate_grad = (upstream * up * gelu_slope).astype(BF16)
    up_grad = (upstream * gelu_value).astype(BF16)
    res_ref[...] += nn(activated, wr)
    back_ref[...] += nt(gate_grad, wg) + nt(up_grad, wu)
    dr_ref[...] = tn(activated, og).astype(BF16)
    xt = xt_ref[...]
    gate_product, up_product = nn(xt, gate_grad).astype(BF16), nn(xt, up_grad).astype(BF16)
    dg_away_ref[...], dg_ref[...] = gate_product[:half], gate_product[half:]
    du_away_ref[...], du_ref[...] = up_product[:half], up_product[half:]

    @pl.when(step == pl.num_programs(0) - 1)
    def _():
        hidden = h_ref[...]
        out_ref[...] = (hidden + res_ref[...]).astype(BF16)
        inverse = inverse_rms(hidden)
        upward = back_ref[...]
        weighted = gain_ref[...] * upward
        dot = jnp.mean(weighted * hidden, axis=-1, keepdims=True)
        part = inverse * weighted - hidden * (inverse * inverse * inverse) * dot
        hgrad_ref[...] = og_ref[...].astype(F32) + part
        gain_grad_ref[...] = jnp.sum(upward * hidden * inverse, axis=0, keepdims=True)


def feed_forward(hidden, gain, og, w_rest, w_red, ff_first):
    count, width = hidden.shape
    ff = w_red.shape[0]
    steps, gate_first = ff // FF_BLOCK, ff_first // FF_BLOCK
    whole = pl.BlockSpec((count, width), lambda j: (0, 0))
    row = pl.BlockSpec((1, width), lambda j: (0, 0))
    down = pl.BlockSpec((FF_BLOCK, width), lambda j: (j, 0))
    cols = pl.BlockSpec((width // 2, FF_BLOCK), lambda j: (0, j))
    core_rows = width // lax.axis_size("batch")
    return pl.pallas_call(
        functools.partial(ffn_kernel, core_rows=core_rows),
        grid=(steps,),
        in_specs=[
            pl.BlockSpec(memory_space=pltpu.SMEM),
            whole, row, whole,
            pl.BlockSpec((width, FF_BLOCK), lambda j: (0, j + gate_first)),
            pl.BlockSpec((width, FF_BLOCK), lambda j: (0, j + gate_first + steps)),
            down,
        ],
        out_specs=[whole, whole, row, cols, cols, cols, cols, down],
        out_shape=[
            jax.ShapeDtypeStruct((count, width), BF16),
            jax.ShapeDtypeStruct((count, width), F32),
            jax.ShapeDtypeStruct((1, width), F32),
            *[jax.ShapeDtypeStruct((width // 2, ff), BF16)] * 4,
            jax.ShapeDtypeStruct((ff, width), BF16),
        ],
        scratch_shapes=[
            pltpu.VMEM((count, width), BF16),
            pltpu.VMEM((width, count), BF16),
            pltpu.VMEM((count, width), F32),
            pltpu.VMEM((count, width), F32),
        ],
        compiler_params=pltpu.CompilerParams(vmem_limit_bytes=56 << 20),
        cost_estimate=pl.CostEstimate(
            flops=18 * count * width * ff, transcendentals=count * ff, bytes_accessed=12 * width * ff
        ),
        name="feed_forward",
    )(my_bit("batch", 0).reshape(1).astype(jnp.int32), hidden, gain, og, w_rest, w_rest, w_red)


def shards(
    tokens, memory, output_grad, segments, memory_segments, buckets,
    w_query, keyvalue_weight, w_output, w_expand, w_reduce, gains, position_bias,
    momentum_query, keyvalue_momentum, momentum_output, momentum_expand, momentum_reduce,
    momentum_gains, momentum_position,
    average_query, keyvalue_average, average_output, average_expand, average_reduce,
    average_gains, average_position,
):
    every = ("batch", "seq")
    seq_count, seq_index = lax.axis_size("seq"), lax.axis_index("seq")
    devices = lax.axis_size("batch") * seq_count
    rows, part, width = tokens.shape
    length = part * seq_count
    memory_part = memory.shape[1]
    own = w_query.shape[1]
    kv_width = keyvalue_weight.shape[3]
    heads_local = QUERY_HEADS // seq_count
    q_local, kv_local = width // seq_count, kv_width // seq_count

    wq, wkv = w_query.astype(BF16), keyvalue_weight.astype(BF16)
    wo, we, wr = w_output.astype(BF16), w_expand.astype(BF16), w_reduce.astype(BF16)
    first = jnp.concatenate(
        [
            wq[0].reshape(own, seq_count, q_local),
            wkv[0, 0].reshape(own, seq_count, kv_local),
            wkv[0, 1].reshape(own, seq_count, kv_local),
        ],
        axis=2,
    )
    cols = first.shape[2]
    bias_own = position_bias.shape[0]
    small = jnp.concatenate([gains.astype(BF16).reshape(-1), position_bias.astype(BF16)])
    small = jnp.pad(small, (0, 8 * cols - small.shape[0])).reshape(1, 8, cols)
    packet = jnp.concatenate([first.transpose(1, 0, 2), jnp.broadcast_to(small, (seq_count, 8, cols))], axis=1)
    packet = lax.all_to_all(packet, "seq", 0, 0, tiled=True)
    batch_far = [("batch", b) for b in reversed(range(1, bit_count("batch")))]
    seq_up = [("seq", b) for b in range(bit_count("seq"))]
    core = [("batch", 0)]
    gather_p = Gather(packet, batch_far + core)
    for _ in batch_far + core:
        gather_p.launch(gather_p.held)
        gather_p.land()
    orders = [[b for _, b in (seq_up if r % 2 == 0 else seq_up[::-1])] for r in range(rows)]
    first_hop = [flip(tokens[r], "seq", 1 << orders[r][0]) for r in range(rows)]
    token_pieces = []
    for r in range(rows):
        pieces = {0: tokens[r], 1 << orders[r][0]: first_hop[r]}
        for bit in orders[r][1:]:
            for j in list(pieces):
                pieces[j | (1 << bit)] = flip(pieces[j], "seq", 1 << bit)
        token_pieces.append([pieces[j] for j in range(seq_count)])
    ids = jnp.concatenate([segments, memory_segments], axis=1)
    all_ids = jnp.stack(absolute(gather_direct(ids, "seq"), "seq"), axis=1)
    all_segments = all_ids[:, :, :part].reshape(rows, length)
    all_memory_segments = all_ids[:, :, part:].reshape(rows, -1)
    packets = gather_p.held.reshape(-1, seq_count, own + 8, cols)
    w_heads = packets[:, :, :own].reshape(width, cols)
    small_rows = packets[:, :, own:].reshape(devices, -1)
    gain_values = (
        small_rows[:, : 3 * own].reshape(devices, 3, own).transpose(1, 0, 2).reshape(3, width).astype(F32)
    )
    table = small_rows[:, 3 * own : 3 * own + bias_own].reshape(NB, QUERY_HEADS).astype(F32)

    ff, ff_own = we.shape[2], wr.shape[0]
    folds = -(-ff_own // own)
    wr_rows = jnp.pad(wr, ((0, folds * own - ff_own), (0, 0))).reshape(folds, own, width)
    pieces = [wkv[1, 0], wkv[1, 1], wo[0], wq[1], wo[1], we[0], we[1], *[wr_rows[i] for i in range(folds)]]
    w_rest = lax.all_gather(jnp.concatenate(pieces, axis=1), every, axis=0, tiled=True)
    w_kv1, w_o0, w_q1, w_o1 = (w_rest[:, i * width : (i + 1) * width] for i in range(4))
    ff_first = 4 * width
    down_first = ff_first + 2 * ff
    w_red = jnp.concatenate(
        [
            w_rest[:, down_first + i * width : down_first + (i + 1) * width].reshape(devices, own, width)
            for i in range(folds)
        ],
        axis=1,
    )[:, :ff_own].reshape(ff, width)

    reach = length // 2
    strip_width = 2 * reach + BQ
    lag = reach - jnp.arange(strip_width, dtype=jnp.int32)
    lag_ok = lag >= 0
    lag_bucket = jnp.where(lag_ok, jnp.take(buckets, jnp.clip(lag, 0, length - 1)), -1)
    picks = (lag_bucket[None, :] == jnp.arange(NB, dtype=jnp.int32)[:, None]).astype(F32)
    table_local = lax.dynamic_slice_in_dim(table, seq_index * heads_local, heads_local, 1)
    base = jnp.dot(table_local.T, picks, precision=lax.Precision.HIGHEST)
    base = jnp.where(lag_ok[None, :], base, NEGATIVE)

    all_tokens = jnp.stack([jnp.stack(p) for p in token_pieces], axis=1).astype(F32)
    all_normed = (all_tokens * inverse_rms(all_tokens) * gain_values[0]).astype(BF16).reshape(-1, width)
    head_qkv = nn(all_normed, w_heads).astype(BF16).reshape(seq_count, rows, part, cols)
    head_qkv = jnp.stack(absolute(head_qkv, "seq"), axis=1).reshape(rows, length, cols)
    head_context, lse = self_attention(head_qkv, all_segments, base)
    context = lax.all_to_all(head_context, "seq", split_axis=1, concat_axis=2, tiled=True).reshape(-1, width)

    mem = memory.reshape(rows * memory_part, width)
    mkv = nn(mem, w_kv1).astype(BF16).reshape(rows, memory_part, -1)
    all_mkv = jnp.stack(absolute(gather_direct(mkv, "seq"), "seq"), axis=1).reshape(rows, -1, 2 * kv_width)
    mk, mv = all_mkv[:, :, :kv_width], all_mkv[:, :, kv_width:]
    x = tokens.astype(F32).reshape(rows * part, width)
    inv_zero = inverse_rms(x)
    hidden_one = x + nn(context, w_o0)
    inv_one = inverse_rms(hidden_one)
    normed_one = (hidden_one * inv_one * gain_values[1]).astype(BF16)
    cross_q = nn(normed_one, w_q1).astype(BF16).reshape(rows, part, width)
    cross_context = cross_attention(cross_q, mk, mv, segments, all_memory_segments)
    cross_flat = cross_context.reshape(-1, width)
    hidden_two = hidden_one + nn(cross_flat, w_o1)
    hidden_two, w_red, w_heads = settle(hidden_two, w_red, w_heads)
    w_first = jnp.concatenate(gather_direct(w_heads, "seq"), axis=1)
    og = output_grad.reshape(rows * part, width)
    result, hidden_two_grad, gain_two, *part_gu, part_reduce = feed_forward(
        hidden_two, gain_values[2:3], og, w_rest, w_red, ff_first
    )
    result, gain_two = result.reshape(tokens.shape), gain_two[0]
    chain_g = chain_of_halves(part_gu[0], part_gu[1])
    chain_u = chain_of_halves(part_gu[2], part_gu[3], turned=True)
    chain_r = chain_of(part_reduce, seq_first=False)
    hidden_two_grad, w_first = tick((hidden_two_grad, w_first), chain_r)

    cross_out_grad = hidden_two_grad.astype(BF16)
    cross_cots = nt(cross_out_grad, w_o1).astype(BF16).reshape(rows, part, width)
    cross_cots = tick(cross_cots, chain_r, chain_g, chain_u)
    cross_dq, mdk, mdv = cross_attention_back(cross_q, mk, mv, cross_cots, segments, all_memory_segments)
    mdkv = jnp.concatenate([mdk, mdv], axis=2).reshape(rows, seq_count, memory_part, -1)
    mdkv = lax.all_to_all(mdkv, "seq", split_axis=1, concat_axis=1, tiled=True)
    cross_dq = cross_dq.reshape(-1, width)
    part_one, gain_one = norm_back(hidden_one, inv_one, gain_values[1], nt(cross_dq, w_q1))
    hidden_one_grad = hidden_two_grad + part_one

    self_out_grad = hidden_one_grad.astype(BF16)
    cots = nt(self_out_grad, w_o0).astype(BF16).reshape(rows, part, width)
    chain_o1 = chain_of(tn(cross_flat, cross_out_grad).astype(BF16))
    chain_q1 = chain_of(tn(normed_one, cross_dq).astype(BF16))
    chain_a = joined([chain_o1, chain_q1], chain_o1.order)
    mdkv = jnp.sum(mdkv.astype(F32), axis=1).astype(BF16).reshape(rows * memory_part, -1)
    memory_grad = nt(mdkv, w_kv1).reshape(memory.shape)
    chain_o0 = chain_of(tn(context, self_out_grad).astype(BF16), turned=True)
    chain_k1 = chain_of(tn(mem, mdkv).astype(BF16), turned=True)
    chain_b = joined([chain_o0, chain_k1], chain_o0.order)
    cots = tick(cots, chain_a, chain_b)
    head_cots = lax.all_to_all(cots, "seq", split_axis=2, concat_axis=1, tiled=True)
    head_cots, memory_grad = tick((head_cots, memory_grad), chain_r, chain_g, chain_u, chain_a, chain_b)
    head_grads, lag_sums = self_attention_back(head_qkv, head_cots, lse, all_segments, base)
    by_place = head_grads.reshape(rows, seq_count, part, cols)
    relative = absolute(by_place.swapaxes(0, 1), "seq")
    batch_bits = [("batch", b) for b in reversed(range(bit_count("batch")))]
    all_grads = jnp.stack(relative).reshape(-1, cols)
    chain_f = Chain(tn(all_normed, all_grads).astype(BF16), batch_bits, hops(False, False)[: len(batch_bits)])
    by_place, lag_sums = land((by_place, lag_sums), chain_g, chain_u, chain_r, chain_a, chain_b)
    while chain_g.order[0][0] == "seq":
        by_place, lag_sums = land(tick((by_place, lag_sums), chain_g, chain_u), chain_g, chain_u)
    chain_gu = joined([chain_g, chain_u], chain_g.order)
    chains = (chain_f, chain_gu, chain_r, chain_a, chain_b)
    dqkv = lax.all_to_all(by_place, "seq", split_axis=1, concat_axis=1, tiled=True)
    lag_sums = tick(lag_sums, *chains)
    dqkv, lag_sums = settle(dqkv, lag_sums)
    dqkv = jnp.concatenate(absolute(dqkv.swapaxes(0, 1), "seq"), axis=-1).reshape(rows * part, -1)
    dqkv = tick(dqkv, chain_f)
    part_zero, gain_zero = norm_back(x, inv_zero, gain_values[0], nt(dqkv, w_first))
    input_grad = (hidden_one_grad + part_zero).reshape(tokens.shape)
    input_grad = land(input_grad, chain_a, chain_b)
    while chain_a.order[0][0] == "seq":
        input_grad = land(tick(input_grad, chain_a, chain_b), chain_a, chain_b)
    chain_ab = joined([chain_a, chain_b], chain_a.order)
    chains = (chain_f, chain_gu, chain_r, chain_ab)
    input_grad = tick(input_grad, *chains)
    for chain in chains:
        chain.finish()
    grad_gu, grad_reduce = chain_gu.result(), chain_r.result()
    grad_gate, grad_up = grad_gu[:, :ff], grad_gu[:, ff:]
    grad_ab = chain_ab.result()
    grad_o1, grad_q1, grad_o0, grad_k1 = (grad_ab[:, i * width : (i + 1) * width] for i in range(4))
    first_grads = lax.all_to_all(chain_f.result().reshape(seq_count, own, cols), "seq", 0, 0, tiled=True)
    first_grads = first_grads.transpose(1, 0, 2)

    table_part = jnp.dot(picks, lag_sums.T, precision=lax.Precision.HIGHEST)
    table_grad = lax.dynamic_update_slice(
        jnp.zeros((NB, QUERY_HEADS), F32), table_part, (0, seq_index * heads_local)
    ).reshape(devices, -1)
    gains_grad = jnp.stack([gain_zero, gain_one, gain_two]).reshape(3, devices, own)
    gains_grad = gains_grad.transpose(1, 0, 2).reshape(devices, -1)
    small_grads = small_sum(jnp.concatenate([gains_grad, table_grad], axis=1))
    shard_gains = small_grads[: 3 * own].reshape(3, own)
    shard_table = small_grads[3 * own :]

    shard_query = jnp.stack([first_grads[:, :, :q_local].reshape(own, width), grad_q1])
    shard_keyval = jnp.stack(
        [
            jnp.stack(
                [
                    first_grads[:, :, q_local : q_local + kv_local].reshape(own, kv_width),
                    first_grads[:, :, q_local + kv_local :].reshape(own, kv_width),
                ]
            ),
            jnp.stack([grad_k1[:, :kv_width], grad_k1[:, kv_width:]]),
        ]
    )
    gradients = (
        shard_query,
        shard_keyval,
        jnp.stack([grad_o0, grad_o1]),
        jnp.stack([grad_gate, grad_up]),
        grad_reduce,
        shard_gains,
        shard_table,
    )
    token_scale = (rows * part * devices) ** (-0.5)
    masters = (w_query, keyvalue_weight, w_output, w_expand, w_reduce, gains, position_bias)
    momenta = (
        momentum_query, keyvalue_momentum, momentum_output, momentum_expand, momentum_reduce,
        momentum_gains, momentum_position,
    )
    averages = (
        average_query, keyvalue_average, average_output, average_expand, average_reduce,
        average_gains, average_position,
    )
    renewals, states = [], []
    for gradient, master, momentum, average, step_rate in zip(gradients, masters, momenta, averages, STEP_RATES):
        renewed = MOMENTUM * momentum + gradient
        weight = master - step_rate * token_scale * (gradient + MOMENTUM * renewed)
        renewals.append(renewed)
        states.append(jnp.stack([weight, AVERAGE * average + (1.0 - AVERAGE) * weight]))
    return (result, input_grad, memory_grad.astype(F32), *gradients, *renewals, *states)


def solution(mesh):
    every = ("batch", "seq")
    params = (
        P(None, every, None),
        P(None, None, every, None),
        P(None, every, None),
        P(None, every, None),
        P(every, None),
        P(None, every),
        P(every),
    )
    stacked_params = (
        P(None, None, every, None),
        P(None, None, None, every, None),
        P(None, None, every, None),
        P(None, None, every, None),
        P(None, every, None),
        P(None, None, every),
        P(None, every),
    )
    acts = P("batch", "seq", None)
    return jax.shard_map(
        shards,
        mesh=mesh,
        in_specs=(acts, acts, acts, P("batch", "seq"), P("batch", "seq"), P(), *params, *params, *params),
        out_specs=(acts, acts, acts, *params, *params, *stacked_params),
        check_vma=False,
    )
```
